32 devices in a mesh: groups: 2 (over x), crate: 16 (over z, y, core).
Axes of the slice: x: 2, y: 2, z: 4, core: 2. Of those that a mesh axis runs over, the one named last changes fastest.
Arguments:
- voltages: bfloat16 [4096, 17920], P(('groups', 'crate')), parts along dimension 0, may hold values from -6 to 6
- gains: float32 [256, 2, 2048], P('crate'), may hold values from -4 to 4
- positions: float32 [3, 2048], replicated, may hold values from -64 to 64
- directions: float32 [3, 512], replicated, may hold values from -0.5 to 0.5
- input_order: int32 [2048], replicated, may hold values from 0 to 2047, each once
- delays: int32 [1024, 256], replicated, may hold values from 0 to 31
- search_beams: int32 [16], replicated, may hold values from 0 to 511, as said below
Outputs:
- beam_power: float32 [512, 512, 32], P(('groups', 'crate')), parts along dimension 0
- dm_plane: float32 [2048, 16, 32], P(('groups', 'crate')), parts along dimension 0
The draws below stay inside these ranges and needn't reach their ends.
There are 2 independent parts, one for each index of `groups`. The reference program is written for one: setup_inputs(seed, part) draws one part's arguments, and reference() takes and returns one part's arrays. A program takes and returns all parts, laid end to end along the dimension named above; an argument that names none is the same for every part. Nothing has to cross between parts.
Inputs may be any that keep to these rules, and one draw needn't show every extreme that they name: `input_order`: each antenna is carried by exactly one input row. `search_beams`: 16 distinct beams, among them beam 0 and beam 512 - 1.
All inputs are finite; a program needn't handle non-finite values.
Results may differ from the reference program's by a relative error of at most 0.0082.
Values may be sent and summed in bfloat16 or wider, within the bound.
No kernel may reach another device: no remote copies, remote signals or barrier semaphores. Data moves between devices by JAX's collectives and lax.ppermute only.
A program may use at most 64 MiB of HBM per device.

```python
import math
import jax
import jax.numpy as jnp
from jax import lax

INPUTS = 2048
CH = 256
BEAMS = 512
TRIALS = 1024
TAPS = 4
TIME = 32
SEARCH = 16
FFTLEN = 512
SAMPLES = 17920
N_CRATE = 16


def draw_search_beams(key, part):
    key_pick, key_order = jax.random.split(jax.random.fold_in(key, 17))
    interior = 1 + jax.random.permutation(key_pick, BEAMS - 2)[:SEARCH - 2]
    listed = jnp.concatenate([jnp.array([0, BEAMS - 1], dtype=jnp.int32), interior.astype(jnp.int32)])
    return listed[jax.random.permutation(key_order, SEARCH)]


def place_ends(values, rng, smallest, high):
    longest = values.shape.index(max(values.shape))
    spots = []
    for shift in (0, 1):
        where = [jax.random.randint(jax.random.fold_in(rng, axis), (), 0, length) for axis, length in enumerate(values.shape)]
        where[longest] = (where[longest] + shift) % values.shape[longest]
        spots.append(tuple(where))
    return values.at[spots[0]].set(smallest).at[spots[1]].set(high)


def levels(rng, shape, cuts, smallest, top_value):
    factor_of, own = 1.0, jax.random.fold_in(rng, 6)
    for dim, shards_of in cuts:
        steps = jnp.exp(jax.random.uniform(jax.random.fold_in(own, dim), (shards_of,), jnp.float32, smallest / len(cuts), top_value / len(cuts)))
        factor_of = factor_of * jnp.repeat(steps, shape[dim] // shards_of).reshape([-1 if axis == dim else 1 for axis in range(len(shape))])
    return factor_of


def bell_draw(stream_key, shape, scale, reach, cuts=(), held_as=jnp.bfloat16):
    entries = scale * jax.random.normal(stream_key, shape, jnp.float32)
    if cuts:
        entries = entries * levels(stream_key, shape, cuts, -0.22, 0.18)
    return jnp.clip(entries, -reach, reach).astype(held_as)


def setup_inputs(seed: int = 0, part: int = 0) -> dict:
    key_list = jax.random.split(jax.random.key(seed), 8)
    own_keys = jax.random.split(jax.random.fold_in(key_list[7], part), 8)
    voltages = bell_draw(own_keys[0], (INPUTS, SAMPLES), 1.0, 6.0, ((0, 16),))
    gains = bell_draw(key_list[1], (CH, 2, INPUTS), 0.7, 4.0, ((0, 16),), jnp.float32)
    positions = jnp.clip(jax.random.uniform(key_list[2], (3, INPUTS), jnp.float32, -64.0, 64.0), -64.0, 64.0)
    directions = jnp.clip(jax.random.uniform(key_list[3], (3, BEAMS), jnp.float32, -0.5, 0.5), -0.5, 0.5)
    input_order = jax.random.permutation(key_list[4], INPUTS).astype(jnp.int32)
    delays = place_ends(jax.random.randint(key_list[5], (TRIALS, CH), 0, TIME), jax.random.fold_in(key_list[5], 1), 0, TIME - 1).astype(jnp.int32)
    search_beams = draw_search_beams(jax.random.fold_in(key_list[7], 71), part)
    return {"voltages": voltages, "gains": gains, "positions": positions, "directions": directions, "input_order": input_order, "delays": delays, "search_beams": search_beams}


TWO_PI = 2.0 * math.pi

def pfb_window():
    window_len = TAPS * FFTLEN
    sample_index = jnp.arange(window_len, dtype=jnp.int32).astype(jnp.float32)
    offsets = (sample_index - 0.5 * window_len + 0.5) / FFTLEN
    tapering = 0.54 - 0.46 * jnp.cos(TWO_PI * sample_index / (window_len - 1))
    return (jnp.sinc(offsets) * tapering).reshape(TAPS, FFTLEN)

def fold_frames(voltages, window):
    frames = voltages.reshape(voltages.shape[0], TIME + TAPS - 1, FFTLEN)
    summed = window[0] * frames[:, 0:TIME].astype(jnp.float32)
    for tap_index in range(1, TAPS):
        summed = summed + window[tap_index] * frames[:, tap_index:tap_index + TIME].astype(jnp.float32)
    return summed.astype(jnp.bfloat16)

def dft_table():
    channel_ids = jnp.arange(CH, dtype=jnp.int32)[:, None]
    sample_ids = jnp.arange(FFTLEN, dtype=jnp.int32)[None, :]
    angles = TWO_PI * (channel_ids * sample_ids % FFTLEN).astype(jnp.float32) / FFTLEN
    factor = 1.0 / math.sqrt(FFTLEN)
    stacked = jnp.stack([jnp.cos(angles) * factor, -jnp.sin(angles) * factor], axis=1)
    return stacked.reshape(2 * CH, FFTLEN).astype(jnp.bfloat16)

def time_table():
    step_ids = jnp.arange(TIME, dtype=jnp.int32)[:, None]
    bin_ids = jnp.arange(1, TIME // 2 + 1, dtype=jnp.int32)[None, :]
    angles = TWO_PI * (step_ids * bin_ids % TIME).astype(jnp.float32) / TIME
    factor = 1.0 / math.sqrt(TIME)
    return jnp.concatenate([jnp.cos(angles) * factor, -jnp.sin(angles) * factor], axis=1)

def array_geometry(positions, directions, input_order):
    placed = jnp.take(positions, input_order, axis=1)
    geometry = directions[0][:, None] * placed[0][None, :]
    geometry = geometry + directions[1][:, None] * placed[1][None, :]
    return geometry + directions[2][:, None] * placed[2][None, :]

def steering(geometry, gain_row, frequency):
    phases = TWO_PI * frequency * geometry
    cosine = jnp.cos(phases)
    sine_part = jnp.sin(phases)
    weight_norm = 1.0 / math.sqrt(INPUTS)
    w_real = ((gain_row[0] * cosine + gain_row[1] * sine_part) * weight_norm).astype(jnp.bfloat16)
    w_imag = ((gain_row[1] * cosine - gain_row[0] * sine_part) * weight_norm).astype(jnp.bfloat16)
    upper_rows = jnp.concatenate([w_real, -w_imag], axis=1)
    lower_rows = jnp.concatenate([w_imag, w_real], axis=1)
    return jnp.concatenate([upper_rows, lower_rows], axis=0)

def dedisperse(spectrum, delay_part):
    half_bins = TIME // 2
    bin_ids = jnp.arange(1, half_bins + 1, dtype=jnp.int32)
    turn_counts = delay_part[:, :, None] * bin_ids[None, None, :] % TIME
    angles = TWO_PI * turn_counts.astype(jnp.float32) / TIME
    cosine = jnp.cos(angles)
    sine_part = jnp.sin(angles)
    spec_real = spectrum[:, :, :half_bins]
    spec_imag = spectrum[:, :, half_bins:]
    highest = lax.Precision.HIGHEST
    out_real = jnp.einsum('cbk,dck->dbk', spec_real, cosine, precision=highest) - jnp.einsum('cbk,dck->dbk', spec_imag, sine_part, precision=highest)
    out_imag = jnp.einsum('cbk,dck->dbk', spec_real, sine_part, precision=highest) + jnp.einsum('cbk,dck->dbk', spec_imag, cosine, precision=highest)
    factor = 1.0 / math.sqrt(CH)
    return jnp.concatenate([out_real, out_imag], axis=2) * factor

def reference(voltages, gains, positions, directions, input_order, delays, search_beams):
    window = pfb_window()
    dft_rows = dft_table().astype(jnp.float32)
    blocks = voltages.reshape(N_CRATE, INPUTS // N_CRATE, SAMPLES)

    def channelize(block_volts):
        folded = fold_frames(block_volts, window)
        spectra_block = jnp.einsum('ks,its->kit', dft_rows, folded.astype(jnp.float32))
        return spectra_block.astype(jnp.bfloat16)
    spectra = lax.map(channelize, blocks)
    spectra = jnp.moveaxis(spectra, 0, 1).reshape(CH, 2, INPUTS, TIME)
    geometry = array_geometry(positions, directions, input_order)

    def one_channel(packed):
        channel, channel_data, gain_row = packed
        frequency = 1.0 + channel.astype(jnp.float32) / CH
        weights = steering(geometry, gain_row, frequency)
        beam_sums = jnp.dot(weights, channel_data.reshape(2 * INPUTS, TIME), preferred_element_type=jnp.float32)
        return beam_sums[:BEAMS] * beam_sums[:BEAMS] + beam_sums[BEAMS:] * beam_sums[BEAMS:]
    beam_power = lax.map(one_channel, (jnp.arange(CH, dtype=jnp.int32), spectra, gains))
    chosen = jnp.take(beam_power, search_beams, axis=1)
    power_spectra = jnp.dot(chosen.reshape(CH * SEARCH, TIME), time_table(), precision=lax.Precision.HIGHEST, preferred_element_type=jnp.float32)
    power_spectra = power_spectra.reshape(CH, SEARCH, TIME)
    dm_plane = dedisperse(power_spectra, delays)
    return (beam_power, dm_plane)
```

```python
import functools
import math

import jax
import jax.numpy as jnp
import numpy as np
from jax import lax
from jax.experimental import pallas as pl
from jax.experimental.pallas import tpu as pltpu
from jax.sharding import PartitionSpec as P

CH = 256
TAPS = 4
TIME = 32
FFTLEN = 512
HALF_BINS = TIME // 2
TWO_PI = 2.0 * math.pi
F32 = jnp.float32
BF16 = jnp.bfloat16
NT = (((1,), (1,)), ((), ()))

SIN_POLY = (
    6.283185302511503,
    -41.34170040531769,
    81.60513138580204,
    -76.7030153539128,
    42.02592698618416,
    -14.899846668691637,
    3.238137510515757,
)
COS_POLY = (
    0.9999999890590228,
    -19.739204499454026,
    64.93911745990036,
    -85.45013953095037,
    60.16763093136588,
    -25.96759924965491,
    6.528658162567069,
)


def pfb_window():
    n = np.arange(TAPS * FFTLEN, dtype=np.float64)
    offsets = (n - 0.5 * TAPS * FFTLEN + 0.5) / FFTLEN
    tapering = 0.54 - 0.46 * np.cos(TWO_PI * n / (TAPS * FFTLEN - 1))
    return (np.sinc(offsets) * tapering).reshape(TAPS, FFTLEN).astype(np.float32)


def dft_table():
    turns = np.arange(CH)[:, None] * np.arange(FFTLEN)[None, :] % FFTLEN
    angles = TWO_PI * turns / FFTLEN
    stacked = np.stack([np.cos(angles), -np.sin(angles)], axis=1) / math.sqrt(FFTLEN)
    return stacked.reshape(2 * CH, FFTLEN).astype(np.float32)


def time_table(search):
    turns = np.arange(TIME)[:, None] * np.arange(1, HALF_BINS + 1)[None, :] % TIME
    angles = TWO_PI * turns / TIME
    table = np.concatenate([np.cos(angles), -np.sin(angles)], axis=1) / math.sqrt(TIME)
    full = np.einsum("tk,qp->tqpk", table, np.eye(search))
    return full.reshape(TIME * search, search * TIME).astype(np.float32)


def polynomial(z, coefficients):
    total = jnp.full_like(z, coefficients[-1])
    for value in coefficients[-2::-1]:
        total = total * z + value
    return total


def cos_sin_turns(turns):
    r = turns - jnp.round(turns)
    z = r * r
    return polynomial(z, COS_POLY), polynomial(z, SIN_POLY) * r


def split_bf16(x):
    high = x.astype(BF16)
    return high, (x - high.astype(F32)).astype(BF16)


def transform_rows(table, folded_ref, spread_ref, out_ref):
    inputs = out_ref.shape[-1]
    rows = table.shape[0]
    group = 2 if inputs % 128 == 0 else 1

    def step(index, carry):
        start = pl.multiple_of(index * (group * inputs), group * inputs)
        frames = folded_ref[pl.ds(start, group * inputs), :]
        out = lax.dot_general(table, frames, NT, preferred_element_type=F32)
        for part in range(group):
            piece = out[:, part * inputs : (part + 1) * inputs]
            spread_ref[pl.ds(index * group + part, rows, stride=TIME), :] = piece
        return carry

    lax.fori_loop(0, TIME // group, step, 0, unroll=2)
    dests, chans = out_ref.shape[:2]
    per_chan = 2 * TIME

    def pack(dest, carry):
        for chan in range(chans):
            start = pl.multiple_of((dest * chans + chan) * per_chan, per_chan)
            out_ref[dest, chan] = spread_ref[pl.ds(start, per_chan), :].astype(BF16)
        return carry

    lax.fori_loop(0, dests, pack, 0)


def fold_kernel(half_ref, volt_ref, window_ref, table_ref, out_ref, folded_ref, spread_ref):
    step = pl.program_id(0)
    rows = volt_ref.shape[0]
    inputs = out_ref.shape[-1]
    lanes = 256
    for lane in range(0, FFTLEN, lanes):
        taps = [window_ref[j : j + 1, lane : lane + lanes] for j in range(TAPS)]
        for row in range(0, rows, 16):
            frames = []
            for t in range(TIME + TAPS - 1):
                start = t * FFTLEN + lane
                frames.append(volt_ref[row : row + 16, start : start + lanes].astype(F32))
                if t >= TAPS - 1:
                    first = t - TAPS + 1
                    total = taps[0] * frames[first]
                    for j in range(1, TAPS):
                        total = total + taps[j] * frames[first + j]
                    place = pl.multiple_of(first * inputs + step * rows + row, 16)
                    folded_ref[pl.ds(place, 16), lane : lane + lanes] = total.astype(BF16)

    @pl.when(step == pl.num_programs(0) - 1)
    def _():
        transform_rows(table_ref[...], folded_ref, spread_ref, out_ref)


def near_kernel(half_ref, folded_ref, table_ref, out_ref, spread_ref):
    transform_rows(table_ref[...], folded_ref, spread_ref, out_ref)


def beam_kernel(
    first_ref, x_ref, gain_ref, place_ref, dir_ref, out_ref, weight_ref, sum_ref
):
    step = pl.program_id(0)
    tiles = pl.num_programs(0) - 1
    chans, _, beams = out_ref.shape
    depth = place_ref.shape[0]
    wide = 256
    chunk = depth // chans
    now = lax.rem(step, 2)
    before = 1 - now

    def generate(part):
        for sub in range(0, chunk, 16):
            row = pl.multiple_of(part * chunk + sub, 16)
            place = place_ref[pl.ds(row, 16), :]
            for lane in range(0, beams, wide):
                lanes = slice(lane, lane + wide)
                direction = dir_ref[:, lanes]
                geometry = place[:, 0:1] * direction[0:1, :]
                geometry = geometry + place[:, 1:2] * direction[1:2, :]
                geometry = geometry + place[:, 2:3] * direction[2:3, :]
                first = 1.0 + first_ref[0].astype(F32) * (1.0 / CH)
                c, s = cos_sin_turns(geometry * first)
                dc, ds = cos_sin_turns(geometry * (1.0 / CH))
                for chan in range(chans):
                    weight_ref[now, chan, pl.ds(row, 16), lanes] = c.astype(BF16)
                    weight_ref[now, chan, pl.ds(depth + row, 16), lanes] = s.astype(BF16)
                    if chan + 1 < chans:
                        c, s = c * dc - s * ds, c * ds + s * dc

    def accumulate(chan):
        blocks = x_ref.shape[0]
        data = jnp.concatenate([x_ref[k, chan] for k in range(blocks)], axis=1).astype(F32)
        real, imag = data[:TIME], data[TIME:]
        gain = gain_ref[chan]
        x0 = (gain[0:1] * real - gain[1:2] * imag).astype(BF16)
        x1 = (gain[0:1] * imag + gain[1:2] * real).astype(BF16)
        top = jnp.concatenate([x0, x1], axis=1)
        bottom = jnp.concatenate([x1, -x0], axis=1)
        both = jnp.concatenate([top, bottom], axis=0)
        return jnp.dot(both, weight_ref[before, chan], preferred_element_type=F32)

    @pl.when(step == 0)
    def _():
        sum_ref[...] = jnp.zeros_like(sum_ref)
        lax.fori_loop(0, chans, lambda m, v: (generate(m), v)[1], 0)

    @pl.when((step > 0) & (step < tiles))
    def _():
        def both(m, v):
            sum_ref[m] += accumulate(m)
            generate(m)
            return v

        lax.fori_loop(0, chans, both, 0)

    @pl.when(step == tiles)
    def _():
        def last(m, v):
            out_ref[m] = (sum_ref[m] + accumulate(m)).astype(out_ref.dtype)
            return v

        lax.fori_loop(0, chans, last, 0)


def power_kernel(
    own_ref, far_ref, pick_ref, high_ref, low_ref, power_ref, spec_ref, chosen_ref
):
    step = pl.program_id(0)
    block, _, beams = own_ref.shape
    search = chosen_ref.shape[1] // TIME
    per = 128 // search
    total = own_ref[...] + far_ref[...].astype(F32)
    real, imag = total[:, :TIME], total[:, TIME:]
    power = (real * real + imag * imag) * (1.0 / 2048)
    power_ref[...] = power
    rows = power.reshape(block * TIME, beams)
    hit = lax.broadcasted_iota(jnp.int32, (beams, 128), 0) == pick_ref[...]
    hot = jnp.where(hit, 1.0, 0.0).astype(BF16)
    high, low = split_bf16(rows)
    picked = jnp.dot(high, hot, preferred_element_type=F32)
    picked = picked + jnp.dot(low, hot, preferred_element_type=F32)
    row_id = lax.broadcasted_iota(jnp.int32, (per, 128), 0)
    lane_id = lax.broadcasted_iota(jnp.int32, (per, 128), 1) // search
    for chan in range(block):
        pieces = []
        for j in range(TIME // per):
            start = chan * TIME + j * per
            piece = jnp.where(row_id == lane_id, picked[start : start + per], 0.0)
            pieces.append(jnp.sum(piece, axis=0, keepdims=True))
        chosen_ref[pl.ds(step * block + chan, 1), :] = jnp.concatenate(pieces, axis=1)

    @pl.when(step == pl.num_programs(0) - 1)
    def _():
        g_high, g_low = split_bf16(chosen_ref[...])
        spectrum = jnp.dot(g_high, high_ref[...], preferred_element_type=F32)
        spectrum = spectrum + jnp.dot(g_low, high_ref[...], preferred_element_type=F32)
        spectrum = spectrum + jnp.dot(g_high, low_ref[...], preferred_element_type=F32)
        spectrum = spectrum.astype(BF16)
        for dest in range(spec_ref.shape[0]):
            spec_ref[dest] = spectrum


def turn_kernel(delay_ref, high_ref, low_ref):
    trials, chans = delay_ref.shape
    dc, ds = cos_sin_turns(delay_ref[...].astype(F32) * (1.0 / TIME))
    c, s = dc, ds
    for k in range(HALF_BINS):
        rows = slice(k * trials, (k + 1) * trials)
        for value, start in ((c, 0), (s, chans)):
            high, low = split_bf16(value)
            high_ref[rows, start : start + chans] = high
            low_ref[rows, start : start + chans] = low
        c, s = c * dc - s * ds, c * ds + s * dc


def plane_kernel(spec_ref, high_ref, low_ref, out_ref):
    chans, width = spec_ref.shape
    search, _, trials = out_ref.shape
    spec = spec_ref[...].astype(F32)
    lane = lax.broadcasted_iota(jnp.int32, (chans, width), 1)
    is_real = lane % TIME < HALF_BINS
    ahead = pltpu.roll(spec, width - HALF_BINS, 1)
    behind = pltpu.roll(spec, HALF_BINS, 1)
    turned = jnp.where(is_real, -ahead, behind)
    both = jnp.concatenate([spec.astype(BF16), turned.astype(BF16)], axis=0)
    bin_id = lax.broadcasted_iota(jnp.int32, (trials, width), 1) % HALF_BINS
    plane = jnp.zeros((trials, width), F32)
    for k in range(HALF_BINS):
        rows = slice(k * trials, (k + 1) * trials)
        part = jnp.dot(high_ref[rows], both, preferred_element_type=F32)
        part = part + jnp.dot(low_ref[rows], both, preferred_element_type=F32)
        plane = jnp.where(bin_id == k, part, plane)
    out_ref[...] = (plane.T * (1.0 / math.sqrt(CH))).reshape(out_ref.shape)


PARAMS = pltpu.CompilerParams(vmem_limit_bytes=60 << 20)


def channelize(voltages, half_id, halves, chans):
    inputs, samples = voltages.shape
    rows = 2 * CH // halves
    dests = rows // 2 // chans
    window = jnp.asarray(pfb_window())
    table = jnp.asarray(dft_table()).astype(BF16)
    block = min(32, inputs)
    out = jax.ShapeDtypeStruct((dests, chans, 2 * TIME, inputs), BF16)
    folded = jax.ShapeDtypeStruct((TIME * inputs, FFTLEN), BF16)
    spread = pltpu.VMEM((rows * TIME, inputs), F32)
    whole4 = pl.BlockSpec(out.shape, lambda i, h: (0, 0, 0, 0))
    whole2 = pl.BlockSpec(folded.shape, lambda i, h: (0, 0))
    far, folded = pl.pallas_call(
        fold_kernel,
        out_shape=(out, folded),
        grid_spec=pltpu.PrefetchScalarGridSpec(
            num_scalar_prefetch=1,
            grid=(inputs // block,),
            in_specs=[
                pl.BlockSpec((block, samples), lambda i, h: (i, 0)),
                pl.BlockSpec(window.shape, lambda i, h: (0, 0)),
                pl.BlockSpec((rows, FFTLEN), lambda i, h: (halves - 1 - h[0], 0)),
            ],
            out_specs=(whole4, whole2),
            scratch_shapes=[spread],
        ),
        compiler_params=PARAMS,
        cost_estimate=pl.CostEstimate(
            flops=4 * rows * FFTLEN * TIME * inputs, bytes_accessed=14 << 20, transcendentals=0
        ),
        name="fold",
    )(half_id, voltages, window, table)
    near = pl.pallas_call(
        near_kernel,
        out_shape=out,
        grid_spec=pltpu.PrefetchScalarGridSpec(
            num_scalar_prefetch=1,
            grid=(1,),
            in_specs=[whole2, pl.BlockSpec((rows, FFTLEN), lambda i, h: (h[0], 0))],
            out_specs=whole4,
            scratch_shapes=[spread],
        ),
        compiler_params=PARAMS,
        cost_estimate=pl.CostEstimate(
            flops=2 * rows * FFTLEN * TIME * inputs, bytes_accessed=8 << 20, transcendentals=0
        ),
        name="near",
    )(half_id, folded, table)
    return far, near


def form_beams(x, gains, places, directions, first, out_type):
    sources, chans, rows, inputs = x.shape
    beams = directions.shape[1]
    total = sources * inputs
    if inputs != 128:
        x = x.transpose(1, 2, 0, 3).reshape(chans, rows, total // 128, 128)
        x = x.transpose(2, 0, 1, 3)
    depth = 256
    blocks = depth // 128
    tiles = total // depth
    return pl.pallas_call(
        beam_kernel,
        out_shape=jax.ShapeDtypeStruct((chans, rows, beams), out_type),
        grid_spec=pltpu.PrefetchScalarGridSpec(
            num_scalar_prefetch=1,
            grid=(tiles + 1,),
            in_specs=[
                pl.BlockSpec(
                    (blocks, chans, rows, 128), lambda i, f: (jnp.maximum(i - 1, 0), 0, 0, 0)
                ),
                pl.BlockSpec((chans, 2, depth), lambda i, f: (0, 0, jnp.maximum(i - 1, 0))),
                pl.BlockSpec((depth, 3), lambda i, f: (jnp.minimum(i, tiles - 1), 0)),
                pl.BlockSpec(directions.shape, lambda i, f: (0, 0)),
            ],
            out_specs=pl.BlockSpec((chans, rows, beams), lambda i, f: (0, 0, 0)),
            scratch_shapes=[
                pltpu.VMEM((2, chans, 2 * depth, beams), BF16),
                pltpu.VMEM((chans, rows, beams), F32),
            ],
        ),
        compiler_params=PARAMS,
        cost_estimate=pl.CostEstimate(
            flops=32 * chans * rows * total * beams, bytes_accessed=6 << 20, transcendentals=0
        ),
        name="beams",
    )(first, x, gains, places, directions)


def powers(own, far, search_beams, copies):
    chans, rows, beams = own.shape
    search = search_beams.shape[0]
    width = TIME * search
    pick = jnp.tile(search_beams, 128 // search)[None, :]
    table = time_table(search)
    high = jnp.asarray(table).astype(BF16)
    low = (jnp.asarray(table) - high.astype(F32)).astype(BF16)
    block = min(4, chans)
    cube = pl.BlockSpec((block, rows, beams), lambda i: (i, 0, 0))
    flat = lambda shape: pl.BlockSpec(shape, lambda i: (0,) * len(shape))
    return pl.pallas_call(
        power_kernel,
        out_shape=(
            jax.ShapeDtypeStruct((chans, TIME, beams), F32),
            jax.ShapeDtypeStruct((copies, chans, width), BF16),
        ),
        grid=(chans // block,),
        in_specs=[cube, cube, flat(pick.shape), flat(high.shape), flat(low.shape)],
        out_specs=(
            pl.BlockSpec((block, TIME, beams), lambda i: (i, 0, 0)),
            flat((copies, chans, width)),
        ),
        scratch_shapes=[pltpu.VMEM((chans, width), F32)],
        compiler_params=PARAMS,
        name="power",
    )(own, far, pick, high, low)


def on_device(voltages, gains, positions, directions, input_order, delays, search_beams):
    devices = lax.axis_size("crate")
    position = lax.axis_index("crate")
    chans = gains.shape[0]
    halves = 2
    per_half = devices // halves
    half_id = position // per_half
    members = [list(range(h * per_half, (h + 1) * per_half)) for h in range(halves)]
    partners = [(d, (d + per_half) % devices) for d in range(devices)]
    inputs = gains.shape[2] // halves

    own_inputs = half_id * inputs
    other_inputs = inputs - own_inputs
    far_gains = lax.ppermute(
        lax.dynamic_slice_in_dim(gains, other_inputs, inputs, 2), "crate", partners
    )
    near_gains = lax.dynamic_slice_in_dim(gains, own_inputs, inputs, 2)
    half_scalar = half_id.astype(jnp.int32).reshape(1)
    far, near = channelize(voltages, half_scalar, halves, chans)

    def exchange(x):
        return lax.all_to_all(
            x, "crate", split_axis=0, concat_axis=0, axis_index_groups=members, tiled=True
        )

    far = exchange(far)
    far, near = lax.optimization_barrier((far, near))
    near = exchange(near)

    order = lax.dynamic_slice_in_dim(input_order, own_inputs, inputs, 0)
    places = jnp.take(positions.T, order, axis=0)
    own_first = (position * chans).astype(jnp.int32).reshape(1)
    far_first = ((position + per_half) % devices * chans).astype(jnp.int32).reshape(1)
    far_sums = form_beams(far, far_gains, places, directions, far_first, BF16)
    far_sums = lax.ppermute(far_sums, "crate", partners)
    near_sums = form_beams(near, near_gains, places, directions, own_first, F32)

    beam_power, spectrum = powers(near_sums, far_sums, search_beams, devices)
    spectrum = lax.all_to_all(spectrum, "crate", split_axis=0, concat_axis=0, tiled=True)
    width = spectrum.shape[-1]
    trials = delays.shape[0] // devices
    own_delays = lax.dynamic_slice_in_dim(delays, position * trials, trials, 0)
    turns = jax.ShapeDtypeStruct((HALF_BINS * trials, 2 * CH), BF16)
    high, low = pl.pallas_call(
        turn_kernel, out_shape=(turns, turns), compiler_params=PARAMS, name="turns"
    )(own_delays)
    dm_plane = pl.pallas_call(
        plane_kernel,
        out_shape=jax.ShapeDtypeStruct((search_beams.shape[0], TIME, trials), F32),
        compiler_params=PARAMS,
        name="plane",
    )(spectrum.reshape(CH, width), high, low)
    return beam_power.transpose(0, 2, 1), dm_plane.transpose(2, 0, 1)


def solution(mesh):
    in_specs = (P(("groups", "crate"), None), P("crate", None, None), P(), P(), P(), P(), P())
    out_specs = (P(("groups", "crate"), None, None), P(("groups", "crate"), None, None))
    return jax.shard_map(
        on_device, mesh=mesh, in_specs=in_specs, out_specs=out_specs, check_vma=False
    )
```

```python
import functools
import math

import jax
import jax.numpy as jnp
import numpy as np
from jax import lax
from jax.experimental import pallas as pl
from jax.experimental.pallas import tpu as pltpu
from jax.sharding import PartitionSpec as P

CH = 256
TAPS = 4
TIME = 32
FFTLEN = 512
HALF_BINS = TIME // 2
TWO_PI = 2.0 * math.pi
F32 = jnp.float32
BF16 = jnp.bfloat16
NT = (((1,), (1,)), ((), ()))

SIN_POLY = (
    6.283185302511503,
    -41.34170040531769,
    81.60513138580204,
    -76.7030153539128,
    42.02592698618416,
    -14.899846668691637,
    3.238137510515757,
)
COS_POLY = (
    0.9999999890590228,
    -19.739204499454026,
    64.93911745990036,
    -85.45013953095037,
    60.16763093136588,
    -25.96759924965491,
    6.528658162567069,
)


def pfb_window():
    n = np.arange(TAPS * FFTLEN, dtype=np.float64)
    offsets = (n - 0.5 * TAPS * FFTLEN + 0.5) / FFTLEN
    tapering = 0.54 - 0.46 * np.cos(TWO_PI * n / (TAPS * FFTLEN - 1))
    return (np.sinc(offsets) * tapering).reshape(TAPS, FFTLEN).astype(np.float32)


def dft_table():
    turns = np.arange(CH)[:, None] * np.arange(FFTLEN)[None, :] % FFTLEN
    angles = TWO_PI * turns / FFTLEN
    stacked = np.stack([np.cos(angles), -np.sin(angles)], axis=1) / math.sqrt(FFTLEN)
    return stacked.reshape(2 * CH, FFTLEN).astype(np.float32)


def time_table(search):
    turns = np.arange(TIME)[:, None] * np.arange(1, HALF_BINS + 1)[None, :] % TIME
    angles = TWO_PI * turns / TIME
    table = np.concatenate([np.cos(angles), -np.sin(angles)], axis=1) / math.sqrt(TIME)
    full = np.einsum("tk,qp->tqpk", table, np.eye(search))
    return full.reshape(TIME * search, search * TIME).astype(np.float32)


def polynomial(z, coefficients):
    total = jnp.full_like(z, coefficients[-1])
    for value in coefficients[-2::-1]:
        total = total * z + value
    return total


def cos_sin_turns(turns):
    r = turns - jnp.round(turns)
    z = r * r
    return polynomial(z, COS_POLY), polynomial(z, SIN_POLY) * r


def split_bf16(x):
    high = x.astype(BF16)
    return high, (x - high.astype(F32)).astype(BF16)


def transform_rows(table, folded_ref, spread_ref, out_ref):
    inputs = out_ref.shape[-1]
    rows = table.shape[0]
    group = 2 if inputs % 128 == 0 else 1

    def step(index, carry):
        start = pl.multiple_of(index * (group * inputs), group * inputs)
        frames = folded_ref[pl.ds(start, group * inputs), :]
        out = lax.dot_general(table, frames, NT, preferred_element_type=F32)
        for part in range(group):
            piece = out[:, part * inputs : (part + 1) * inputs]
            spread_ref[pl.ds(index * group + part, rows, stride=TIME), :] = piece
        return carry

    lax.fori_loop(0, TIME // group, step, 0, unroll=4)
    dests, chans = out_ref.shape[:2]
    per_chan = 2 * TIME

    def pack(dest, carry):
        for chan in range(chans):
            start = pl.multiple_of((dest * chans + chan) * per_chan, per_chan)
            out_ref[dest, chan] = spread_ref[pl.ds(start, per_chan), :].astype(BF16)
        return carry

    lax.fori_loop(0, dests, pack, 0, unroll=2)


def fold_kernel(half_ref, volt_ref, window_ref, table_ref, out_ref, folded_ref, spread_ref):
    step = pl.program_id(0)
    rows = volt_ref.shape[0]
    inputs = out_ref.shape[-1]
    lanes = 256
    for lane in range(0, FFTLEN, lanes):
        taps = [window_ref[j : j + 1, lane : lane + lanes] for j in range(TAPS)]
        for row in range(0, rows, 16):
            frames = []
            for t in range(TIME + TAPS - 1):
                start = t * FFTLEN + lane
                frames.append(volt_ref[row : row + 16, start : start + lanes].astype(F32))
                if t >= TAPS - 1:
                    first = t - TAPS + 1
                    total = taps[0] * frames[first]
                    for j in range(1, TAPS):
                        total = total + taps[j] * frames[first + j]
                    place = pl.multiple_of(first * inputs + step * rows + row, 16)
                    folded_ref[pl.ds(place, 16), lane : lane + lanes] = total.astype(BF16)

    @pl.when(step == pl.num_programs(0) - 1)
    def _():
        transform_rows(table_ref[...], folded_ref, spread_ref, out_ref)


def near_kernel(half_ref, folded_ref, table_ref, out_ref, spread_ref):
    transform_rows(table_ref[...], folded_ref, spread_ref, out_ref)


def beam_kernel(
    first_ref, x_ref, gain_ref, place_ref, dir_ref, out_ref, even_ref, odd_ref, sum_ref
):
    step = pl.program_id(0)
    tiles = pl.num_programs(0) - 1
    chans, _, beams = out_ref.shape
    depth = place_ref.shape[0]
    wide = 256
    chunk = depth // chans

    def generate(part, weight_ref):
        for sub in range(0, chunk, 16):
            row = pl.multiple_of(part * chunk + sub, 16)
            place = place_ref[pl.ds(row, 16), :]
            for lane in range(0, beams, wide):
                lanes = slice(lane, lane + wide)
                direction = dir_ref[:, lanes]
                geometry = place[:, 0:1] * direction[0:1, :]
                geometry = geometry + place[:, 1:2] * direction[1:2, :]
                geometry = geometry + place[:, 2:3] * direction[2:3, :]
                first = 1.0 + first_ref[0].astype(F32) * (1.0 / CH)
                c, s = cos_sin_turns(geometry * first)
                dc, ds = cos_sin_turns(geometry * (1.0 / CH))
                next_c, next_s = c * dc - s * ds, c * ds + s * dc
                twice = dc + dc
                for chan in range(chans):
                    weight_ref[chan, pl.ds(row, 16), lanes] = c.astype(BF16)
                    weight_ref[chan, pl.ds(depth + row, 16), lanes] = s.astype(BF16)
                    if chan + 2 < chans:
                        c, next_c = next_c, twice * next_c - c
                        s, next_s = next_s, twice * next_s - s
                    else:
                        c, s = next_c, next_s

    def accumulate(chan, weight_ref):
        blocks = x_ref.shape[0]
        data = jnp.concatenate([x_ref[k, chan] for k in range(blocks)], axis=1).astype(F32)
        real, imag = data[:TIME], data[TIME:]
        gain = gain_ref[chan]
        x0 = (gain[0:1] * real - gain[1:2] * imag).astype(BF16)
        x1 = (gain[0:1] * imag + gain[1:2] * real).astype(BF16)
        top = jnp.concatenate([x0, x1], axis=1)
        bottom = jnp.concatenate([x1, -x0], axis=1)
        both = jnp.concatenate([top, bottom], axis=0)
        return jnp.dot(both, weight_ref[chan], preferred_element_type=F32)

    def both(m, weights):
        sum_ref[m] += accumulate(m, weights[0])
        generate(m, weights[1])

    def last(m, weights):
        out_ref[m] = (sum_ref[m] + accumulate(m, weights[0])).astype(out_ref.dtype)

    def over_channels(body, weights):
        lax.fori_loop(0, chans, lambda m, v: (body(m, weights), v)[1], 0, unroll=min(8, chans))

    @pl.when(step == 0)
    def _():
        sum_ref[...] = jnp.zeros_like(sum_ref)
        over_channels(lambda m, w: generate(m, w), even_ref)

    for parity, weights in ((1, (even_ref, odd_ref)), (0, (odd_ref, even_ref))):

        @pl.when((step > 0) & (step < tiles) & (lax.rem(step, 2) == parity))
        def _(weights=weights):
            over_channels(both, weights)

        @pl.when((step == tiles) & (lax.rem(step, 2) == parity))
        def _(weights=weights):
            over_channels(last, weights)


def power_kernel(
    own_ref, far0_ref, far1_ref, pick_ref, high_ref, low_ref, power_ref, spec_ref, chosen_ref
):
    step = pl.program_id(0)
    block, _, beams = own_ref.shape
    search = chosen_ref.shape[1] // TIME
    per = 128 // search
    far = jnp.concatenate([far0_ref[...], far1_ref[...]], axis=2)
    total = own_ref[...] + far.astype(F32)
    real, imag = total[:, :TIME], total[:, TIME:]
    power = (real * real + imag * imag) * (1.0 / 2048)
    power_ref[...] = power
    rows = power.reshape(block * TIME, beams)
    hit = lax.broadcasted_iota(jnp.int32, (beams, 128), 0) == pick_ref[...]
    hot = jnp.where(hit, 1.0, 0.0).astype(BF16)
    high, low = split_bf16(rows)
    picked = jnp.dot(high, hot, preferred_element_type=F32)
    picked = picked + jnp.dot(low, hot, preferred_element_type=F32)
    row_id = lax.broadcasted_iota(jnp.int32, (per, 128), 0)
    lane_id = lax.broadcasted_iota(jnp.int32, (per, 128), 1) // search
    for chan in range(block):
        pieces = []
        for j in range(TIME // per):
            start = chan * TIME + j * per
            piece = jnp.where(row_id == lane_id, picked[start : start + per], 0.0)
            pieces.append(jnp.sum(piece, axis=0, keepdims=True))
        chosen_ref[pl.ds(step * block + chan, 1), :] = jnp.concatenate(pieces, axis=1)

    @pl.when(step == pl.num_programs(0) - 1)
    def _():
        g_high, g_low = split_bf16(chosen_ref[...])
        spectrum = jnp.dot(g_high, high_ref[...], preferred_element_type=F32)
        spectrum = spectrum + jnp.dot(g_low, high_ref[...], preferred_element_type=F32)
        spectrum = spectrum + jnp.dot(g_high, low_ref[...], preferred_element_type=F32)
        spectrum = spectrum.astype(BF16)
        for dest in range(spec_ref.shape[0]):
            spec_ref[dest] = spectrum


def turn_kernel(delay_ref, high_ref, low_ref):
    trials, chans = delay_ref.shape
    dc, ds = cos_sin_turns(delay_ref[...].astype(F32) * (1.0 / TIME))
    c, s = dc, ds
    for k in range(HALF_BINS):
        rows = slice(k * trials, (k + 1) * trials)
        for value, start in ((c, 0), (s, chans)):
            high, low = split_bf16(value)
            high_ref[rows, start : start + chans] = high
            low_ref[rows, start : start + chans] = low
        c, s = c * dc - s * ds, c * ds + s * dc


def plane_kernel(spec_ref, high_ref, low_ref, out_ref):
    chans, width = spec_ref.shape
    search, _, trials = out_ref.shape
    spec = spec_ref[...].astype(F32)
    lane = lax.broadcasted_iota(jnp.int32, (chans, width), 1)
    is_real = lane % TIME < HALF_BINS
    ahead = pltpu.roll(spec, width - HALF_BINS, 1)
    behind = pltpu.roll(spec, HALF_BINS, 1)
    turned = jnp.where(is_real, -ahead, behind)
    both = jnp.concatenate([spec.astype(BF16), turned.astype(BF16)], axis=0)
    bin_id = lax.broadcasted_iota(jnp.int32, (trials, width), 1) % HALF_BINS
    plane = jnp.zeros((trials, width), F32)
    for k in range(HALF_BINS):
        rows = slice(k * trials, (k + 1) * trials)
        part = jnp.dot(high_ref[rows], both, preferred_element_type=F32)
        part = part + jnp.dot(low_ref[rows], both, preferred_element_type=F32)
        plane = jnp.where(bin_id == k, part, plane)
    out_ref[...] = (plane.T * (1.0 / math.sqrt(CH))).reshape(out_ref.shape)


PARAMS = pltpu.CompilerParams(vmem_limit_bytes=60 << 20)


def channelize(voltages, half_id, halves, chans):
    inputs, samples = voltages.shape
    rows = 2 * CH // halves
    dests = rows // 2 // chans
    window = jnp.asarray(pfb_window())
    table = jnp.asarray(dft_table()).astype(BF16)
    block = min(32, inputs)
    out = jax.ShapeDtypeStruct((dests, chans, 2 * TIME, inputs), BF16)
    folded = jax.ShapeDtypeStruct((TIME * inputs, FFTLEN), BF16)
    spread = pltpu.VMEM((rows * TIME, inputs), F32)
    whole4 = pl.BlockSpec(out.shape, lambda i, h: (0, 0, 0, 0))
    whole2 = pl.BlockSpec(folded.shape, lambda i, h: (0, 0))
    far, folded = pl.pallas_call(
        fold_kernel,
        out_shape=(out, folded),
        grid_spec=pltpu.PrefetchScalarGridSpec(
            num_scalar_prefetch=1,
            grid=(inputs // block,),
            in_specs=[
                pl.BlockSpec((block, samples), lambda i, h: (i, 0)),
                pl.BlockSpec(window.shape, lambda i, h: (0, 0)),
                pl.BlockSpec((rows, FFTLEN), lambda i, h: (halves - 1 - h[0], 0)),
            ],
            out_specs=(whole4, whole2),
            scratch_shapes=[spread],
        ),
        compiler_params=PARAMS,
        cost_estimate=pl.CostEstimate(
            flops=4 * rows * FFTLEN * TIME * inputs, bytes_accessed=14 << 20, transcendentals=0
        ),
        name="fold",
    )(half_id, voltages, window, table)
    near = pl.pallas_call(
        near_kernel,
        out_shape=out,
        grid_spec=pltpu.PrefetchScalarGridSpec(
            num_scalar_prefetch=1,
            grid=(1,),
            in_specs=[whole2, pl.BlockSpec((rows, FFTLEN), lambda i, h: (h[0], 0))],
            out_specs=whole4,
            scratch_shapes=[spread],
        ),
        compiler_params=PARAMS,
        cost_estimate=pl.CostEstimate(
            flops=2 * rows * FFTLEN * TIME * inputs, bytes_accessed=8 << 20, transcendentals=0
        ),
        name="near",
    )(half_id, folded, table)
    return far, near


def form_beams(x, gains, places, directions, first, out_type):
    sources, chans, rows, inputs = x.shape
    beams = directions.shape[1]
    total = sources * inputs
    if inputs != 128:
        x = x.transpose(1, 2, 0, 3).reshape(chans, rows, total // 128, 128)
        x = x.transpose(2, 0, 1, 3)
    depth = 256
    blocks = depth // 128
    tiles = total // depth
    return pl.pallas_call(
        beam_kernel,
        out_shape=jax.ShapeDtypeStruct((chans, rows, beams), out_type),
        grid_spec=pltpu.PrefetchScalarGridSpec(
            num_scalar_prefetch=1,
            grid=(tiles + 1,),
            in_specs=[
                pl.BlockSpec(
                    (blocks, chans, rows, 128), lambda i, f: (jnp.maximum(i - 1, 0), 0, 0, 0)
                ),
                pl.BlockSpec((chans, 2, depth), lambda i, f: (0, 0, jnp.maximum(i - 1, 0))),
                pl.BlockSpec((depth, 3), lambda i, f: (jnp.minimum(i, tiles - 1), 0)),
                pl.BlockSpec(directions.shape, lambda i, f: (0, 0)),
            ],
            out_specs=pl.BlockSpec((chans, rows, beams), lambda i, f: (0, 0, 0)),
            scratch_shapes=[
                pltpu.VMEM((chans, 2 * depth, beams), BF16),
                pltpu.VMEM((chans, 2 * depth, beams), BF16),
                pltpu.VMEM((chans, rows, beams), F32),
            ],
        ),
        compiler_params=PARAMS,
        cost_estimate=pl.CostEstimate(
            flops=32 * chans * rows * total * beams, bytes_accessed=6 << 20, transcendentals=0
        ),
        name="beams",
    )(first, x, gains, places, directions)


def powers(own, far, pick, search, copies):
    chans, rows, beams = own.shape
    width = TIME * search
    table = time_table(search)
    high = jnp.asarray(table).astype(BF16)
    low = (jnp.asarray(table) - high.astype(F32)).astype(BF16)
    block = min(4, chans)
    cube = pl.BlockSpec((block, rows, beams), lambda i: (i, 0, 0))
    far_cubes = [pl.BlockSpec((block, rows, x.shape[2]), lambda i: (i, 0, 0)) for x in far]
    flat = lambda shape: pl.BlockSpec(shape, lambda i: (0,) * len(shape))
    return pl.pallas_call(
        power_kernel,
        out_shape=(
            jax.ShapeDtypeStruct((chans, TIME, beams), F32),
            jax.ShapeDtypeStruct((copies, chans, width), BF16),
        ),
        grid=(chans // block,),
        in_specs=[cube, *far_cubes, flat(pick.shape), flat(high.shape), flat(low.shape)],
        out_specs=(
            pl.BlockSpec((block, TIME, beams), lambda i: (i, 0, 0)),
            flat((copies, chans, width)),
        ),
        scratch_shapes=[pltpu.VMEM((chans, width), F32)],
        compiler_params=PARAMS,
        name="power",
    )(own, *far, pick, high, low)


def on_device(voltages, gains, positions, directions, input_order, delays, search_beams):
    devices = lax.axis_size("crate")
    position = lax.axis_index("crate")
    chans = gains.shape[0]
    halves = 2
    per_half = devices // halves
    half_id = position // per_half
    members = [list(range(h * per_half, (h + 1) * per_half)) for h in range(halves)]
    partners = [(d, (d + per_half) % devices) for d in range(devices)]
    inputs = gains.shape[2] // halves
    own_inputs = half_id * inputs
    half_scalar = half_id.astype(jnp.int32).reshape(1)
    far, near = channelize(voltages, half_scalar, halves, chans)

    def exchange(x):
        return lax.all_to_all(
            x, "crate", split_axis=0, concat_axis=0, axis_index_groups=members, tiled=True
        )

    far = exchange(far)
    near, gains, positions = lax.optimization_barrier((near, gains, positions))
    far_gains = lax.ppermute(
        lax.dynamic_slice_in_dim(gains, inputs - own_inputs, inputs, 2), "crate", partners
    )
    near_gains = lax.dynamic_slice_in_dim(gains, own_inputs, inputs, 2)
    order = lax.dynamic_slice_in_dim(input_order, own_inputs, inputs, 0)
    places = jnp.take(positions.T, order, axis=0)
    search = search_beams.shape[0]
    pick = jnp.tile(search_beams, 128 // search)[None, :]
    own_first = (position * chans).astype(jnp.int32).reshape(1)
    far_first = ((position + per_half) % devices * chans).astype(jnp.int32).reshape(1)
    far, near, far_gains, near_gains, places, pick = lax.optimization_barrier(
        (far, near, far_gains, near_gains, places, pick)
    )
    near = exchange(near)

    beams = directions.shape[1]
    cut = beams // 2
    far_sums = []
    for start in range(0, beams, cut):
        some = lax.slice_in_dim(directions, start, start + cut, axis=1)
        part = form_beams(far, far_gains, places, some, far_first, BF16)
        far_sums.append(lax.ppermute(part, "crate", partners))
    near_sums = form_beams(near, near_gains, places, directions, own_first, F32)

    beam_power, spectrum = powers(near_sums, far_sums, pick, search, devices)
    spectrum = lax.all_to_all(spectrum, "crate", split_axis=0, concat_axis=0, tiled=True)
    width = spectrum.shape[-1]
    trials = delays.shape[0] // devices
    own_delays = lax.dynamic_slice_in_dim(delays, position * trials, trials, 0)
    turns = jax.ShapeDtypeStruct((HALF_BINS * trials, 2 * CH), BF16)
    high, low = pl.pallas_call(
        turn_kernel, out_shape=(turns, turns), compiler_params=PARAMS, name="turns"
    )(own_delays)
    dm_plane = pl.pallas_call(
        plane_kernel,
        out_shape=jax.ShapeDtypeStruct((search_beams.shape[0], TIME, trials), F32),
        compiler_params=PARAMS,
        name="plane",
    )(spectrum.reshape(CH, width), high, low)
    return beam_power.transpose(0, 2, 1), dm_plane.transpose(2, 0, 1)


def solution(mesh):
    in_specs = (P(("groups", "crate"), None), P("crate", None, None), P(), P(), P(), P(), P())
    out_specs = (P(("groups", "crate"), None, None), P(("groups", "crate"), None, None))
    return jax.shard_map(
        on_device, mesh=mesh, in_specs=in_specs, out_specs=out_specs, check_vma=False
    )
```

```python
import functools
import math

import jax
import jax.numpy as jnp
import numpy as np
from jax import lax
from jax.experimental import pallas as pl
from jax.experimental.pallas import tpu as pltpu
from jax.sharding import PartitionSpec as P

CH = 256
TAPS = 4
TIME = 32
PITCH = 40
PARTS = 2
FFTLEN = 512
HALF_BINS = TIME // 2
TWO_PI = 2.0 * math.pi
F32 = jnp.float32
BF16 = jnp.bfloat16
NT = (((1,), (1,)), ((), ()))

SIN_POLY = (
    6.283185302511503,
    -41.34170040531769,
    81.60513138580204,
    -76.7030153539128,
    42.02592698618416,
    -14.899846668691637,
    3.238137510515757,
)
COS_POLY = (
    0.9999999890590228,
    -19.739204499454026,
    64.93911745990036,
    -85.45013953095037,
    60.16763093136588,
    -25.96759924965491,
    6.528658162567069,
)


def pfb_window():
    n = np.arange(TAPS * FFTLEN, dtype=np.float64)
    offsets = (n - 0.5 * TAPS * FFTLEN + 0.5) / FFTLEN
    tapering = 0.54 - 0.46 * np.cos(TWO_PI * n / (TAPS * FFTLEN - 1))
    return (np.sinc(offsets) * tapering).reshape(TAPS, FFTLEN).astype(np.float32)


def dft_table(halves, dests, chans):
    ids = np.arange(CH).reshape(halves, dests, PARTS, chans // PARTS)
    ids = ids.transpose(0, 2, 1, 3).reshape(CH)
    angles = TWO_PI * (ids[:, None] * np.arange(FFTLEN)[None, :] % FFTLEN) / FFTLEN
    stacked = np.stack([np.cos(angles), -np.sin(angles)], axis=1) / math.sqrt(FFTLEN)
    return stacked.reshape(2 * CH, FFTLEN).astype(np.float32)


def time_table(search):
    turns = np.arange(TIME)[:, None] * np.arange(1, HALF_BINS + 1)[None, :] % TIME
    angles = TWO_PI * turns / TIME
    table = np.concatenate([np.cos(angles), -np.sin(angles)], axis=1) / math.sqrt(TIME)
    full = np.einsum("tk,qp->tqpk", table, np.eye(search))
    return full.reshape(TIME * search, search * TIME).astype(np.float32)


def polynomial(z, coefficients):
    total = jnp.full_like(z, coefficients[-1])
    for value in coefficients[-2::-1]:
        total = total * z + value
    return total


def cos_sin_turns(turns):
    r = turns - jnp.round(turns)
    z = r * r
    return polynomial(z, COS_POLY), polynomial(z, SIN_POLY) * r


def split_bf16(x):
    high = x.astype(BF16)
    return high, (x - high.astype(F32)).astype(BF16)


def transform_rows(table, folded_ref, spread_ref, out_ref, first_chan, chans):
    dests, inputs = out_ref.shape[0], out_ref.shape[-1]
    rows = table.shape[0]
    group = 2 if inputs % 128 == 0 else 1

    def step(index, carry):
        start = pl.multiple_of(index * (group * inputs), group * inputs)
        frames = folded_ref[pl.ds(start, group * inputs), :]
        out = lax.dot_general(table, frames, NT, preferred_element_type=F32)
        for part in range(group):
            piece = out[:, part * inputs : (part + 1) * inputs]
            spread_ref[pl.ds(index * group + part, rows, stride=PITCH), :] = piece
        return carry

    lax.fori_loop(0, TIME // group, step, 0, unroll=8)

    def pack(dest, carry):
        for chan in range(chans):
            for part in range(2):
                start = pl.multiple_of(((dest * chans + chan) * 2 + part) * PITCH, 8)
                block = spread_ref[pl.ds(start, TIME), :].astype(BF16)
                out_ref[dest, first_chan + chan, part * TIME : (part + 1) * TIME] = block
        return carry

    lax.fori_loop(0, dests, pack, 0, unroll=4)


def fold_kernel(half_ref, volt_ref, window_ref, table_ref, out_ref, folded_ref, spread_ref):
    step = pl.program_id(0)
    rows = volt_ref.shape[0]
    inputs = out_ref.shape[-1]
    lanes = 256
    for lane in range(0, FFTLEN, lanes):
        taps = [window_ref[j : j + 1, lane : lane + lanes] for j in range(TAPS)]
        for row in range(0, rows, 16):
            frames = []
            for t in range(TIME + TAPS - 1):
                start = t * FFTLEN + lane
                frames.append(volt_ref[row : row + 16, start : start + lanes].astype(F32))
                if t >= TAPS - 1:
                    first = t - TAPS + 1
                    total = taps[0] * frames[first]
                    for j in range(1, TAPS):
                        total = total + taps[j] * frames[first + j]
                    place = pl.multiple_of(first * inputs + step * rows + row, 16)
                    folded_ref[pl.ds(place, 16), lane : lane + lanes] = total.astype(BF16)

    @pl.when(step == pl.num_programs(0) - 1)
    def _():
        transform_rows(table_ref[...], folded_ref, spread_ref, out_ref, 0, out_ref.shape[1])


def spectra_kernel(base_ref, folded_ref, table_ref, out_ref, spread_ref):
    chans = out_ref.shape[1] // table_ref.shape[0]
    for part in range(table_ref.shape[0]):
        table = table_ref[part]
        transform_rows(table, folded_ref, spread_ref, out_ref, part * chans, chans)


def beam_kernel(mode, first_ref, x_ref, gain_ref, *refs):
    if mode == "start":
        place_ref, dir_ref, out_ref, dc_ref, ds_ref, c_ref, s_ref = refs[:-3]
    elif mode == "more":
        dc_ref, ds_ref, c_ref, s_ref, out_ref = refs[:-3]
    else:
        place_ref, dir_ref, dc_ref, ds_ref, out_ref = refs[:-3]
    even_ref, odd_ref, sum_ref = refs[-3:]
    step = pl.program_id(0)
    tiles = pl.num_programs(0) - 1
    chans, _, beams = out_ref.shape
    depth = dc_ref.shape[0]
    wide = 256
    chunk = depth // chans

    def generate(part, weight_ref):
        for sub in range(0, chunk, 16):
            row = pl.multiple_of(part * chunk + sub, 16)
            rows = pl.ds(row, 16)
            for lane in range(0, beams, wide):
                lanes = slice(lane, lane + wide)
                if mode != "more":
                    place = place_ref[rows, :]
                    direction = dir_ref[:, lanes]
                    geometry = place[:, 0:1] * direction[0:1, :]
                    geometry = geometry + place[:, 1:2] * direction[1:2, :]
                    geometry = geometry + place[:, 2:3] * direction[2:3, :]
                    first = 1.0 + first_ref[0].astype(F32) * (1.0 / CH)
                    c, s = cos_sin_turns(geometry * first)
                else:
                    c, s = c_ref[rows, lanes], s_ref[rows, lanes]
                if mode == "start":
                    dc, ds = cos_sin_turns(geometry * (1.0 / CH))
                    dc_ref[rows, lanes] = dc
                    ds_ref[rows, lanes] = ds
                else:
                    dc, ds = dc_ref[rows, lanes], ds_ref[rows, lanes]
                next_c, next_s = c * dc - s * ds, c * ds + s * dc
                twice = dc + dc
                for chan in range(chans):
                    weight_ref[chan, rows, lanes] = c.astype(BF16)
                    weight_ref[chan, pl.ds(depth + row, 16), lanes] = s.astype(BF16)
                    if chan + 2 < chans + (mode == "start"):
                        c, next_c = next_c, twice * next_c - c
                        s, next_s = next_s, twice * next_s - s
                    else:
                        c, s = next_c, next_s
                if mode == "start":
                    c_ref[rows, lanes] = c
                    s_ref[rows, lanes] = s

    def accumulate(chan, weight_ref):
        blocks = x_ref.shape[0]
        data = jnp.concatenate([x_ref[k, chan] for k in range(blocks)], axis=1).astype(F32)
        real, imag = data[:TIME], data[TIME:]
        gain = gain_ref[chan]
        x0 = (gain[0:1] * real - gain[1:2] * imag).astype(BF16)
        x1 = (gain[0:1] * imag + gain[1:2] * real).astype(BF16)
        top = jnp.concatenate([x0, x1], axis=1)
        bottom = jnp.concatenate([x1, -x0], axis=1)
        both = jnp.concatenate([top, bottom], axis=0)
        return jnp.dot(both, weight_ref[chan], preferred_element_type=F32)

    def both(m, weights):
        sum_ref[m] += accumulate(m, weights[0])
        generate(m, weights[1])

    def last(m, weights):
        out_ref[m] = (sum_ref[m] + accumulate(m, weights[0])).astype(out_ref.dtype)

    def over_channels(body, weights):
        unroll = min(4, chans)
        lax.fori_loop(0, chans, lambda m, v: (body(m, weights), v)[1], 0, unroll=unroll)

    @pl.when(step == 0)
    def _():
        sum_ref[...] = jnp.zeros_like(sum_ref)
        over_channels(generate, even_ref)

    for parity, weights in ((1, (even_ref, odd_ref)), (0, (odd_ref, even_ref))):

        @pl.when((step > 0) & (step < tiles) & (lax.rem(step, 2) == parity))
        def _(weights=weights):
            over_channels(both, weights)

        @pl.when((step == tiles) & (lax.rem(step, 2) == parity))
        def _(weights=weights):
            over_channels(last, weights)


def power_kernel(
    own_ref, far0_ref, far1_ref, pick_ref, high_ref, low_ref, power_ref, spec_ref, chosen_ref
):
    step = pl.program_id(0)
    block, _, beams = own_ref.shape
    search = chosen_ref.shape[1] // TIME
    per = 128 // search
    early = step < pl.num_programs(0) // PARTS
    far = jnp.where(early, far0_ref[...].astype(F32), far1_ref[...].astype(F32))
    total = own_ref[...] + far
    real, imag = total[:, :TIME], total[:, TIME:]
    power = (real * real + imag * imag) * (1.0 / 2048)
    power_ref[...] = power
    rows = power.reshape(block * TIME, beams)
    hit = lax.broadcasted_iota(jnp.int32, (beams, 128), 0) == pick_ref[...]
    hot = jnp.where(hit, 1.0, 0.0).astype(BF16)
    high, low = split_bf16(rows)
    picked = jnp.dot(high, hot, preferred_element_type=F32)
    picked = picked + jnp.dot(low, hot, preferred_element_type=F32)
    row_id = lax.broadcasted_iota(jnp.int32, (per, 128), 0)
    lane_id = lax.broadcasted_iota(jnp.int32, (per, 128), 1) // search
    for chan in range(block):
        pieces = []
        for j in range(TIME // per):
            start = chan * TIME + j * per
            piece = jnp.where(row_id == lane_id, picked[start : start + per], 0.0)
            pieces.append(jnp.sum(piece, axis=0, keepdims=True))
        chosen_ref[pl.ds(step * block + chan, 1), :] = jnp.concatenate(pieces, axis=1)

    @pl.when(step == pl.num_programs(0) - 1)
    def _():
        g_high, g_low = split_bf16(chosen_ref[...])
        spectrum = jnp.dot(g_high, high_ref[...], preferred_element_type=F32)
        spectrum = spectrum + jnp.dot(g_low, high_ref[...], preferred_element_type=F32)
        spectrum = spectrum + jnp.dot(g_high, low_ref[...], preferred_element_type=F32)
        spectrum = spectrum.astype(BF16)
        for dest in range(spec_ref.shape[0]):
            spec_ref[dest] = spectrum


def turn_kernel(delay_ref, high_ref, low_ref):
    trials, chans = delay_ref.shape
    dc, ds = cos_sin_turns(delay_ref[...].astype(F32) * (1.0 / TIME))
    c, s = dc, ds
    for k in range(HALF_BINS):
        rows = slice(k * trials, (k + 1) * trials)
        for value, start in ((c, 0), (s, chans)):
            high, low = split_bf16(value)
            high_ref[rows, start : start + chans] = high
            low_ref[rows, start : start + chans] = low
        c, s = c * dc - s * ds, c * ds + s * dc


def plane_kernel(spec_ref, high_ref, low_ref, out_ref):
    chans, width = spec_ref.shape
    _, _, trials = out_ref.shape
    spec = spec_ref[...].astype(F32)
    lane = lax.broadcasted_iota(jnp.int32, (chans, width), 1)
    is_real = lane % TIME < HALF_BINS
    ahead = pltpu.roll(spec, width - HALF_BINS, 1)
    behind = pltpu.roll(spec, HALF_BINS, 1)
    turned = jnp.where(is_real, -ahead, behind)
    both = jnp.concatenate([spec.astype(BF16), turned.astype(BF16)], axis=0)
    bin_id = lax.broadcasted_iota(jnp.int32, (trials, width), 1) % HALF_BINS
    plane = jnp.zeros((trials, width), F32)
    for k in range(HALF_BINS):
        rows = slice(k * trials, (k + 1) * trials)
        part = jnp.dot(high_ref[rows], both, preferred_element_type=F32)
        part = part + jnp.dot(low_ref[rows], both, preferred_element_type=F32)
        plane = jnp.where(bin_id == k, part, plane)
    out_ref[...] = (plane.T * (1.0 / math.sqrt(CH))).reshape(out_ref.shape)


PARAMS = pltpu.CompilerParams(vmem_limit_bytes=60 << 20)


def channel_table(halves, dests, chans):
    table = dft_table(halves, dests, chans).reshape(halves * PARTS, -1, FFTLEN)
    return jnp.asarray(table).astype(BF16)


def fold(voltages, table, block_id, dests, chans):
    inputs, samples = voltages.shape
    rows = table.shape[1]
    window = jnp.asarray(pfb_window())
    block = min(32, inputs)
    spectra = jax.ShapeDtypeStruct((dests, chans, 2 * TIME, inputs), BF16)
    folded = jax.ShapeDtypeStruct((TIME * inputs, FFTLEN), BF16)
    whole = lambda x: pl.BlockSpec(x.shape, lambda i, k: (0,) * len(x.shape))
    return pl.pallas_call(
        fold_kernel,
        out_shape=(spectra, folded),
        grid_spec=pltpu.PrefetchScalarGridSpec(
            num_scalar_prefetch=1,
            grid=(inputs // block,),
            in_specs=[
                pl.BlockSpec((block, samples), lambda i, k: (i, 0)),
                whole(window),
                pl.BlockSpec((None, rows, FFTLEN), lambda i, k: (k[0], 0, 0)),
            ],
            out_specs=(whole(spectra), whole(folded)),
            scratch_shapes=[pltpu.VMEM((rows * PITCH, inputs), F32)],
        ),
        compiler_params=PARAMS,
        cost_estimate=pl.CostEstimate(
            flops=8 * rows * FFTLEN * TIME * inputs, bytes_accessed=12 << 20, transcendentals=0
        ),
        name="fold",
    )(block_id, voltages, window, table)


def more_spectra(folded, table, block_id, blocks, dests, chans):
    rows = table.shape[1]
    inputs = folded.shape[0] // TIME
    out = jax.ShapeDtypeStruct((dests, chans * blocks, 2 * TIME, inputs), BF16)
    return pl.pallas_call(
        spectra_kernel,
        out_shape=out,
        grid_spec=pltpu.PrefetchScalarGridSpec(
            num_scalar_prefetch=1,
            grid=(1,),
            in_specs=[
                pl.BlockSpec(folded.shape, lambda i, k: (0, 0)),
                pl.BlockSpec((blocks, rows, FFTLEN), lambda i, k: (k[0], 0, 0)),
            ],
            out_specs=pl.BlockSpec(out.shape, lambda i, k: (0, 0, 0, 0)),
            scratch_shapes=[pltpu.VMEM((rows * PITCH, inputs), F32)],
        ),
        compiler_params=PARAMS,
        cost_estimate=pl.CostEstimate(
            flops=2 * blocks * rows * FFTLEN * TIME * inputs,
            bytes_accessed=6 << 20,
            transcendentals=0,
        ),
        name="spectra",
    )(block_id, folded, table)


def form_beams(mode, x, gains, part, first, places, directions, state, out_type):
    sources, chans, rows, inputs = x.shape
    beams = directions.shape[1]
    total = sources * inputs
    if inputs != 128:
        x = x.transpose(1, 2, 0, 3).reshape(chans, rows, total // 128, 128)
        x = x.transpose(2, 0, 1, 3)
    depth = 256
    blocks = depth // 128
    tiles = total // depth
    late = lambda i: jnp.maximum(i - 1, 0)
    now = lambda i: jnp.minimum(i, tiles - 1)
    state_spec = pl.BlockSpec((depth, beams), lambda i, f: (now(i), 0))
    in_specs = [
        pl.BlockSpec((blocks, chans, rows, 128), lambda i, f: (late(i), 0, 0, 0)),
        pl.BlockSpec((chans, 2, depth), lambda i, f: (part, 0, late(i))),
    ]
    operands = [x, gains]
    if mode != "more":
        in_specs.append(pl.BlockSpec((depth, 3), lambda i, f: (now(i), 0)))
        in_specs.append(pl.BlockSpec(directions.shape, lambda i, f: (0, 0)))
        operands += [places, directions]
    in_specs += [state_spec] * len(state)
    operands += state
    out_shape = [jax.ShapeDtypeStruct((chans, rows, beams), out_type)]
    out_specs = [pl.BlockSpec((chans, rows, beams), lambda i, f: (0, 0, 0))]
    if mode == "start":
        out_shape += [jax.ShapeDtypeStruct((total, beams), F32)] * 4
        out_specs += [state_spec] * 4
    return pl.pallas_call(
        functools.partial(beam_kernel, mode),
        out_shape=out_shape,
        grid_spec=pltpu.PrefetchScalarGridSpec(
            num_scalar_prefetch=1,
            grid=(tiles + 1,),
            in_specs=in_specs,
            out_specs=out_specs,
            scratch_shapes=[
                pltpu.VMEM((chans, 2 * depth, beams), BF16),
                pltpu.VMEM((chans, 2 * depth, beams), BF16),
                pltpu.VMEM((chans, rows, beams), F32),
            ],
        ),
        compiler_params=PARAMS,
        cost_estimate=pl.CostEstimate(
            flops=16 * chans * rows * total * beams, bytes_accessed=12 << 20, transcendentals=0
        ),
    )(first, *operands)


def powers(own, far, pick, search, copies):
    chans, rows, beams = own.shape
    width = TIME * search
    table = time_table(search)
    high = jnp.asarray(table).astype(BF16)
    low = (jnp.asarray(table) - high.astype(F32)).astype(BF16)
    block = min(4, chans // PARTS)
    cube = pl.BlockSpec((block, rows, beams), lambda i: (i, 0, 0))
    half = chans // block // PARTS
    far_cubes = [
        pl.BlockSpec((block, rows, beams), lambda i: (jnp.minimum(i, half - 1), 0, 0)),
        pl.BlockSpec((block, rows, beams), lambda i: (jnp.maximum(i - half, 0), 0, 0)),
    ]
    flat = lambda shape: pl.BlockSpec(shape, lambda i: (0,) * len(shape))
    return pl.pallas_call(
        power_kernel,
        out_shape=(
            jax.ShapeDtypeStruct((chans, TIME, beams), F32),
            jax.ShapeDtypeStruct((copies, chans, width), BF16),
        ),
        grid=(chans // block,),
        in_specs=[cube, *far_cubes, flat(pick.shape), flat(high.shape), flat(low.shape)],
        out_specs=(
            pl.BlockSpec((block, TIME, beams), lambda i: (i, 0, 0)),
            flat((copies, chans, width)),
        ),
        scratch_shapes=[pltpu.VMEM((chans, width), F32)],
        compiler_params=PARAMS,
        name="power",
    )(own, *far, pick, high, low)


def on_device(voltages, gains, positions, directions, input_order, delays, search_beams):
    devices = lax.axis_size("crate")
    position = lax.axis_index("crate")
    chans = gains.shape[0]
    halves = 2
    per_half = devices // halves
    half_id = position // per_half
    members = [list(range(h * per_half, (h + 1) * per_half)) for h in range(halves)]
    partners = [(d, (d + per_half) % devices) for d in range(devices)]
    inputs = gains.shape[2] // halves
    own_inputs = half_id * inputs
    half_scalar = half_id.astype(jnp.int32).reshape(1)
    some = chans // PARTS
    table = channel_table(halves, per_half, chans)
    far_block = (1 - half_scalar) * PARTS
    far0, folded = fold(voltages, table, far_block, per_half, some)

    def exchange(x):
        return lax.all_to_all(
            x, "crate", split_axis=0, concat_axis=0, axis_index_groups=members, tiled=True
        )

    far0 = exchange(far0)
    far1 = more_spectra(folded, table, far_block + 1, 1, per_half, some)
    far1, gains, positions = lax.optimization_barrier((far1, gains, positions))
    far_gains = lax.ppermute(
        lax.dynamic_slice_in_dim(gains, inputs - own_inputs, inputs, 2), "crate", partners
    )
    near_gains = lax.dynamic_slice_in_dim(gains, own_inputs, inputs, 2)
    order = lax.dynamic_slice_in_dim(input_order, own_inputs, inputs, 0)
    places = jnp.take(positions.T, order, axis=0)
    search = search_beams.shape[0]
    pick = jnp.tile(search_beams, 128 // search)[None, :]
    own_first = (position * chans).astype(jnp.int32).reshape(1)
    far_first = ((position + per_half) % devices * chans).astype(jnp.int32).reshape(1)
    far0, far1, far_gains, near_gains, places, pick = lax.optimization_barrier(
        (far0, far1, far_gains, near_gains, places, pick)
    )
    far1 = exchange(far1)
    beams = functools.partial(form_beams, places=places, directions=directions)
    sums0, dc, ds, c, s = beams(
        "start", far0, far_gains, 0, far_first, state=[], out_type=BF16
    )
    sums0, folded = lax.optimization_barrier((sums0, folded))
    sums0 = lax.ppermute(sums0, "crate", partners)
    near = more_spectra(folded, table, half_scalar, PARTS, per_half, some)
    far1, near = lax.optimization_barrier((far1, near))
    near = exchange(near)
    (sums1,) = beams(
        "more", far1, far_gains, 1, far_first, state=[dc, ds, c, s], out_type=BF16
    )
    sums1 = lax.ppermute(sums1, "crate", partners)
    (near_sums,) = beams("step", near, near_gains, 0, own_first, state=[dc, ds], out_type=F32)

    beam_power, spectrum = powers(near_sums, [sums0, sums1], pick, search, devices)
    spectrum = lax.all_to_all(spectrum, "crate", split_axis=0, concat_axis=0, tiled=True)
    width = spectrum.shape[-1]
    trials = delays.shape[0] // devices
    own_delays = lax.dynamic_slice_in_dim(delays, position * trials, trials, 0)
    turns = jax.ShapeDtypeStruct((HALF_BINS * trials, 2 * CH), BF16)
    high, low = pl.pallas_call(
        turn_kernel, out_shape=(turns, turns), compiler_params=PARAMS, name="turns"
    )(own_delays)
    dm_plane = pl.pallas_call(
        plane_kernel,
        out_shape=jax.ShapeDtypeStruct((search_beams.shape[0], TIME, trials), F32),
        compiler_params=PARAMS,
        name="plane",
    )(spectrum.reshape(CH, width), high, low)
    return beam_power.transpose(0, 2, 1), dm_plane.transpose(2, 0, 1)


def solution(mesh):
    in_specs = (P(("groups", "crate"), None), P("crate", None, None), P(), P(), P(), P(), P())
    out_specs = (P(("groups", "crate"), None, None), P(("groups", "crate"), None, None))
    return jax.shard_map(
        on_device, mesh=mesh, in_specs=in_specs, out_specs=out_specs, check_vma=False
    )
```

```python
import math

import jax
import jax.numpy as jnp
import numpy as np
from jax import lax
from jax.experimental import pallas as pl
from jax.experimental.pallas import tpu as pltpu
from jax.sharding import PartitionSpec as P

CH = 256
TAPS = 4
TIME = 32
PITCH = 40
FFTLEN = 512
HALF_BINS = TIME // 2
TWO_PI = 2.0 * math.pi
F32 = jnp.float32
BF16 = jnp.bfloat16
NT = (((1,), (1,)), ((), ()))

SIN_POLY = (
    6.283185302511503,
    -41.34170040531769,
    81.60513138580204,
    -76.7030153539128,
    42.02592698618416,
    -14.899846668691637,
    3.238137510515757,
)
COS_POLY = (
    0.9999999890590228,
    -19.739204499454026,
    64.93911745990036,
    -85.45013953095037,
    60.16763093136588,
    -25.96759924965491,
    6.528658162567069,
)


def pfb_window():
    n = np.arange(TAPS * FFTLEN, dtype=np.float64)
    offsets = (n - 0.5 * TAPS * FFTLEN + 0.5) / FFTLEN
    tapering = 0.54 - 0.46 * np.cos(TWO_PI * n / (TAPS * FFTLEN - 1))
    return (np.sinc(offsets) * tapering).reshape(TAPS, FFTLEN).astype(np.float32)


def dft_table():
    angles = TWO_PI * (np.arange(CH)[:, None] * np.arange(FFTLEN)[None, :] % FFTLEN) / FFTLEN
    stacked = np.stack([np.cos(angles), -np.sin(angles)], axis=1) / math.sqrt(FFTLEN)
    return stacked.reshape(2 * CH, FFTLEN).astype(np.float32)


def time_table(search):
    turns = np.arange(TIME)[:, None] * np.arange(1, HALF_BINS + 1)[None, :] % TIME
    angles = TWO_PI * turns / TIME
    table = np.concatenate([np.cos(angles), -np.sin(angles)], axis=1) / math.sqrt(TIME)
    full = np.einsum("tk,qp->tqpk", table, np.eye(search))
    return full.reshape(TIME * search, search * TIME).astype(np.float32)


def polynomial(z, coefficients):
    total = jnp.full_like(z, coefficients[-1])
    for value in coefficients[-2::-1]:
        total = total * z + value
    return total


def cos_sin_turns(turns):
    r = turns - jnp.round(turns)
    z = r * r
    return polynomial(z, COS_POLY), polynomial(z, SIN_POLY) * r


def split_bf16(x):
    high = x.astype(BF16)
    return high, (x - high.astype(F32)).astype(BF16)


def transform_rows(table, folded_ref, spread_ref, out_ref):
    dests, chans, _, inputs = out_ref.shape
    rows = table.shape[0]
    group = 2 if inputs % 128 == 0 else 1

    def step(index, carry):
        start = pl.multiple_of(index * (group * inputs), group * inputs)
        frames = folded_ref[pl.ds(start, group * inputs), :]
        out = lax.dot_general(table, frames, NT, preferred_element_type=F32)
        for part in range(group):
            piece = out[:, part * inputs : (part + 1) * inputs]
            spread_ref[pl.ds(index * group + part, rows, stride=PITCH), :] = piece
        return carry

    lax.fori_loop(0, TIME // group, step, 0, unroll=4)

    def pack(dest, carry):
        for chan in range(chans):
            for part in range(2):
                start = pl.multiple_of(((dest * chans + chan) * 2 + part) * PITCH, 8)
                block = spread_ref[pl.ds(start, TIME), :].astype(BF16)
                out_ref[dest, chan, part * TIME : (part + 1) * TIME] = block
        return carry

    lax.fori_loop(0, dests, pack, 0, unroll=2)


def fold_kernel(half_ref, volt_ref, window_ref, table_ref, out_ref, folded_ref, spread_ref):
    step = pl.program_id(0)
    rows = volt_ref.shape[0]
    inputs = out_ref.shape[-1]
    lanes = 256
    for lane in range(0, FFTLEN, lanes):
        taps = [window_ref[j : j + 1, lane : lane + lanes] for j in range(TAPS)]
        for row in range(0, rows, 16):
            frames = []
            for t in range(TIME + TAPS - 1):
                start = t * FFTLEN + lane
                frames.append(volt_ref[row : row + 16, start : start + lanes].astype(F32))
                if t >= TAPS - 1:
                    first = t - TAPS + 1
                    total = taps[0] * frames[first]
                    for j in range(1, TAPS):
                        total = total + taps[j] * frames[first + j]
                    place = pl.multiple_of(first * inputs + step * rows + row, 16)
                    folded_ref[pl.ds(place, 16), lane : lane + lanes] = total.astype(BF16)

    @pl.when(step == pl.num_programs(0) - 1)
    def _():
        transform_rows(table_ref[...], folded_ref, spread_ref, out_ref)


def spectra_kernel(block_ref, folded_ref, table_ref, out_ref, spread_ref):
    transform_rows(table_ref[...], folded_ref, spread_ref, out_ref)


def phasor_kernel(first_ref, place_ref, dir_ref, dc_ref, ds_ref, *start_refs):
    depth, beams = dc_ref.shape
    wide = 256

    def block(index, carry):
        rows = pl.ds(pl.multiple_of(index * 16, 16), 16)
        place = place_ref[rows, :]
        for lane in range(0, beams, wide):
            lanes = slice(lane, lane + wide)
            direction = dir_ref[:, lanes]
            geometry = place[:, 0:1] * direction[0:1, :]
            geometry = geometry + place[:, 1:2] * direction[1:2, :]
            geometry = geometry + place[:, 2:3] * direction[2:3, :]
            dc_ref[rows, lanes], ds_ref[rows, lanes] = cos_sin_turns(geometry * (1.0 / CH))
            for k in range(len(start_refs) // 2):
                first = 1.0 + first_ref[k].astype(F32) * (1.0 / CH)
                c, s = cos_sin_turns(geometry * first)
                start_refs[2 * k][rows, lanes], start_refs[2 * k + 1][rows, lanes] = c, s
        return carry

    lax.fori_loop(0, depth // 16, block, 0, unroll=2)


def beam_kernel(
    x_ref, gain_ref, dc_ref, ds_ref, c_ref, s_ref, out_ref, even_ref, odd_ref, sum_ref
):
    step = pl.program_id(0)
    tiles = pl.num_programs(0) - 1
    chans, _, beams = out_ref.shape
    depth = dc_ref.shape[0]
    wide = 256
    chunk = depth // chans

    def generate(part, weight_ref):
        for sub in range(0, chunk, 16):
            row = pl.multiple_of(part * chunk + sub, 16)
            rows = pl.ds(row, 16)
            for lane in range(0, beams, wide):
                lanes = slice(lane, lane + wide)
                c, s = c_ref[rows, lanes], s_ref[rows, lanes]
                dc, ds = dc_ref[rows, lanes], ds_ref[rows, lanes]
                next_c, next_s = c * dc - s * ds, c * ds + s * dc
                twice = dc + dc
                for chan in range(chans):
                    weight_ref[chan, rows, lanes] = c.astype(BF16)
                    weight_ref[chan, pl.ds(depth + row, 16), lanes] = s.astype(BF16)
                    if chan + 2 < chans:
                        c, next_c = next_c, twice * next_c - c
                        s, next_s = next_s, twice * next_s - s
                    else:
                        c, s = next_c, next_s

    def accumulate(chan, weight_ref):
        blocks = x_ref.shape[0]
        data = jnp.concatenate([x_ref[k, chan] for k in range(blocks)], axis=1).astype(F32)
        real, imag = data[:TIME], data[TIME:]
        gain = gain_ref[chan]
        x0 = (gain[0:1] * real - gain[1:2] * imag).astype(BF16)
        x1 = (gain[0:1] * imag + gain[1:2] * real).astype(BF16)
        top = jnp.concatenate([x0, x1], axis=1)
        bottom = jnp.concatenate([x1, -x0], axis=1)
        both = jnp.concatenate([top, bottom], axis=0)
        return jnp.dot(both, weight_ref[chan], preferred_element_type=F32)

    def both(m, weights):
        sum_ref[m] += accumulate(m, weights[0])
        generate(m, weights[1])

    def last(m, weights):
        out_ref[m] = (sum_ref[m] + accumulate(m, weights[0])).astype(out_ref.dtype)

    def over_channels(body, weights):
        unroll = min(8, chans)
        lax.fori_loop(0, chans, lambda m, v: (body(m, weights), v)[1], 0, unroll=unroll)

    @pl.when(step == 0)
    def _():
        sum_ref[...] = jnp.zeros_like(sum_ref)
        over_channels(generate, even_ref)

    for parity, weights in ((1, (even_ref, odd_ref)), (0, (odd_ref, even_ref))):

        @pl.when((step > 0) & (step < tiles) & (lax.rem(step, 2) == parity))
        def _(weights=weights):
            over_channels(both, weights)

        @pl.when((step == tiles) & (lax.rem(step, 2) == parity))
        def _(weights=weights):
            over_channels(last, weights)


def power_kernel(
    own_ref, far0_ref, far1_ref, pick_ref, high_ref, low_ref, power_ref, spec_ref, chosen_ref
):
    step = pl.program_id(0)
    block, _, beams = own_ref.shape
    search = chosen_ref.shape[1] // TIME
    per = 128 // search
    far = jnp.concatenate([far0_ref[...], far1_ref[...]], axis=2)
    total = own_ref[...] + far.astype(F32)
    real, imag = total[:, :TIME], total[:, TIME:]
    power = (real * real + imag * imag) * (1.0 / 2048)
    power_ref[...] = power
    rows = power.reshape(block * TIME, beams)
    hit = lax.broadcasted_iota(jnp.int32, (beams, 128), 0) == pick_ref[...]
    hot = jnp.where(hit, 1.0, 0.0).astype(BF16)
    high, low = split_bf16(rows)
    picked = jnp.dot(high, hot, preferred_element_type=F32)
    picked = picked + jnp.dot(low, hot, preferred_element_type=F32)
    row_id = lax.broadcasted_iota(jnp.int32, (per, 128), 0)
    lane_id = lax.broadcasted_iota(jnp.int32, (per, 128), 1) // search
    for chan in range(block):
        pieces = []
        for j in range(TIME // per):
            start = chan * TIME + j * per
            piece = jnp.where(row_id == lane_id, picked[start : start + per], 0.0)
            pieces.append(jnp.sum(piece, axis=0, keepdims=True))
        chosen_ref[pl.ds(step * block + chan, 1), :] = jnp.concatenate(pieces, axis=1)

    @pl.when(step == pl.num_programs(0) - 1)
    def _():
        g_high, g_low = split_bf16(chosen_ref[...])
        spectrum = jnp.dot(g_high, high_ref[...], preferred_element_type=F32)
        spectrum = spectrum + jnp.dot(g_low, high_ref[...], preferred_element_type=F32)
        spectrum = spectrum + jnp.dot(g_high, low_ref[...], preferred_element_type=F32)
        spectrum = spectrum.astype(BF16)
        for dest in range(spec_ref.shape[0]):
            spec_ref[dest] = spectrum


def turn_kernel(delay_ref, high_ref, low_ref):
    trials, chans = delay_ref.shape
    dc, ds = cos_sin_turns(delay_ref[...].astype(F32) * (1.0 / TIME))
    c, s = dc, ds
    for k in range(HALF_BINS):
        rows = slice(k * trials, (k + 1) * trials)
        for value, start in ((c, 0), (s, chans)):
            high, low = split_bf16(value)
            high_ref[rows, start : start + chans] = high
            low_ref[rows, start : start + chans] = low
        c, s = c * dc - s * ds, c * ds + s * dc


def plane_kernel(spec_ref, high_ref, low_ref, out_ref):
    chans, width = spec_ref.shape
    _, _, trials = out_ref.shape
    spec = spec_ref[...].astype(F32)
    lane = lax.broadcasted_iota(jnp.int32, (chans, width), 1)
    is_real = lane % TIME < HALF_BINS
    ahead = pltpu.roll(spec, width - HALF_BINS, 1)
    behind = pltpu.roll(spec, HALF_BINS, 1)
    turned = jnp.where(is_real, -ahead, behind)
    both = jnp.concatenate([spec.astype(BF16), turned.astype(BF16)], axis=0)
    bin_id = lax.broadcasted_iota(jnp.int32, (trials, width), 1) % HALF_BINS
    plane = jnp.zeros((trials, width), F32)
    for k in range(HALF_BINS):
        rows = slice(k * trials, (k + 1) * trials)
        part = jnp.dot(high_ref[rows], both, preferred_element_type=F32)
        part = part + jnp.dot(low_ref[rows], both, preferred_element_type=F32)
        plane = jnp.where(bin_id == k, part, plane)
    out_ref[...] = (plane.T * (1.0 / math.sqrt(CH))).reshape(out_ref.shape)


PARAMS = pltpu.CompilerParams(vmem_limit_bytes=60 << 20)


def fold(voltages, table, block_id, dests, chans):
    inputs, samples = voltages.shape
    rows = 2 * dests * chans
    window = jnp.asarray(pfb_window())
    block = min(32, inputs)
    spectra = jax.ShapeDtypeStruct((dests, chans, 2 * TIME, inputs), BF16)
    folded = jax.ShapeDtypeStruct((TIME * inputs, FFTLEN), BF16)
    whole = lambda x: pl.BlockSpec(x.shape, lambda i, k: (0,) * len(x.shape))
    return pl.pallas_call(
        fold_kernel,
        out_shape=(spectra, folded),
        grid_spec=pltpu.PrefetchScalarGridSpec(
            num_scalar_prefetch=1,
            grid=(inputs // block,),
            in_specs=[
                pl.BlockSpec((block, samples), lambda i, k: (i, 0)),
                whole(window),
                pl.BlockSpec((rows, FFTLEN), lambda i, k: (k[0], 0)),
            ],
            out_specs=(whole(spectra), whole(folded)),
            scratch_shapes=[pltpu.VMEM((rows * PITCH, inputs), F32)],
        ),
        compiler_params=PARAMS,
        cost_estimate=pl.CostEstimate(
            flops=8 * rows * FFTLEN * TIME * inputs, bytes_accessed=12 << 20, transcendentals=0
        ),
        name="fold",
    )(block_id, voltages, window, table)


def more_spectra(folded, table, block_id, dests, chans):
    rows = 2 * dests * chans
    inputs = folded.shape[0] // TIME
    out = jax.ShapeDtypeStruct((dests, chans, 2 * TIME, inputs), BF16)
    return pl.pallas_call(
        spectra_kernel,
        out_shape=out,
        grid_spec=pltpu.PrefetchScalarGridSpec(
            num_scalar_prefetch=1,
            grid=(1,),
            in_specs=[
                pl.BlockSpec(folded.shape, lambda i, k: (0, 0)),
                pl.BlockSpec((rows, FFTLEN), lambda i, k: (k[0], 0)),
            ],
            out_specs=pl.BlockSpec(out.shape, lambda i, k: (0, 0, 0, 0)),
            scratch_shapes=[pltpu.VMEM((rows * PITCH, inputs), F32)],
        ),
        compiler_params=PARAMS,
        cost_estimate=pl.CostEstimate(
            flops=4 * rows * FFTLEN * TIME * inputs, bytes_accessed=6 << 20, transcendentals=0
        ),
        name="spectra",
    )(block_id, folded, table)


def phasors(firsts, places, directions):
    total, beams = places.shape[0], directions.shape[1]
    depth = 128
    count = 2 + 2 * firsts.shape[0]
    return pl.pallas_call(
        phasor_kernel,
        out_shape=[jax.ShapeDtypeStruct((total, beams), F32)] * count,
        grid_spec=pltpu.PrefetchScalarGridSpec(
            num_scalar_prefetch=1,
            grid=(total // depth,),
            in_specs=[
                pl.BlockSpec((depth, 3), lambda i, f: (i, 0)),
                pl.BlockSpec(directions.shape, lambda i, f: (0, 0)),
            ],
            out_specs=[pl.BlockSpec((depth, beams), lambda i, f: (i, 0))] * count,
        ),
        compiler_params=PARAMS,
        cost_estimate=pl.CostEstimate(
            flops=8000 * total * beams, bytes_accessed=count * 4 * total * beams, transcendentals=0
        ),
        name="phasors",
    )(firsts, places, directions)


def form_beams(x, gains, state, start, beams, out_type):
    sources, chans, rows, inputs = x.shape
    total = sources * inputs
    if inputs != 128:
        x = x.transpose(1, 2, 0, 3).reshape(chans, rows, total // 128, 128)
        x = x.transpose(2, 0, 1, 3)
    depth = 256
    blocks = depth // 128
    tiles = total // depth
    late = lambda i: jnp.maximum(i - 1, 0)
    state_spec = pl.BlockSpec((depth, beams), lambda i: (jnp.minimum(i, tiles - 1), start))
    return pl.pallas_call(
        beam_kernel,
        out_shape=jax.ShapeDtypeStruct((chans, rows, beams), out_type),
        grid=(tiles + 1,),
        in_specs=[
            pl.BlockSpec((blocks, chans, rows, 128), lambda i: (late(i), 0, 0, 0)),
            pl.BlockSpec((chans, 2, depth), lambda i: (0, 0, late(i))),
        ]
        + [state_spec] * 4,
        out_specs=pl.BlockSpec((chans, rows, beams), lambda i: (0, 0, 0)),
        scratch_shapes=[
            pltpu.VMEM((chans, 2 * depth, beams), BF16),
            pltpu.VMEM((chans, 2 * depth, beams), BF16),
            pltpu.VMEM((chans, rows, beams), F32),
        ],
        compiler_params=PARAMS,
        cost_estimate=pl.CostEstimate(
            flops=16 * chans * rows * total * beams, bytes_accessed=12 << 20, transcendentals=0
        ),
        name="beams",
    )(x, gains, *state)


def powers(own, far, pick, search, copies):
    chans, rows, beams = own.shape
    width = TIME * search
    table = time_table(search)
    high = jnp.asarray(table).astype(BF16)
    low = (jnp.asarray(table) - high.astype(F32)).astype(BF16)
    block = min(4, chans)
    cube = pl.BlockSpec((block, rows, beams), lambda i: (i, 0, 0))
    far_cubes = [pl.BlockSpec((block, rows, x.shape[2]), lambda i: (i, 0, 0)) for x in far]
    flat = lambda shape: pl.BlockSpec(shape, lambda i: (0,) * len(shape))
    return pl.pallas_call(
        power_kernel,
        out_shape=(
            jax.ShapeDtypeStruct((chans, TIME, beams), F32),
            jax.ShapeDtypeStruct((copies, chans, width), BF16),
        ),
        grid=(chans // block,),
        in_specs=[cube, *far_cubes, flat(pick.shape), flat(high.shape), flat(low.shape)],
        out_specs=(
            pl.BlockSpec((block, TIME, beams), lambda i: (i, 0, 0)),
            flat((copies, chans, width)),
        ),
        scratch_shapes=[pltpu.VMEM((chans, width), F32)],
        compiler_params=PARAMS,
        name="power",
    )(own, *far, pick, high, low)


def on_device(voltages, gains, positions, directions, input_order, delays, search_beams):
    devices = lax.axis_size("crate")
    position = lax.axis_index("crate")
    chans = gains.shape[0]
    halves = 2
    per_half = devices // halves
    half_id = position // per_half
    members = [list(range(h * per_half, (h + 1) * per_half)) for h in range(halves)]
    partners = [(d, (d + per_half) % devices) for d in range(devices)]
    inputs = gains.shape[2] // halves
    own_inputs = half_id * inputs
    half_scalar = half_id.astype(jnp.int32).reshape(1)
    table = jnp.asarray(dft_table()).astype(BF16)
    far, folded = fold(voltages, table, 1 - half_scalar, per_half, chans)

    def exchange(x):
        return lax.all_to_all(
            x, "crate", split_axis=0, concat_axis=0, axis_index_groups=members, tiled=True
        )

    far = exchange(far)
    near = more_spectra(folded, table, half_scalar, per_half, chans)
    near, gains, positions = lax.optimization_barrier((near, gains, positions))
    far_gains = lax.dynamic_slice_in_dim(gains, inputs - own_inputs, inputs, 2)
    far_gains = lax.ppermute(far_gains, "crate", partners)
    near_gains = lax.dynamic_slice_in_dim(gains, own_inputs, inputs, 2)
    order = lax.dynamic_slice_in_dim(input_order, own_inputs, inputs, 0)
    places = jnp.take(positions.T, order, axis=0)
    search = search_beams.shape[0]
    pick = jnp.tile(search_beams, 128 // search)[None, :]
    firsts = jnp.stack([(position + per_half) % devices, position]) * chans
    dc, ds, far_c, far_s, near_c, near_s = phasors(
        firsts.astype(jnp.int32), places, directions
    )
    near, near_gains, pick, dc, ds, far_c, far_s = lax.optimization_barrier(
        (near, near_gains, pick, dc, ds, far_c, far_s)
    )
    near = exchange(near)

    beams = directions.shape[1]
    cut = beams // 2
    far_sums = []
    for part in range(2):
        sums = form_beams(far, far_gains, (dc, ds, far_c, far_s), part, cut, BF16)
        far_sums.append(lax.ppermute(sums, "crate", partners))
    near_sums = form_beams(near, near_gains, (dc, ds, near_c, near_s), 0, beams, F32)

    beam_power, spectrum = powers(near_sums, far_sums, pick, search, devices)
    spectrum = lax.all_to_all(spectrum, "crate", split_axis=0, concat_axis=0, tiled=True)
    width = spectrum.shape[-1]
    trials = delays.shape[0] // devices
    own_delays = lax.dynamic_slice_in_dim(delays, position * trials, trials, 0)
    turns = jax.ShapeDtypeStruct((HALF_BINS * trials, 2 * CH), BF16)
    high, low = pl.pallas_call(
        turn_kernel, out_shape=(turns, turns), compiler_params=PARAMS, name="turns"
    )(own_delays)
    dm_plane = pl.pallas_call(
        plane_kernel,
        out_shape=jax.ShapeDtypeStruct((search_beams.shape[0], TIME, trials), F32),
        compiler_params=PARAMS,
        name="plane",
    )(spectrum.reshape(CH, width), high, low)
    return beam_power.transpose(0, 2, 1), dm_plane.transpose(2, 0, 1)


def solution(mesh):
    in_specs = (P(("groups", "crate"), None), P("crate", None, None), P(), P(), P(), P(), P())
    out_specs = (P(("groups", "crate"), None, None), P(("groups", "crate"), None, None))
    return jax.shard_map(
        on_device, mesh=mesh, in_specs=in_specs, out_specs=out_specs, check_vma=False
    )
```

```python
import functools
import math

import jax
import jax.numpy as jnp
import numpy as np
from jax import lax
from jax.experimental import pallas as pl
from jax.experimental.pallas import tpu as pltpu
from jax.sharding import PartitionSpec as P

CH = 256
TAPS = 4
TIME = 32
PITCH = 40
FFTLEN = 512
HALF_BINS = TIME // 2
TWO_PI = 2.0 * math.pi
F32 = jnp.float32
BF16 = jnp.bfloat16
NT = (((1,), (1,)), ((), ()))

SIN_POLY = (
    6.283185302511503,
    -41.34170040531769,
    81.60513138580204,
    -76.7030153539128,
    42.02592698618416,
    -14.899846668691637,
    3.238137510515757,
)
COS_POLY = (
    0.9999999890590228,
    -19.739204499454026,
    64.93911745990036,
    -85.45013953095037,
    60.16763093136588,
    -25.96759924965491,
    6.528658162567069,
)


def pfb_window():
    n = np.arange(TAPS * FFTLEN, dtype=np.float64)
    offsets = (n - 0.5 * TAPS * FFTLEN + 0.5) / FFTLEN
    tapering = 0.54 - 0.46 * np.cos(TWO_PI * n / (TAPS * FFTLEN - 1))
    return (np.sinc(offsets) * tapering).reshape(TAPS, FFTLEN).astype(np.float32)


def dft_table():
    angles = TWO_PI * (np.arange(CH)[:, None] * np.arange(FFTLEN)[None, :] % FFTLEN) / FFTLEN
    stacked = np.stack([np.cos(angles), -np.sin(angles)], axis=1) / math.sqrt(FFTLEN)
    return stacked.reshape(2 * CH, FFTLEN).astype(np.float32)


def time_table(search):
    turns = np.arange(TIME)[:, None] * np.arange(1, HALF_BINS + 1)[None, :] % TIME
    angles = TWO_PI * turns / TIME
    table = np.concatenate([np.cos(angles), -np.sin(angles)], axis=1) / math.sqrt(TIME)
    full = np.einsum("tk,qp->tqpk", table, np.eye(search))
    return full.reshape(TIME * search, search * TIME).astype(np.float32)


def polynomial(z, coefficients):
    total = jnp.full_like(z, coefficients[-1])
    for value in coefficients[-2::-1]:
        total = total * z + value
    return total


def cos_sin_turns(turns):
    r = turns - jnp.round(turns)
    z = r * r
    return polynomial(z, COS_POLY), polynomial(z, SIN_POLY) * r


def split_bf16(x):
    high = x.astype(BF16)
    return high, (x - high.astype(F32)).astype(BF16)


def transform_rows(table, folded_ref, spread_ref, out_ref):
    dests, chans, _, inputs = out_ref.shape
    rows = table.shape[0]
    group = 2 if inputs % 128 == 0 else 1

    def step(index, carry):
        start = pl.multiple_of(index * (group * inputs), group * inputs)
        frames = folded_ref[pl.ds(start, group * inputs), :]
        out = lax.dot_general(table, frames, NT, preferred_element_type=F32)
        for part in range(group):
            piece = out[:, part * inputs : (part + 1) * inputs]
            spread_ref[pl.ds(index * group + part, rows, stride=PITCH), :] = piece
        return carry

    lax.fori_loop(0, TIME // group, step, 0, unroll=4)

    def pack(dest, carry):
        for chan in range(chans):
            for part in range(2):
                start = pl.multiple_of(((dest * chans + chan) * 2 + part) * PITCH, 8)
                block = spread_ref[pl.ds(start, TIME), :].astype(BF16)
                out_ref[dest, chan, part * TIME : (part + 1) * TIME] = block
        return carry

    lax.fori_loop(0, dests, pack, 0, unroll=2)


def fold_kernel(half_ref, volt_ref, window_ref, table_ref, out_ref, folded_ref, spread_ref):
    step = pl.program_id(0)
    rows = volt_ref.shape[0]
    inputs = out_ref.shape[-1]
    lanes = 256
    for lane in range(0, FFTLEN, lanes):
        taps = [window_ref[j : j + 1, lane : lane + lanes] for j in range(TAPS)]
        for row in range(0, rows, 16):
            frames = []
            for t in range(TIME + TAPS - 1):
                start = t * FFTLEN + lane
                frames.append(volt_ref[row : row + 16, start : start + lanes].astype(F32))
                if t >= TAPS - 1:
                    first = t - TAPS + 1
                    total = taps[0] * frames[first]
                    for j in range(1, TAPS):
                        total = total + taps[j] * frames[first + j]
                    place = pl.multiple_of(first * inputs + step * rows + row, 16)
                    folded_ref[pl.ds(place, 16), lane : lane + lanes] = total.astype(BF16)

    @pl.when(step == pl.num_programs(0) - 1)
    def _():
        transform_rows(table_ref[...], folded_ref, spread_ref, out_ref)


def spectra_kernel(block_ref, folded_ref, table_ref, out_ref, spread_ref):
    transform_rows(table_ref[...], folded_ref, spread_ref, out_ref)


def phasor_kernel(first_ref, place_ref, dir_ref, dc_ref, ds_ref, *start_refs):
    depth, beams = dc_ref.shape
    wide = 256

    def block(index, carry):
        rows = pl.ds(pl.multiple_of(index * 16, 16), 16)
        place = place_ref[rows, :]
        for lane in range(0, beams, wide):
            lanes = slice(lane, lane + wide)
            direction = dir_ref[:, lanes]
            geometry = place[:, 0:1] * direction[0:1, :]
            geometry = geometry + place[:, 1:2] * direction[1:2, :]
            geometry = geometry + place[:, 2:3] * direction[2:3, :]
            dc_ref[rows, lanes], ds_ref[rows, lanes] = cos_sin_turns(geometry * (1.0 / CH))
            for k in range(len(start_refs) // 2):
                first = 1.0 + first_ref[k].astype(F32) * (1.0 / CH)
                c, s = cos_sin_turns(geometry * first)
                start_refs[2 * k][rows, lanes], start_refs[2 * k + 1][rows, lanes] = c, s
        return carry

    lax.fori_loop(0, depth // 16, block, 0, unroll=2)


def beam_kernel(
    x_ref, gain_ref, dc_ref, ds_ref, c_ref, s_ref, out_ref, even_ref, odd_ref, sum_ref
):
    step = pl.program_id(0)
    tiles = pl.num_programs(0) - 1
    chans, _, beams = out_ref.shape
    depth = dc_ref.shape[0]
    wide = 256
    chunk = depth // chans

    def generate(part, weight_ref):
        for sub in range(0, chunk, 16):
            row = pl.multiple_of(part * chunk + sub, 16)
            rows = pl.ds(row, 16)
            for lane in range(0, beams, wide):
                lanes = slice(lane, lane + wide)
                c, s = c_ref[rows, lanes], s_ref[rows, lanes]
                dc, ds = dc_ref[rows, lanes], ds_ref[rows, lanes]
                next_c, next_s = c * dc - s * ds, c * ds + s * dc
                twice = dc + dc
                for chan in range(chans):
                    weight_ref[chan, rows, lanes] = c.astype(BF16)
                    weight_ref[chan, pl.ds(depth + row, 16), lanes] = s.astype(BF16)
                    if chan + 2 < chans:
                        c, next_c = next_c, twice * next_c - c
                        s, next_s = next_s, twice * next_s - s
                    else:
                        c, s = next_c, next_s

    def accumulate(chan, weight_ref):
        blocks = x_ref.shape[0]
        data = jnp.concatenate([x_ref[k, chan] for k in range(blocks)], axis=1).astype(F32)
        real, imag = data[:TIME], data[TIME:]
        gain = gain_ref[chan]
        x0 = (gain[0:1] * real - gain[1:2] * imag).astype(BF16)
        x1 = (gain[0:1] * imag + gain[1:2] * real).astype(BF16)
        top = jnp.concatenate([x0, x1], axis=1)
        bottom = jnp.concatenate([x1, -x0], axis=1)
        both = jnp.concatenate([top, bottom], axis=0)
        return jnp.dot(both, weight_ref[chan], preferred_element_type=F32)

    def both(m, weights):
        sum_ref[m] += accumulate(m, weights[0])
        generate(m, weights[1])

    def last(m, weights):
        out_ref[m] = (sum_ref[m] + accumulate(m, weights[0])).astype(out_ref.dtype)

    def over_channels(body, weights, unroll=min(8, chans)):
        lax.fori_loop(0, chans, lambda m, v: (body(m, weights), v)[1], 0, unroll=unroll)

    @pl.when(step == 0)
    def _():
        sum_ref[...] = jnp.zeros_like(sum_ref)
        over_channels(generate, even_ref, 1)

    for parity, weights in ((1, (even_ref, odd_ref)), (0, (odd_ref, even_ref))):

        @pl.when((step > 0) & (step < tiles) & (lax.rem(step, 2) == parity))
        def _(weights=weights):
            over_channels(both, weights)

        @pl.when((step == tiles) & (lax.rem(step, 2) == parity))
        def _(weights=weights):
            over_channels(last, weights)


def pick_beams(rows, pick_ref, chans, search):
    per = 128 // search
    hit = lax.broadcasted_iota(jnp.int32, (rows.shape[1], 128), 0) == pick_ref[...]
    hot = jnp.where(hit, 1.0, 0.0).astype(BF16)
    if rows.dtype == BF16:
        picked = jnp.dot(rows, hot, preferred_element_type=F32)
    else:
        high, low = split_bf16(rows)
        picked = jnp.dot(high, hot, preferred_element_type=F32)
        picked = picked + jnp.dot(low, hot, preferred_element_type=F32)
    row_id = lax.broadcasted_iota(jnp.int32, (per, 128), 0)
    lane_id = lax.broadcasted_iota(jnp.int32, (per, 128), 1) // search
    chosen = []
    for chan in range(chans):
        pieces = []
        for j in range(TIME // per):
            start = chan * TIME + j * per
            piece = jnp.where(row_id == lane_id, picked[start : start + per], 0.0)
            pieces.append(jnp.sum(piece, axis=0, keepdims=True))
        chosen.append(jnp.concatenate(pieces, axis=1))
    return chosen


def far_pick_kernel(sum0_ref, sum1_ref, pick_ref, out_ref, picked_ref):
    step = pl.program_id(0)
    block = sum0_ref.shape[0]
    search = out_ref.shape[1] // TIME
    both = jnp.concatenate([sum0_ref[...], sum1_ref[...]], axis=2)
    rows = both.reshape(block * 2 * TIME, both.shape[2])
    half = picked_ref.shape[0] // 2
    for k, row in enumerate(pick_beams(rows, pick_ref, 2 * block, search)):
        place = (k % 2) * half + step * block + k // 2
        picked_ref[pl.ds(place, 1), :] = row

    @pl.when(step == pl.num_programs(0) - 1)
    def _():
        out_ref[...] = picked_ref[...].astype(BF16)


def spectrum_kernel(
    own_ref, far_ref, pick_ref, high_ref, low_ref, spec_ref, picked_ref, norm
):
    step = pl.program_id(0)
    block = own_ref.shape[0]
    copies, chans, width = spec_ref.shape
    search = width // TIME
    rows = own_ref[...].reshape(block * 2 * TIME, own_ref.shape[2])
    for k, row in enumerate(pick_beams(rows, pick_ref, 2 * block, search)):
        place = (k % 2) * chans + step * block + k // 2
        picked_ref[pl.ds(place, 1), :] = row

    @pl.when(step == pl.num_programs(0) - 1)
    def _():
        real = picked_ref[:chans] + far_ref[:chans].astype(F32)
        imag = picked_ref[chans:] + far_ref[chans:].astype(F32)
        g_high, g_low = split_bf16((real * real + imag * imag) * norm)
        spectrum = jnp.dot(g_high, high_ref[...], preferred_element_type=F32)
        spectrum = spectrum + jnp.dot(g_low, high_ref[...], preferred_element_type=F32)
        spectrum = spectrum + jnp.dot(g_high, low_ref[...], preferred_element_type=F32)
        spectrum = spectrum.astype(BF16)
        for dest in range(copies):
            spec_ref[dest] = spectrum


def power_kernel(own_ref, far0_ref, far1_ref, power_ref, norm):
    far = jnp.concatenate([far0_ref[...], far1_ref[...]], axis=2)
    total = own_ref[...] + far.astype(F32)
    real, imag = total[:, :TIME], total[:, TIME:]
    power_ref[...] = (real * real + imag * imag) * norm


def turn_kernel(delay_ref, turn_ref):
    trials, chans = delay_ref.shape
    dc, ds = cos_sin_turns(delay_ref[...].astype(F32) * (1.0 / TIME))
    c, s = dc, ds
    for k in range(HALF_BINS):
        rows = slice(k * trials, (k + 1) * trials)
        turn_ref[rows, :chans] = c.astype(BF16)
        turn_ref[rows, chans:] = s.astype(BF16)
        c, s = c * dc - s * ds, c * ds + s * dc


def plane_kernel(spec_ref, turn_ref, out_ref, both_ref, part_ref):
    chans, width = spec_ref.shape
    _, _, trials = out_ref.shape
    spec = spec_ref[...]
    values = spec.astype(F32)
    lane = lax.broadcasted_iota(jnp.int32, (chans, width), 1)
    ahead = pltpu.roll(values, width - HALF_BINS, 1)
    behind = pltpu.roll(values, HALF_BINS, 1)
    turned = jnp.where(lane % TIME < HALF_BINS, -ahead, behind)
    both_ref[:chans] = spec
    both_ref[chans:] = turned.astype(BF16)
    bin_id = lax.broadcasted_iota(jnp.int32, (trials, width), 1) % HALF_BINS
    plane = jnp.zeros((trials, width), F32)
    group = HALF_BINS // 2
    for first in range(0, HALF_BINS, group):
        rows = slice(first * trials, (first + group) * trials)
        part_ref[...] = jnp.dot(turn_ref[rows], both_ref[...], preferred_element_type=F32)
        for k in range(group):
            part = part_ref[k * trials : (k + 1) * trials]
            plane = jnp.where(bin_id == first + k, part, plane)
    out_ref[...] = (plane.T * (1.0 / math.sqrt(CH))).reshape(out_ref.shape)


PARAMS = pltpu.CompilerParams(vmem_limit_bytes=60 << 20)


def fold(voltages, table, block_id, dests, chans):
    inputs, samples = voltages.shape
    rows = 2 * dests * chans
    window = jnp.asarray(pfb_window())
    block = min(32, inputs)
    spectra = jax.ShapeDtypeStruct((dests, chans, 2 * TIME, inputs), BF16)
    folded = jax.ShapeDtypeStruct((TIME * inputs, FFTLEN), BF16)
    whole = lambda x: pl.BlockSpec(x.shape, lambda i, k: (0,) * len(x.shape))
    return pl.pallas_call(
        fold_kernel,
        out_shape=(spectra, folded),
        grid_spec=pltpu.PrefetchScalarGridSpec(
            num_scalar_prefetch=1,
            grid=(inputs // block,),
            in_specs=[
                pl.BlockSpec((block, samples), lambda i, k: (i, 0)),
                whole(window),
                pl.BlockSpec((rows, FFTLEN), lambda i, k: (k[0], 0)),
            ],
            out_specs=(whole(spectra), whole(folded)),
            scratch_shapes=[pltpu.VMEM((rows * PITCH, inputs), F32)],
        ),
        compiler_params=PARAMS,
        cost_estimate=pl.CostEstimate(
            flops=8 * rows * FFTLEN * TIME * inputs, bytes_accessed=12 << 20, transcendentals=0
        ),
        name="fold",
    )(block_id, voltages, window, table)


def more_spectra(folded, table, block_id, dests, chans):
    rows = 2 * dests * chans
    inputs = folded.shape[0] // TIME
    out = jax.ShapeDtypeStruct((dests, chans, 2 * TIME, inputs), BF16)
    return pl.pallas_call(
        spectra_kernel,
        out_shape=out,
        grid_spec=pltpu.PrefetchScalarGridSpec(
            num_scalar_prefetch=1,
            grid=(1,),
            in_specs=[
                pl.BlockSpec(folded.shape, lambda i, k: (0, 0)),
                pl.BlockSpec((rows, FFTLEN), lambda i, k: (k[0], 0)),
            ],
            out_specs=pl.BlockSpec(out.shape, lambda i, k: (0, 0, 0, 0)),
            scratch_shapes=[pltpu.VMEM((rows * PITCH, inputs), F32)],
        ),
        compiler_params=PARAMS,
        cost_estimate=pl.CostEstimate(
            flops=4 * rows * FFTLEN * TIME * inputs, bytes_accessed=6 << 20, transcendentals=0
        ),
        name="spectra",
    )(block_id, folded, table)


def phasors(firsts, places, directions):
    total, beams = places.shape[0], directions.shape[1]
    depth = 128
    count = 2 + 2 * firsts.shape[0]
    return pl.pallas_call(
        phasor_kernel,
        out_shape=[jax.ShapeDtypeStruct((total, beams), F32)] * count,
        grid_spec=pltpu.PrefetchScalarGridSpec(
            num_scalar_prefetch=1,
            grid=(total // depth,),
            in_specs=[
                pl.BlockSpec((depth, 3), lambda i, f: (i, 0)),
                pl.BlockSpec(directions.shape, lambda i, f: (0, 0)),
            ],
            out_specs=[pl.BlockSpec((depth, beams), lambda i, f: (i, 0))] * count,
        ),
        compiler_params=PARAMS,
        cost_estimate=pl.CostEstimate(
            flops=8000 * total * beams, bytes_accessed=count * 4 * total * beams, transcendentals=0
        ),
        name="phasors",
    )(firsts, places, directions)


def form_beams(x, gains, state, start, beams, out_type):
    sources, chans, rows, inputs = x.shape
    total = sources * inputs
    if inputs != 128:
        x = x.transpose(1, 2, 0, 3).reshape(chans, rows, total // 128, 128)
        x = x.transpose(2, 0, 1, 3)
    depth = 256
    blocks = depth // 128
    tiles = total // depth
    late = lambda i: jnp.maximum(i - 1, 0)
    state_spec = pl.BlockSpec((depth, beams), lambda i: (jnp.minimum(i, tiles - 1), start))
    return pl.pallas_call(
        beam_kernel,
        out_shape=jax.ShapeDtypeStruct((chans, rows, beams), out_type),
        grid=(tiles + 1,),
        in_specs=[
            pl.BlockSpec((blocks, chans, rows, 128), lambda i: (late(i), 0, 0, 0)),
            pl.BlockSpec((chans, 2, depth), lambda i: (0, 0, late(i))),
        ]
        + [state_spec] * 4,
        out_specs=pl.BlockSpec((chans, rows, beams), lambda i: (0, 0, 0)),
        scratch_shapes=[
            pltpu.VMEM((chans, 2 * depth, beams), BF16),
            pltpu.VMEM((chans, 2 * depth, beams), BF16),
            pltpu.VMEM((chans, rows, beams), F32),
        ],
        compiler_params=PARAMS,
        cost_estimate=pl.CostEstimate(
            flops=16 * chans * rows * total * beams, bytes_accessed=12 << 20, transcendentals=0
        ),
        name="beams",
    )(x, gains, *state)


def flat(shape):
    return pl.BlockSpec(shape, lambda i: (0,) * len(shape))


def cubes(block, *arrays):
    return [pl.BlockSpec((block, *x.shape[1:]), lambda i: (i, 0, 0)) for x in arrays]


def pick_far(sums, pick, search):
    chans = sums[0].shape[0]
    block = min(4, chans)
    out = jax.ShapeDtypeStruct((2 * chans, TIME * search), BF16)
    return pl.pallas_call(
        far_pick_kernel,
        out_shape=out,
        grid=(chans // block,),
        in_specs=cubes(block, *sums) + [flat(pick.shape)],
        out_specs=flat(out.shape),
        scratch_shapes=[pltpu.VMEM(out.shape, F32)],
        compiler_params=PARAMS,
        cost_estimate=pl.CostEstimate(
            flops=1 << 30, bytes_accessed=2 << 20, transcendentals=0
        ),
        name="pick",
    )(*sums, pick)


def search_spectra(own, far, pick, search, copies, norm):
    chans = own.shape[0]
    width = TIME * search
    table = time_table(search)
    high = jnp.asarray(table).astype(BF16)
    low = (jnp.asarray(table) - high.astype(F32)).astype(BF16)
    block = min(4, chans)
    out = jax.ShapeDtypeStruct((copies, chans, width), BF16)
    return pl.pallas_call(
        functools.partial(spectrum_kernel, norm=norm),
        out_shape=out,
        grid=(chans // block,),
        in_specs=cubes(block, own) + [flat(x.shape) for x in (far, pick, high, low)],
        out_specs=flat(out.shape),
        scratch_shapes=[pltpu.VMEM((2 * chans, width), F32)],
        compiler_params=PARAMS,
        cost_estimate=pl.CostEstimate(
            flops=2 << 30, bytes_accessed=4 << 20, transcendentals=0
        ),
        name="spectrum",
    )(own, far, pick, high, low)


def powers(own, far, norm):
    chans, _, beams = own.shape
    block = min(4, chans)
    out = jax.ShapeDtypeStruct((chans, TIME, beams), F32)
    return pl.pallas_call(
        functools.partial(power_kernel, norm=norm),
        out_shape=out,
        grid=(chans // block,),
        in_specs=cubes(block, own, *far),
        out_specs=cubes(block, out)[0],
        compiler_params=PARAMS,
        cost_estimate=pl.CostEstimate(
            flops=1 << 28, bytes_accessed=5 << 20, transcendentals=0
        ),
        name="power",
    )(own, *far)


def on_device(voltages, gains, positions, directions, input_order, delays, search_beams):
    devices = lax.axis_size("crate")
    position = lax.axis_index("crate")
    chans = gains.shape[0]
    halves = 2
    per_half = devices // halves
    half_id = position // per_half
    members = [list(range(h * per_half, (h + 1) * per_half)) for h in range(halves)]
    partners = [(d, (d + per_half) % devices) for d in range(devices)]
    inputs = gains.shape[2] // halves
    own_inputs = half_id * inputs
    half_scalar = half_id.astype(jnp.int32).reshape(1)
    table = jnp.asarray(dft_table()).astype(BF16)
    far, folded = fold(voltages, table, 1 - half_scalar, per_half, chans)

    def exchange(x):
        return lax.all_to_all(
            x, "crate", split_axis=0, concat_axis=0, axis_index_groups=members, tiled=True
        )

    far = exchange(far)
    near = more_spectra(folded, table, half_scalar, per_half, chans)
    near, gains, positions = lax.optimization_barrier((near, gains, positions))
    far_gains = lax.dynamic_slice_in_dim(gains, inputs - own_inputs, inputs, 2)
    far_gains = lax.ppermute(far_gains, "crate", partners)
    near_gains = lax.dynamic_slice_in_dim(gains, own_inputs, inputs, 2)
    order = lax.dynamic_slice_in_dim(input_order, own_inputs, inputs, 0)
    places = jnp.take(positions.T, order, axis=0)
    search = search_beams.shape[0]
    pick = jnp.tile(search_beams, 128 // search)[None, :]
    firsts = jnp.stack([(position + per_half) % devices, position]) * chans
    dc, ds, far_c, far_s, near_c, near_s = phasors(
        firsts.astype(jnp.int32), places, directions
    )
    near, near_gains, pick, dc, ds, far_c, far_s = lax.optimization_barrier(
        (near, near_gains, pick, dc, ds, far_c, far_s)
    )
    near = exchange(near)

    beams = directions.shape[1]
    cut = beams // 2
    norm = 1.0 / gains.shape[2]
    far_state = (dc, ds, far_c, far_s)
    sums0 = form_beams(far, far_gains, far_state, 0, cut, BF16)
    far0 = lax.ppermute(sums0, "crate", partners)
    sums1 = form_beams(far, far_gains, far_state, 1, cut, BF16)
    picked = pick_far((sums0, sums1), pick, search)
    picked = lax.ppermute(picked, "crate", partners)
    far1 = lax.ppermute(sums1, "crate", partners)
    near_sums = form_beams(near, near_gains, (dc, ds, near_c, near_s), 0, beams, F32)
    spectrum = search_spectra(near_sums, picked, pick, search, devices, norm)
    near_sums, spectrum = lax.optimization_barrier((near_sums, spectrum))
    spectrum = lax.all_to_all(spectrum, "crate", split_axis=0, concat_axis=0, tiled=True)
    beam_power = powers(near_sums, (far0, far1), norm)
    width = spectrum.shape[-1]
    trials = delays.shape[0] // devices
    own_delays = lax.dynamic_slice_in_dim(delays, position * trials, trials, 0)
    turns = pl.pallas_call(
        turn_kernel,
        out_shape=jax.ShapeDtypeStruct((HALF_BINS * trials, 2 * CH), BF16),
        compiler_params=PARAMS,
        name="turns",
    )(own_delays)
    dm_plane = pl.pallas_call(
        plane_kernel,
        out_shape=jax.ShapeDtypeStruct((search, TIME, trials), F32),
        scratch_shapes=[
            pltpu.VMEM((2 * CH, width), BF16),
            pltpu.VMEM((HALF_BINS // 2 * trials, width), F32),
        ],
        compiler_params=PARAMS,
        name="plane",
    )(spectrum.reshape(CH, width), turns)
    return beam_power.transpose(0, 2, 1), dm_plane.transpose(2, 0, 1)


def solution(mesh):
    in_specs = (P(("groups", "crate"), None), P("crate", None, None), P(), P(), P(), P(), P())
    out_specs = (P(("groups", "crate"), None, None), P(("groups", "crate"), None, None))
    return jax.shard_map(
        on_device, mesh=mesh, in_specs=in_specs, out_specs=out_specs, check_vma=False
    )
```

```python
import functools
import math

import jax
import jax.numpy as jnp
import numpy as np
from jax import lax
from jax.experimental import pallas as pl
from jax.experimental.pallas import tpu as pltpu
from jax.sharding import PartitionSpec as P

CH = 256
TAPS = 4
TIME = 32
PITCH = 40
FFTLEN = 512
HALF_BINS = TIME // 2
TWO_PI = 2.0 * math.pi
F32 = jnp.float32
BF16 = jnp.bfloat16
NT = (((1,), (1,)), ((), ()))

SIN_POLY = (
    6.283185302511503,
    -41.34170040531769,
    81.60513138580204,
    -76.7030153539128,
    42.02592698618416,
    -14.899846668691637,
    3.238137510515757,
)
COS_POLY = (
    0.9999999890590228,
    -19.739204499454026,
    64.93911745990036,
    -85.45013953095037,
    60.16763093136588,
    -25.96759924965491,
    6.528658162567069,
)


def pfb_window():
    n = np.arange(TAPS * FFTLEN, dtype=np.float64)
    offsets = (n - 0.5 * TAPS * FFTLEN + 0.5) / FFTLEN
    tapering = 0.54 - 0.46 * np.cos(TWO_PI * n / (TAPS * FFTLEN - 1))
    return (np.sinc(offsets) * tapering).reshape(TAPS, FFTLEN).astype(np.float32)


def dft_table():
    angles = TWO_PI * (np.arange(CH)[:, None] * np.arange(FFTLEN)[None, :] % FFTLEN) / FFTLEN
    stacked = np.stack([np.cos(angles), -np.sin(angles)], axis=1) / math.sqrt(FFTLEN)
    return stacked.reshape(2 * CH, FFTLEN).astype(np.float32)


def time_table(search):
    turns = np.arange(TIME)[:, None] * np.arange(1, HALF_BINS + 1)[None, :] % TIME
    angles = TWO_PI * turns / TIME
    table = np.concatenate([np.cos(angles), -np.sin(angles)], axis=1) / math.sqrt(TIME)
    full = np.einsum("tk,qp->tqpk", table, np.eye(search))
    return full.reshape(TIME * search, search * TIME).astype(np.float32)


def polynomial(z, coefficients):
    total = jnp.full_like(z, coefficients[-1])
    for value in coefficients[-2::-1]:
        total = total * z + value
    return total


def cos_sin_turns(turns):
    r = turns - jnp.round(turns)
    z = r * r
    return polynomial(z, COS_POLY), polynomial(z, SIN_POLY) * r


def split_bf16(x):
    high = x.astype(BF16)
    return high, (x - high.astype(F32)).astype(BF16)


def transform_rows(table, folded_ref, spread_ref, out_ref):
    dests, chans, _, inputs = out_ref.shape
    rows = table.shape[0]
    group = 2 if inputs % 128 == 0 else 1

    def step(index, carry):
        start = pl.multiple_of(index * (group * inputs), group * inputs)
        frames = folded_ref[pl.ds(start, group * inputs), :]
        out = lax.dot_general(table, frames, NT, preferred_element_type=F32)
        for part in range(group):
            piece = out[:, part * inputs : (part + 1) * inputs]
            spread_ref[pl.ds(index * group + part, rows, stride=PITCH), :] = piece
        return carry

    lax.fori_loop(0, TIME // group, step, 0, unroll=4)

    def pack(dest, carry):
        for chan in range(chans):
            for part in range(2):
                start = pl.multiple_of(((dest * chans + chan) * 2 + part) * PITCH, 8)
                block = spread_ref[pl.ds(start, TIME), :].astype(BF16)
                out_ref[dest, chan, part * TIME : (part + 1) * TIME] = block
        return carry

    lax.fori_loop(0, dests, pack, 0, unroll=2)


def fold_kernel(half_ref, volt_ref, window_ref, table_ref, out_ref, folded_ref, spread_ref):
    step = pl.program_id(0)
    rows = volt_ref.shape[0]
    inputs = out_ref.shape[-1]
    lanes = 256
    for lane in range(0, FFTLEN, lanes):
        taps = [window_ref[j : j + 1, lane : lane + lanes] for j in range(TAPS)]
        for row in range(0, rows, 16):
            frames = []
            for t in range(TIME + TAPS - 1):
                start = t * FFTLEN + lane
                frames.append(volt_ref[row : row + 16, start : start + lanes].astype(F32))
                if t >= TAPS - 1:
                    first = t - TAPS + 1
                    total = taps[0] * frames[first]
                    for j in range(1, TAPS):
                        total = total + taps[j] * frames[first + j]
                    place = pl.multiple_of(first * inputs + step * rows + row, 16)
                    folded_ref[pl.ds(place, 16), lane : lane + lanes] = total.astype(BF16)

    @pl.when(step == pl.num_programs(0) - 1)
    def _():
        transform_rows(table_ref[...], folded_ref, spread_ref, out_ref)


def spectra_kernel(block_ref, folded_ref, table_ref, out_ref, spread_ref):
    transform_rows(table_ref[...], folded_ref, spread_ref, out_ref)


def phasor_kernel(first_ref, place_ref, dir_ref, *out_refs):
    depth, beams = out_refs[0].shape
    wide = 256

    def block(index, carry):
        rows = pl.ds(pl.multiple_of(index * 16, 16), 16)
        place = place_ref[rows, :]
        for lane in range(0, beams, wide):
            lanes = slice(lane, lane + wide)
            direction = dir_ref[:, lanes]
            geometry = place[:, 0:1] * direction[0:1, :]
            geometry = geometry + place[:, 1:2] * direction[1:2, :]
            geometry = geometry + place[:, 2:3] * direction[2:3, :]
            first = 1.0 + first_ref[0].astype(F32) * (1.0 / CH)
            for k, scale in enumerate((first, 1.0 / CH)[: len(out_refs) // 2]):
                c, s = cos_sin_turns(geometry * scale)
                out_refs[2 * k][rows, lanes], out_refs[2 * k + 1][rows, lanes] = c, s
        return carry

    lax.fori_loop(0, depth // 16, block, 0, unroll=2)


def beam_kernel(
    x_ref, gain_ref, dc_ref, ds_ref, c_ref, s_ref, out_ref, even_ref, odd_ref, sum_ref
):
    step = pl.program_id(0)
    tiles = pl.num_programs(0) - 1
    chans, _, beams = out_ref.shape
    depth = dc_ref.shape[0]
    wide = 256
    chunk = depth // chans

    def generate(part, weight_ref):
        for sub in range(0, chunk, 16):
            row = pl.multiple_of(part * chunk + sub, 16)
            rows = pl.ds(row, 16)
            for lane in range(0, beams, wide):
                lanes = slice(lane, lane + wide)
                c, s = c_ref[rows, lanes], s_ref[rows, lanes]
                dc, ds = dc_ref[rows, lanes], ds_ref[rows, lanes]
                next_c, next_s = c * dc - s * ds, c * ds + s * dc
                twice = dc + dc
                for chan in range(chans):
                    weight_ref[chan, rows, lanes] = c.astype(BF16)
                    weight_ref[chan, pl.ds(depth + row, 16), lanes] = s.astype(BF16)
                    if chan + 2 < chans:
                        c, next_c = next_c, twice * next_c - c
                        s, next_s = next_s, twice * next_s - s
                    else:
                        c, s = next_c, next_s

    def accumulate(chan, weight_ref):
        blocks = x_ref.shape[0]
        data = jnp.concatenate([x_ref[k, chan] for k in range(blocks)], axis=1).astype(F32)
        real, imag = data[:TIME], data[TIME:]
        gain = gain_ref[chan]
        x0 = (gain[0:1] * real - gain[1:2] * imag).astype(BF16)
        x1 = (gain[0:1] * imag + gain[1:2] * real).astype(BF16)
        top = jnp.concatenate([x0, x1], axis=1)
        bottom = jnp.concatenate([x1, -x0], axis=1)
        both = jnp.concatenate([top, bottom], axis=0)
        return jnp.dot(both, weight_ref[chan], preferred_element_type=F32)

    def both(m, weights):
        sum_ref[m] += accumulate(m, weights[0])
        generate(m, weights[1])

    def last(m, weights):
        out_ref[m] = (sum_ref[m] + accumulate(m, weights[0])).astype(out_ref.dtype)

    def over_channels(body, weights, unroll=min(8, chans)):
        lax.fori_loop(0, chans, lambda m, v: (body(m, weights), v)[1], 0, unroll=unroll)

    @pl.when(step == 0)
    def _():
        sum_ref[...] = jnp.zeros_like(sum_ref)
        over_channels(generate, even_ref, 1)

    for parity, weights in ((1, (even_ref, odd_ref)), (0, (odd_ref, even_ref))):

        @pl.when((step > 0) & (step < tiles) & (lax.rem(step, 2) == parity))
        def _(weights=weights):
            over_channels(both, weights)

        @pl.when((step == tiles) & (lax.rem(step, 2) == parity))
        def _(weights=weights):
            over_channels(last, weights)


def pick_beams(rows, pick_ref, chans, search):
    per = 128 // search
    hit = lax.broadcasted_iota(jnp.int32, (rows.shape[1], 128), 0) == pick_ref[...]
    hot = jnp.where(hit, 1.0, 0.0).astype(BF16)
    if rows.dtype == BF16:
        picked = jnp.dot(rows, hot, preferred_element_type=F32)
    else:
        high, low = split_bf16(rows)
        picked = jnp.dot(high, hot, preferred_element_type=F32)
        picked = picked + jnp.dot(low, hot, preferred_element_type=F32)
    row_id = lax.broadcasted_iota(jnp.int32, (per, 128), 0)
    lane_id = lax.broadcasted_iota(jnp.int32, (per, 128), 1) // search
    chosen = []
    for chan in range(chans):
        pieces = []
        for j in range(TIME // per):
            start = chan * TIME + j * per
            piece = jnp.where(row_id == lane_id, picked[start : start + per], 0.0)
            pieces.append(jnp.sum(piece, axis=0, keepdims=True))
        chosen.append(jnp.concatenate(pieces, axis=1))
    return chosen


def far_pick_kernel(sum_ref, pick_ref, out_ref, picked_ref):
    step = pl.program_id(0)
    block = sum_ref.shape[0]
    search = out_ref.shape[1] // TIME
    rows = sum_ref[...].reshape(block * 2 * TIME, sum_ref.shape[2])
    half = picked_ref.shape[0] // 2
    for k, row in enumerate(pick_beams(rows, pick_ref, 2 * block, search)):
        place = (k % 2) * half + step * block + k // 2
        picked_ref[pl.ds(place, 1), :] = row

    @pl.when(step == pl.num_programs(0) - 1)
    def _():
        out_ref[...] = picked_ref[...].astype(BF16)


def spectrum_kernel(
    own_ref, far_ref, pick_ref, high_ref, low_ref, spec_ref, picked_ref, norm
):
    step = pl.program_id(0)
    block = own_ref.shape[0]
    copies, chans, width = spec_ref.shape
    search = width // TIME
    rows = own_ref[...].reshape(block * 2 * TIME, own_ref.shape[2])
    for k, row in enumerate(pick_beams(rows, pick_ref, 2 * block, search)):
        place = (k % 2) * chans + step * block + k // 2
        picked_ref[pl.ds(place, 1), :] = row

    @pl.when(step == pl.num_programs(0) - 1)
    def _():
        real = picked_ref[:chans] + far_ref[:chans].astype(F32)
        imag = picked_ref[chans:] + far_ref[chans:].astype(F32)
        g_high, g_low = split_bf16((real * real + imag * imag) * norm)
        spectrum = jnp.dot(g_high, high_ref[...], preferred_element_type=F32)
        spectrum = spectrum + jnp.dot(g_low, high_ref[...], preferred_element_type=F32)
        spectrum = spectrum + jnp.dot(g_high, low_ref[...], preferred_element_type=F32)
        spectrum = spectrum.astype(BF16)
        for dest in range(copies):
            spec_ref[dest] = spectrum


def power_kernel(own_ref, far_ref, power_ref, norm):
    total = own_ref[...] + far_ref[...].astype(F32)
    real, imag = total[:, :TIME], total[:, TIME:]
    power_ref[...] = (real * real + imag * imag) * norm


def turn_kernel(delay_ref, turn_ref):
    trials, chans = delay_ref.shape
    dc, ds = cos_sin_turns(delay_ref[...].astype(F32) * (1.0 / TIME))
    c, s = dc, ds
    for k in range(HALF_BINS):
        rows = slice(k * trials, (k + 1) * trials)
        turn_ref[rows, :chans] = c.astype(BF16)
        turn_ref[rows, chans:] = s.astype(BF16)
        c, s = c * dc - s * ds, c * ds + s * dc


def plane_kernel(spec_ref, turn_ref, out_ref, both_ref, part_ref):
    chans, width = spec_ref.shape
    _, _, trials = out_ref.shape
    spec = spec_ref[...]
    values = spec.astype(F32)
    lane = lax.broadcasted_iota(jnp.int32, (chans, width), 1)
    ahead = pltpu.roll(values, width - HALF_BINS, 1)
    behind = pltpu.roll(values, HALF_BINS, 1)
    turned = jnp.where(lane % TIME < HALF_BINS, -ahead, behind)
    both_ref[:chans] = spec
    both_ref[chans:] = turned.astype(BF16)
    bin_id = lax.broadcasted_iota(jnp.int32, (trials, width), 1) % HALF_BINS
    plane = jnp.zeros((trials, width), F32)
    group = HALF_BINS // 2
    for first in range(0, HALF_BINS, group):
        rows = slice(first * trials, (first + group) * trials)
        part_ref[...] = jnp.dot(turn_ref[rows], both_ref[...], preferred_element_type=F32)
        for k in range(group):
            part = part_ref[k * trials : (k + 1) * trials]
            plane = jnp.where(bin_id == first + k, part, plane)
    out_ref[...] = (plane.T * (1.0 / math.sqrt(CH))).reshape(out_ref.shape)


SMALL = pltpu.CompilerParams(vmem_limit_bytes=12 << 20)
LARGE = pltpu.CompilerParams(vmem_limit_bytes=60 << 20)


def fold(voltages, table, block_id, dests, chans):
    inputs, samples = voltages.shape
    rows = 2 * dests * chans
    window = jnp.asarray(pfb_window())
    block = min(32, inputs)
    spectra = jax.ShapeDtypeStruct((dests, chans, 2 * TIME, inputs), BF16)
    folded = jax.ShapeDtypeStruct((TIME * inputs, FFTLEN), BF16)
    whole = lambda x: pl.BlockSpec(x.shape, lambda i, k: (0,) * len(x.shape))
    return pl.pallas_call(
        fold_kernel,
        out_shape=(spectra, folded),
        grid_spec=pltpu.PrefetchScalarGridSpec(
            num_scalar_prefetch=1,
            grid=(inputs // block,),
            in_specs=[
                pl.BlockSpec((block, samples), lambda i, k: (i, 0)),
                whole(window),
                pl.BlockSpec((rows, FFTLEN), lambda i, k: (k[0], 0)),
            ],
            out_specs=(whole(spectra), whole(folded)),
            scratch_shapes=[pltpu.VMEM((rows * PITCH, inputs), F32)],
        ),
        compiler_params=LARGE,
        cost_estimate=pl.CostEstimate(
            flops=8 * rows * FFTLEN * TIME * inputs, bytes_accessed=12 << 20, transcendentals=0
        ),
        name="fold",
    )(block_id, voltages, window, table)


def more_spectra(folded, table, block_id, dests, chans):
    rows = 2 * dests * chans
    inputs = folded.shape[0] // TIME
    out = jax.ShapeDtypeStruct((dests, chans, 2 * TIME, inputs), BF16)
    return pl.pallas_call(
        spectra_kernel,
        out_shape=out,
        grid_spec=pltpu.PrefetchScalarGridSpec(
            num_scalar_prefetch=1,
            grid=(1,),
            in_specs=[
                pl.BlockSpec(folded.shape, lambda i, k: (0, 0)),
                pl.BlockSpec((rows, FFTLEN), lambda i, k: (k[0], 0)),
            ],
            out_specs=pl.BlockSpec(out.shape, lambda i, k: (0, 0, 0, 0)),
            scratch_shapes=[pltpu.VMEM((rows * PITCH, inputs), F32)],
        ),
        compiler_params=LARGE,
        cost_estimate=pl.CostEstimate(
            flops=4 * rows * FFTLEN * TIME * inputs, bytes_accessed=6 << 20, transcendentals=0
        ),
        name="spectra",
    )(block_id, folded, table)


def phasors(first, places, directions, count):
    total, beams = places.shape[0], directions.shape[1]
    depth = 128
    return pl.pallas_call(
        phasor_kernel,
        out_shape=[jax.ShapeDtypeStruct((total, beams), F32)] * count,
        grid_spec=pltpu.PrefetchScalarGridSpec(
            num_scalar_prefetch=1,
            grid=(total // depth,),
            in_specs=[
                pl.BlockSpec((depth, 3), lambda i, f: (i, 0)),
                pl.BlockSpec(directions.shape, lambda i, f: (0, 0)),
            ],
            out_specs=[pl.BlockSpec((depth, beams), lambda i, f: (i, 0))] * count,
        ),
        compiler_params=LARGE,
        cost_estimate=pl.CostEstimate(
            flops=8000 * total * beams, bytes_accessed=count * 4 * total * beams, transcendentals=0
        ),
        name="phasors",
    )(first, places, directions)


def form_beams(x, gains, state, beams, out_type):
    sources, chans, rows, inputs = x.shape
    total = sources * inputs
    if inputs != 128:
        x = x.transpose(1, 2, 0, 3).reshape(chans, rows, total // 128, 128)
        x = x.transpose(2, 0, 1, 3)
    depth = 256
    blocks = depth // 128
    tiles = total // depth
    late = lambda i: jnp.maximum(i - 1, 0)
    state_spec = pl.BlockSpec((depth, beams), lambda i: (jnp.minimum(i, tiles - 1), 0))
    return pl.pallas_call(
        beam_kernel,
        out_shape=jax.ShapeDtypeStruct((chans, rows, beams), out_type),
        grid=(tiles + 1,),
        in_specs=[
            pl.BlockSpec((blocks, chans, rows, 128), lambda i: (late(i), 0, 0, 0)),
            pl.BlockSpec((chans, 2, depth), lambda i: (0, 0, late(i))),
        ]
        + [state_spec] * 4,
        out_specs=pl.BlockSpec((chans, rows, beams), lambda i: (0, 0, 0)),
        scratch_shapes=[
            pltpu.VMEM((chans, 2 * depth, beams), BF16),
            pltpu.VMEM((chans, 2 * depth, beams), BF16),
            pltpu.VMEM((chans, rows, beams), F32),
        ],
        compiler_params=LARGE,
        cost_estimate=pl.CostEstimate(
            flops=16 * chans * rows * total * beams, bytes_accessed=12 << 20, transcendentals=0
        ),
        name="beams",
    )(x, gains, *state)


def flat(shape):
    return pl.BlockSpec(shape, lambda i: (0,) * len(shape))


def cubes(block, *arrays):
    return [pl.BlockSpec((block, *x.shape[1:]), lambda i: (i, 0, 0)) for x in arrays]


def pick_far(sums, pick, search):
    chans = sums.shape[0]
    block = min(4, chans)
    out = jax.ShapeDtypeStruct((2 * chans, TIME * search), BF16)
    return pl.pallas_call(
        far_pick_kernel,
        out_shape=out,
        grid=(chans // block,),
        in_specs=cubes(block, sums) + [flat(pick.shape)],
        out_specs=flat(out.shape),
        scratch_shapes=[pltpu.VMEM(out.shape, F32)],
        compiler_params=LARGE,
        cost_estimate=pl.CostEstimate(
            flops=1 << 30, bytes_accessed=2 << 20, transcendentals=0
        ),
        name="pick",
    )(sums, pick)


def search_spectra(own, far, pick, search, copies, norm):
    chans = own.shape[0]
    width = TIME * search
    table = time_table(search)
    high = jnp.asarray(table).astype(BF16)
    low = (jnp.asarray(table) - high.astype(F32)).astype(BF16)
    block = min(4, chans)
    out = jax.ShapeDtypeStruct((copies, chans, width), BF16)
    return pl.pallas_call(
        functools.partial(spectrum_kernel, norm=norm),
        out_shape=out,
        grid=(chans // block,),
        in_specs=cubes(block, own) + [flat(x.shape) for x in (far, pick, high, low)],
        out_specs=flat(out.shape),
        scratch_shapes=[pltpu.VMEM((2 * chans, width), F32)],
        compiler_params=LARGE,
        cost_estimate=pl.CostEstimate(
            flops=2 << 30, bytes_accessed=4 << 20, transcendentals=0
        ),
        name="spectrum",
    )(own, far, pick, high, low)


def powers(own, far, norm):
    chans, _, beams = own.shape
    block = min(4, chans)
    out = jax.ShapeDtypeStruct((chans, TIME, beams), F32)
    return pl.pallas_call(
        functools.partial(power_kernel, norm=norm),
        out_shape=out,
        grid=(chans // block,),
        in_specs=cubes(block, own, far),
        out_specs=cubes(block, out)[0],
        compiler_params=LARGE,
        cost_estimate=pl.CostEstimate(
            flops=1 << 28, bytes_accessed=5 << 20, transcendentals=0
        ),
        name="power",
    )(own, far)


def on_device(voltages, gains, positions, directions, input_order, delays, search_beams):
    devices = lax.axis_size("crate")
    position = lax.axis_index("crate")
    chans = gains.shape[0]
    halves = 2
    per_half = devices // halves
    half_id = position // per_half
    members = [list(range(h * per_half, (h + 1) * per_half)) for h in range(halves)]
    partners = [(d, (d + per_half) % devices) for d in range(devices)]
    inputs = gains.shape[2] // halves
    own_inputs = half_id * inputs
    half_scalar = half_id.astype(jnp.int32).reshape(1)
    table = jnp.asarray(dft_table()).astype(BF16)
    far, folded = fold(voltages, table, 1 - half_scalar, per_half, chans)

    def exchange(x):
        return lax.all_to_all(
            x, "crate", split_axis=0, concat_axis=0, axis_index_groups=members, tiled=True
        )

    far = exchange(far)
    near = more_spectra(folded, table, half_scalar, per_half, chans)
    near, gains, positions = lax.optimization_barrier((near, gains, positions))
    far_gains = lax.dynamic_slice_in_dim(gains, inputs - own_inputs, inputs, 2)
    far_gains = lax.ppermute(far_gains, "crate", partners)
    near_gains = lax.dynamic_slice_in_dim(gains, own_inputs, inputs, 2)
    order = lax.dynamic_slice_in_dim(input_order, own_inputs, inputs, 0)
    places = jnp.take(positions.T, order, axis=0)
    search = search_beams.shape[0]
    pick = jnp.tile(search_beams, 128 // search)[None, :]
    own_first = (position * chans).astype(jnp.int32).reshape(1)
    far_first = ((position + per_half) % devices * chans).astype(jnp.int32).reshape(1)
    far_c, far_s, dc, ds = phasors(far_first, places, directions, 4)
    near, near_gains, pick, own_first, dc, ds, far_c, far_s = lax.optimization_barrier(
        (near, near_gains, pick, own_first, dc, ds, far_c, far_s)
    )
    near = exchange(near)

    beams = directions.shape[1]
    norm = 1.0 / gains.shape[2]
    sums = form_beams(far, far_gains, (dc, ds, far_c, far_s), beams, BF16)
    picked = pick_far(sums, pick, search)
    far_picked = lax.ppermute(picked, "crate", partners)
    far_sums = lax.ppermute(sums, "crate", partners)
    own_first, picked = lax.optimization_barrier((own_first, picked))
    near_c, near_s = phasors(own_first, places, directions, 2)
    near_sums = form_beams(near, near_gains, (dc, ds, near_c, near_s), beams, F32)

    spectrum = search_spectra(near_sums, far_picked, pick, search, devices, norm)
    near_sums, spectrum = lax.optimization_barrier((near_sums, spectrum))
    spectrum = lax.all_to_all(spectrum, "crate", split_axis=0, concat_axis=0, tiled=True)
    beam_power = powers(near_sums, far_sums, norm)
    width = spectrum.shape[-1]
    trials = delays.shape[0] // devices
    own_delays = lax.dynamic_slice_in_dim(delays, position * trials, trials, 0)
    turns = pl.pallas_call(
        turn_kernel,
        out_shape=jax.ShapeDtypeStruct((HALF_BINS * trials, 2 * CH), BF16),
        compiler_params=LARGE,
        name="turns",
    )(own_delays)
    dm_plane = pl.pallas_call(
        plane_kernel,
        out_shape=jax.ShapeDtypeStruct((search, TIME, trials), F32),
        scratch_shapes=[
            pltpu.VMEM((2 * CH, width), BF16),
            pltpu.VMEM((HALF_BINS // 2 * trials, width), F32),
        ],
        compiler_params=SMALL,
        name="plane",
    )(spectrum.reshape(CH, width), turns)
    return beam_power.transpose(0, 2, 1), dm_plane.transpose(2, 0, 1)


def solution(mesh):
    in_specs = (P(("groups", "crate"), None), P("crate", None, None), P(), P(), P(), P(), P())
    out_specs = (P(("groups", "crate"), None, None), P(("groups", "crate"), None, None))
    return jax.shard_map(
        on_device, mesh=mesh, in_specs=in_specs, out_specs=out_specs, check_vma=False
    )
```

```python
import functools
import math

import jax
import jax.numpy as jnp
import numpy as np
from jax import lax
from jax.experimental import pallas as pl
from jax.experimental.pallas import tpu as pltpu
from jax.sharding import PartitionSpec as P

CH = 256
TAPS = 4
TIME = 32
PITCH = 40
FFTLEN = 512
HALF_BINS = TIME // 2
TWO_PI = 2.0 * math.pi
F32 = jnp.float32
BF16 = jnp.bfloat16
NT = (((1,), (1,)), ((), ()))

SIN_POLY = (
    6.283185302511503,
    -41.34170040531769,
    81.60513138580204,
    -76.7030153539128,
    42.02592698618416,
    -14.899846668691637,
    3.238137510515757,
)
COS_POLY = (
    0.9999999890590228,
    -19.739204499454026,
    64.93911745990036,
    -85.45013953095037,
    60.16763093136588,
    -25.96759924965491,
    6.528658162567069,
)


def pfb_window():
    n = np.arange(TAPS * FFTLEN, dtype=np.float64)
    offsets = (n - 0.5 * TAPS * FFTLEN + 0.5) / FFTLEN
    tapering = 0.54 - 0.46 * np.cos(TWO_PI * n / (TAPS * FFTLEN - 1))
    return (np.sinc(offsets) * tapering).reshape(TAPS, FFTLEN).astype(np.float32)


def dft_table():
    angles = TWO_PI * (np.arange(CH)[:, None] * np.arange(FFTLEN)[None, :] % FFTLEN) / FFTLEN
    stacked = np.stack([np.cos(angles), -np.sin(angles)], axis=1) / math.sqrt(FFTLEN)
    return stacked.reshape(2 * CH, FFTLEN).astype(np.float32)


def time_table(search):
    turns = np.arange(TIME)[:, None] * np.arange(1, HALF_BINS + 1)[None, :] % TIME
    angles = TWO_PI * turns / TIME
    table = np.concatenate([np.cos(angles), -np.sin(angles)], axis=1) / math.sqrt(TIME)
    full = np.einsum("tk,qp->tqpk", table, np.eye(search))
    return full.reshape(TIME * search, search * TIME).astype(np.float32)


def polynomial(z, coefficients):
    total = jnp.full_like(z, coefficients[-1])
    for value in coefficients[-2::-1]:
        total = total * z + value
    return total


def cos_sin_turns(turns):
    r = turns - jnp.round(turns)
    z = r * r
    return polynomial(z, COS_POLY), polynomial(z, SIN_POLY) * r


def split_bf16(x):
    high = x.astype(BF16)
    return high, (x - high.astype(F32)).astype(BF16)


def transform_rows(table, folded_ref, spread_ref, out_ref):
    dests, chans, _, inputs = out_ref.shape
    rows = table.shape[0]
    group = 2 if inputs % 128 == 0 else 1

    def step(index, carry):
        start = pl.multiple_of(index * (group * inputs), group * inputs)
        frames = folded_ref[pl.ds(start, group * inputs), :]
        out = lax.dot_general(table, frames, NT, preferred_element_type=F32)
        for part in range(group):
            piece = out[:, part * inputs : (part + 1) * inputs]
            spread_ref[pl.ds(index * group + part, rows, stride=PITCH), :] = piece
        return carry

    lax.fori_loop(0, TIME // group, step, 0, unroll=4)

    def pack(dest, carry):
        for chan in range(chans):
            for part in range(2):
                start = pl.multiple_of(((dest * chans + chan) * 2 + part) * PITCH, 8)
                block = spread_ref[pl.ds(start, TIME), :].astype(BF16)
                out_ref[dest, chan, part * TIME : (part + 1) * TIME] = block
        return carry

    lax.fori_loop(0, dests, pack, 0, unroll=2)


def fold_kernel(half_ref, volt_ref, window_ref, table_ref, out_ref, folded_ref, spread_ref):
    step = pl.program_id(0)
    rows = volt_ref.shape[0]
    inputs = out_ref.shape[-1]
    lanes = 256
    for lane in range(0, FFTLEN, lanes):
        taps = [window_ref[j : j + 1, lane : lane + lanes] for j in range(TAPS)]
        for row in range(0, rows, 16):
            frames = []
            for t in range(TIME + TAPS - 1):
                start = t * FFTLEN + lane
                frames.append(volt_ref[row : row + 16, start : start + lanes].astype(F32))
                if t >= TAPS - 1:
                    first = t - TAPS + 1
                    total = taps[0] * frames[first]
                    for j in range(1, TAPS):
                        total = total + taps[j] * frames[first + j]
                    place = pl.multiple_of(first * inputs + step * rows + row, 16)
                    folded_ref[pl.ds(place, 16), lane : lane + lanes] = total.astype(BF16)

    @pl.when(step == pl.num_programs(0) - 1)
    def _():
        transform_rows(table_ref[...], folded_ref, spread_ref, out_ref)


def spectra_kernel(block_ref, folded_ref, table_ref, out_ref, spread_ref):
    transform_rows(table_ref[...], folded_ref, spread_ref, out_ref)


def phasor_kernel(first_ref, place_ref, dir_ref, *out_refs):
    depth, beams = out_refs[0].shape
    wide = 256

    def block(index, carry):
        rows = pl.ds(pl.multiple_of(index * 16, 16), 16)
        place = place_ref[rows, :]
        for lane in range(0, beams, wide):
            lanes = slice(lane, lane + wide)
            direction = dir_ref[:, lanes]
            geometry = place[:, 0:1] * direction[0:1, :]
            geometry = geometry + place[:, 1:2] * direction[1:2, :]
            geometry = geometry + place[:, 2:3] * direction[2:3, :]
            first = 1.0 + first_ref[0].astype(F32) * (1.0 / CH)
            for k, scale in enumerate((first, 1.0 / CH)[: len(out_refs) // 2]):
                c, s = cos_sin_turns(geometry * scale)
                out_refs[2 * k][rows, lanes], out_refs[2 * k + 1][rows, lanes] = c, s
        return carry

    lax.fori_loop(0, depth // 16, block, 0, unroll=2)


def beam_kernel(
    x_ref, gain_ref, dc_ref, ds_ref, c_ref, s_ref, out_ref, even_ref, odd_ref, sum_ref
):
    step = pl.program_id(0)
    tiles = pl.num_programs(0) - 1
    chans, _, beams = out_ref.shape
    depth = dc_ref.shape[0]
    wide = 256 if beams % 256 == 0 else 128
    chunk = depth // chans

    def generate(part, weight_ref):
        for sub in range(0, chunk, 16):
            row = pl.multiple_of(part * chunk + sub, 16)
            rows = pl.ds(row, 16)
            for lane in range(0, beams, wide):
                lanes = slice(lane, lane + wide)
                c, s = c_ref[rows, lanes], s_ref[rows, lanes]
                dc, ds = dc_ref[rows, lanes], ds_ref[rows, lanes]
                next_c, next_s = c * dc - s * ds, c * ds + s * dc
                twice = dc + dc
                for chan in range(chans):
                    weight_ref[chan, rows, lanes] = c.astype(BF16)
                    weight_ref[chan, pl.ds(depth + row, 16), lanes] = s.astype(BF16)
                    if chan + 2 < chans:
                        c, next_c = next_c, twice * next_c - c
                        s, next_s = next_s, twice * next_s - s
                    else:
                        c, s = next_c, next_s

    def accumulate(chan, weight_ref):
        blocks = x_ref.shape[0]
        data = jnp.concatenate([x_ref[k, chan] for k in range(blocks)], axis=1).astype(F32)
        real, imag = data[:TIME], data[TIME:]
        gain = gain_ref[chan]
        x0 = (gain[0:1] * real - gain[1:2] * imag).astype(BF16)
        x1 = (gain[0:1] * imag + gain[1:2] * real).astype(BF16)
        top = jnp.concatenate([x0, x1], axis=1)
        bottom = jnp.concatenate([x1, -x0], axis=1)
        both = jnp.concatenate([top, bottom], axis=0)
        return jnp.dot(both, weight_ref[chan], preferred_element_type=F32)

    def both(m, weights):
        sum_ref[m] += accumulate(m, weights[0])
        generate(m, weights[1])

    def last(m, weights):
        out_ref[m] = (sum_ref[m] + accumulate(m, weights[0])).astype(out_ref.dtype)

    def over_channels(body, weights, unroll=min(8, chans)):
        lax.fori_loop(0, chans, lambda m, v: (body(m, weights), v)[1], 0, unroll=unroll)

    @pl.when(step == 0)
    def _():
        sum_ref[...] = jnp.zeros_like(sum_ref)
        over_channels(generate, even_ref, 1)

    for parity, weights in ((1, (even_ref, odd_ref)), (0, (odd_ref, even_ref))):

        @pl.when((step > 0) & (step < tiles) & (lax.rem(step, 2) == parity))
        def _(weights=weights):
            over_channels(both, weights)

        @pl.when((step == tiles) & (lax.rem(step, 2) == parity))
        def _(weights=weights):
            over_channels(last, weights)


def pick_beams(rows, pick_ref, chans, search):
    per = 128 // search
    hit = lax.broadcasted_iota(jnp.int32, (rows.shape[1], 128), 0) == pick_ref[...]
    hot = jnp.where(hit, 1.0, 0.0).astype(BF16)
    if rows.dtype == BF16:
        picked = jnp.dot(rows, hot, preferred_element_type=F32)
    else:
        high, low = split_bf16(rows)
        picked = jnp.dot(high, hot, preferred_element_type=F32)
        picked = picked + jnp.dot(low, hot, preferred_element_type=F32)
    row_id = lax.broadcasted_iota(jnp.int32, (per, 128), 0)
    lane_id = lax.broadcasted_iota(jnp.int32, (per, 128), 1) // search
    chosen = []
    for chan in range(chans):
        pieces = []
        for j in range(TIME // per):
            start = chan * TIME + j * per
            piece = jnp.where(row_id == lane_id, picked[start : start + per], 0.0)
            pieces.append(jnp.sum(piece, axis=0, keepdims=True))
        chosen.append(jnp.concatenate(pieces, axis=1))
    return chosen


def far_pick_kernel(sum0_ref, sum1_ref, pick_ref, out_ref, picked_ref):
    step = pl.program_id(0)
    block = sum0_ref.shape[0]
    search = out_ref.shape[1] // TIME
    both = jnp.concatenate([sum0_ref[...], sum1_ref[...]], axis=2)
    rows = both.reshape(block * 2 * TIME, both.shape[2])
    half = picked_ref.shape[0] // 2
    for k, row in enumerate(pick_beams(rows, pick_ref, 2 * block, search)):
        place = (k % 2) * half + step * block + k // 2
        picked_ref[pl.ds(place, 1), :] = row

    @pl.when(step == pl.num_programs(0) - 1)
    def _():
        out_ref[...] = picked_ref[...].astype(BF16)


def spectrum_kernel(
    own_ref, far_ref, pick_ref, high_ref, low_ref, spec_ref, picked_ref, norm
):
    step = pl.program_id(0)
    block = own_ref.shape[0]
    copies, chans, width = spec_ref.shape
    search = width // TIME
    rows = own_ref[...].reshape(block * 2 * TIME, own_ref.shape[2])
    for k, row in enumerate(pick_beams(rows, pick_ref, 2 * block, search)):
        place = (k % 2) * chans + step * block + k // 2
        picked_ref[pl.ds(place, 1), :] = row

    @pl.when(step == pl.num_programs(0) - 1)
    def _():
        real = picked_ref[:chans] + far_ref[:chans].astype(F32)
        imag = picked_ref[chans:] + far_ref[chans:].astype(F32)
        g_high, g_low = split_bf16((real * real + imag * imag) * norm)
        spectrum = jnp.dot(g_high, high_ref[...], preferred_element_type=F32)
        spectrum = spectrum + jnp.dot(g_low, high_ref[...], preferred_element_type=F32)
        spectrum = spectrum + jnp.dot(g_high, low_ref[...], preferred_element_type=F32)
        spectrum = spectrum.astype(BF16)
        for dest in range(copies):
            spec_ref[dest] = spectrum


def power_kernel(own_ref, far0_ref, far1_ref, power_ref, norm):
    far = jnp.concatenate([far0_ref[...], far1_ref[...]], axis=2)
    total = own_ref[...] + far.astype(F32)
    real, imag = total[:, :TIME], total[:, TIME:]
    power_ref[...] = (real * real + imag * imag) * norm


def turn_kernel(delay_ref, turn_ref):
    trials, chans = delay_ref.shape
    dc, ds = cos_sin_turns(delay_ref[...].astype(F32) * (1.0 / TIME))
    c, s = dc, ds
    for k in range(HALF_BINS):
        rows = slice(k * trials, (k + 1) * trials)
        turn_ref[rows, :chans] = c.astype(BF16)
        turn_ref[rows, chans:] = s.astype(BF16)
        c, s = c * dc - s * ds, c * ds + s * dc


def plane_kernel(spec_ref, turn_ref, out_ref, both_ref, part_ref):
    chans, width = spec_ref.shape
    _, _, trials = out_ref.shape
    spec = spec_ref[...]
    values = spec.astype(F32)
    lane = lax.broadcasted_iota(jnp.int32, (chans, width), 1)
    ahead = pltpu.roll(values, width - HALF_BINS, 1)
    behind = pltpu.roll(values, HALF_BINS, 1)
    turned = jnp.where(lane % TIME < HALF_BINS, -ahead, behind)
    both_ref[:chans] = spec
    both_ref[chans:] = turned.astype(BF16)
    bin_id = lax.broadcasted_iota(jnp.int32, (trials, width), 1) % HALF_BINS
    plane = jnp.zeros((trials, width), F32)
    group = HALF_BINS // 2
    for first in range(0, HALF_BINS, group):
        rows = slice(first * trials, (first + group) * trials)
        part_ref[...] = jnp.dot(turn_ref[rows], both_ref[...], preferred_element_type=F32)
        for k in range(group):
            part = part_ref[k * trials : (k + 1) * trials]
            plane = jnp.where(bin_id == first + k, part, plane)
    out_ref[...] = (plane.T * (1.0 / math.sqrt(CH))).reshape(out_ref.shape)


SMALL = pltpu.CompilerParams(vmem_limit_bytes=12 << 20)
LARGE = pltpu.CompilerParams(vmem_limit_bytes=60 << 20)


def fold(voltages, table, block_id, dests, chans):
    inputs, samples = voltages.shape
    rows = 2 * dests * chans
    window = jnp.asarray(pfb_window())
    block = min(32, inputs)
    spectra = jax.ShapeDtypeStruct((dests, chans, 2 * TIME, inputs), BF16)
    folded = jax.ShapeDtypeStruct((TIME * inputs, FFTLEN), BF16)
    whole = lambda x: pl.BlockSpec(x.shape, lambda i, k: (0,) * len(x.shape))
    return pl.pallas_call(
        fold_kernel,
        out_shape=(spectra, folded),
        grid_spec=pltpu.PrefetchScalarGridSpec(
            num_scalar_prefetch=1,
            grid=(inputs // block,),
            in_specs=[
                pl.BlockSpec((block, samples), lambda i, k: (i, 0)),
                whole(window),
                pl.BlockSpec((rows, FFTLEN), lambda i, k: (k[0], 0)),
            ],
            out_specs=(whole(spectra), whole(folded)),
            scratch_shapes=[pltpu.VMEM((rows * PITCH, inputs), F32)],
        ),
        compiler_params=LARGE,
        cost_estimate=pl.CostEstimate(
            flops=8 * rows * FFTLEN * TIME * inputs, bytes_accessed=12 << 20, transcendentals=0
        ),
        name="fold",
    )(block_id, voltages, window, table)


def more_spectra(folded, table, block_id, dests, chans):
    rows = 2 * dests * chans
    inputs = folded.shape[0] // TIME
    out = jax.ShapeDtypeStruct((dests, chans, 2 * TIME, inputs), BF16)
    return pl.pallas_call(
        spectra_kernel,
        out_shape=out,
        grid_spec=pltpu.PrefetchScalarGridSpec(
            num_scalar_prefetch=1,
            grid=(1,),
            in_specs=[
                pl.BlockSpec(folded.shape, lambda i, k: (0, 0)),
                pl.BlockSpec((rows, FFTLEN), lambda i, k: (k[0], 0)),
            ],
            out_specs=pl.BlockSpec(out.shape, lambda i, k: (0, 0, 0, 0)),
            scratch_shapes=[pltpu.VMEM((rows * PITCH, inputs), F32)],
        ),
        compiler_params=LARGE,
        cost_estimate=pl.CostEstimate(
            flops=4 * rows * FFTLEN * TIME * inputs, bytes_accessed=6 << 20, transcendentals=0
        ),
        name="spectra",
    )(block_id, folded, table)


def phasors(first, places, directions, count):
    total, beams = places.shape[0], directions.shape[1]
    depth = 128
    return pl.pallas_call(
        phasor_kernel,
        out_shape=[jax.ShapeDtypeStruct((total, beams), F32)] * count,
        grid_spec=pltpu.PrefetchScalarGridSpec(
            num_scalar_prefetch=1,
            grid=(total // depth,),
            in_specs=[
                pl.BlockSpec((depth, 3), lambda i, f: (i, 0)),
                pl.BlockSpec(directions.shape, lambda i, f: (0, 0)),
            ],
            out_specs=[pl.BlockSpec((depth, beams), lambda i, f: (i, 0))] * count,
        ),
        compiler_params=LARGE,
        cost_estimate=pl.CostEstimate(
            flops=8000 * total * beams, bytes_accessed=count * 4 * total * beams, transcendentals=0
        ),
        name="phasors",
    )(first, places, directions)


def form_beams(x, gains, state, block, beams, out_type):
    sources, chans, rows, inputs = x.shape
    total = sources * inputs
    if inputs != 128:
        x = x.transpose(1, 2, 0, 3).reshape(chans, rows, total // 128, 128)
        x = x.transpose(2, 0, 1, 3)
    depth = 256
    blocks = depth // 128
    tiles = total // depth
    late = lambda i: jnp.maximum(i - 1, 0)
    state_spec = pl.BlockSpec((depth, beams), lambda i: (jnp.minimum(i, tiles - 1), block))
    return pl.pallas_call(
        beam_kernel,
        out_shape=jax.ShapeDtypeStruct((chans, rows, beams), out_type),
        grid=(tiles + 1,),
        in_specs=[
            pl.BlockSpec((blocks, chans, rows, 128), lambda i: (late(i), 0, 0, 0)),
            pl.BlockSpec((chans, 2, depth), lambda i: (0, 0, late(i))),
        ]
        + [state_spec] * 4,
        out_specs=pl.BlockSpec((chans, rows, beams), lambda i: (0, 0, 0)),
        scratch_shapes=[
            pltpu.VMEM((chans, 2 * depth, beams), BF16),
            pltpu.VMEM((chans, 2 * depth, beams), BF16),
            pltpu.VMEM((chans, rows, beams), F32),
        ],
        compiler_params=LARGE,
        cost_estimate=pl.CostEstimate(
            flops=16 * chans * rows * total * beams, bytes_accessed=12 << 20, transcendentals=0
        ),
        name="beams",
    )(x, gains, *state)


def flat(shape):
    return pl.BlockSpec(shape, lambda i: (0,) * len(shape))


def cubes(block, *arrays):
    return [pl.BlockSpec((block, *x.shape[1:]), lambda i: (i, 0, 0)) for x in arrays]


def pick_far(sums0, sums1, pick, search):
    chans = sums0.shape[0]
    block = min(4, chans)
    out = jax.ShapeDtypeStruct((2 * chans, TIME * search), BF16)
    return pl.pallas_call(
        far_pick_kernel,
        out_shape=out,
        grid=(chans // block,),
        in_specs=cubes(block, sums0, sums1) + [flat(pick.shape)],
        out_specs=flat(out.shape),
        scratch_shapes=[pltpu.VMEM(out.shape, F32)],
        compiler_params=LARGE,
        cost_estimate=pl.CostEstimate(
            flops=1 << 30, bytes_accessed=2 << 20, transcendentals=0
        ),
        name="pick",
    )(sums0, sums1, pick)


def search_spectra(own, far, pick, search, copies, norm):
    chans = own.shape[0]
    width = TIME * search
    table = time_table(search)
    high = jnp.asarray(table).astype(BF16)
    low = (jnp.asarray(table) - high.astype(F32)).astype(BF16)
    block = min(4, chans)
    out = jax.ShapeDtypeStruct((copies, chans, width), BF16)
    return pl.pallas_call(
        functools.partial(spectrum_kernel, norm=norm),
        out_shape=out,
        grid=(chans // block,),
        in_specs=cubes(block, own) + [flat(x.shape) for x in (far, pick, high, low)],
        out_specs=flat(out.shape),
        scratch_shapes=[pltpu.VMEM((2 * chans, width), F32)],
        compiler_params=LARGE,
        cost_estimate=pl.CostEstimate(
            flops=2 << 30, bytes_accessed=4 << 20, transcendentals=0
        ),
        name="spectrum",
    )(own, far, pick, high, low)


def powers(own, far, norm):
    chans, _, beams = own.shape
    block = min(4, chans)
    out = jax.ShapeDtypeStruct((chans, TIME, beams), F32)
    return pl.pallas_call(
        functools.partial(power_kernel, norm=norm),
        out_shape=out,
        grid=(chans // block,),
        in_specs=cubes(block, own, *far),
        out_specs=cubes(block, out)[0],
        compiler_params=LARGE,
        cost_estimate=pl.CostEstimate(
            flops=1 << 28, bytes_accessed=5 << 20, transcendentals=0
        ),
        name="power",
    )(own, *far)


def on_device(voltages, gains, positions, directions, input_order, delays, search_beams):
    devices = lax.axis_size("crate")
    position = lax.axis_index("crate")
    chans = gains.shape[0]
    halves = 2
    per_half = devices // halves
    half_id = position // per_half
    members = [list(range(h * per_half, (h + 1) * per_half)) for h in range(halves)]
    partners = [(d, (d + per_half) % devices) for d in range(devices)]
    inputs = gains.shape[2] // halves
    own_inputs = half_id * inputs
    half_scalar = half_id.astype(jnp.int32).reshape(1)
    table = jnp.asarray(dft_table()).astype(BF16)
    far, folded = fold(voltages, table, 1 - half_scalar, per_half, chans)

    def exchange(x):
        return lax.all_to_all(
            x, "crate", split_axis=0, concat_axis=0, axis_index_groups=members, tiled=True
        )

    far = exchange(far)
    near = more_spectra(folded, table, half_scalar, per_half, chans)
    near, gains, positions = lax.optimization_barrier((near, gains, positions))
    far_gains = lax.dynamic_slice_in_dim(gains, inputs - own_inputs, inputs, 2)
    far_gains = lax.ppermute(far_gains, "crate", partners)
    near_gains = lax.dynamic_slice_in_dim(gains, own_inputs, inputs, 2)
    order = lax.dynamic_slice_in_dim(input_order, own_inputs, inputs, 0)
    places = jnp.take(positions.T, order, axis=0)
    search = search_beams.shape[0]
    pick = jnp.tile(search_beams, 128 // search)[None, :]
    own_first = (position * chans).astype(jnp.int32).reshape(1)
    far_first = ((position + per_half) % devices * chans).astype(jnp.int32).reshape(1)
    far_c, far_s, dc, ds = phasors(far_first, places, directions, 4)
    near, near_gains, pick, own_first, dc, ds, far_c, far_s = lax.optimization_barrier(
        (near, near_gains, pick, own_first, dc, ds, far_c, far_s)
    )
    near = exchange(near)

    beams = directions.shape[1]
    norm = 1.0 / gains.shape[2]
    far_state = (dc, ds, far_c, far_s)
    few = beams // 4
    sums1 = form_beams(far, far_gains, far_state, 3, few, BF16)
    far1 = lax.ppermute(sums1, "crate", partners)
    far, far1_sums = lax.optimization_barrier((far, sums1))
    sums0 = form_beams(far, far_gains, far_state, 0, beams - few, BF16)
    picked = pick_far(sums0, far1_sums, pick, search)
    far_picked = lax.ppermute(picked, "crate", partners)
    far0 = lax.ppermute(sums0, "crate", partners)
    own_first, picked = lax.optimization_barrier((own_first, picked))
    near_c, near_s = phasors(own_first, places, directions, 2)
    near_sums = form_beams(near, near_gains, (dc, ds, near_c, near_s), 0, beams, F32)

    spectrum = search_spectra(near_sums, far_picked, pick, search, devices, norm)
    near_sums, spectrum = lax.optimization_barrier((near_sums, spectrum))
    spectrum = lax.all_to_all(spectrum, "crate", split_axis=0, concat_axis=0, tiled=True)
    beam_power = powers(near_sums, (far0, far1), norm)
    width = spectrum.shape[-1]
    trials = delays.shape[0] // devices
    own_delays = lax.dynamic_slice_in_dim(delays, position * trials, trials, 0)
    turns = pl.pallas_call(
        turn_kernel,
        out_shape=jax.ShapeDtypeStruct((HALF_BINS * trials, 2 * CH), BF16),
        compiler_params=LARGE,
        name="turns",
    )(own_delays)
    dm_plane = pl.pallas_call(
        plane_kernel,
        out_shape=jax.ShapeDtypeStruct((search, TIME, trials), F32),
        scratch_shapes=[
            pltpu.VMEM((2 * CH, width), BF16),
            pltpu.VMEM((HALF_BINS // 2 * trials, width), F32),
        ],
        compiler_params=SMALL,
        name="plane",
    )(spectrum.reshape(CH, width), turns)
    return beam_power.transpose(0, 2, 1), dm_plane.transpose(2, 0, 1)


def solution(mesh):
    in_specs = (P(("groups", "crate"), None), P("crate", None, None), P(), P(), P(), P(), P())
    out_specs = (P(("groups", "crate"), None, None), P(("groups", "crate"), None, None))
    return jax.shard_map(
        on_device, mesh=mesh, in_specs=in_specs, out_specs=out_specs, check_vma=False
    )
```

```python
import functools
import math

import jax
import jax.numpy as jnp
import numpy as np
from jax import lax
from jax.experimental import pallas as pl
from jax.experimental.pallas import tpu as pltpu
from jax.sharding import PartitionSpec as P

CH = 256
TAPS = 4
TIME = 32
PITCH = 40
FRAMES = 8
FFTLEN = 512
HALF_BINS = TIME // 2
TWO_PI = 2.0 * math.pi
F32 = jnp.float32
BF16 = jnp.bfloat16
NT = (((1,), (1,)), ((), ()))

SIN_POLY = (
    6.283185302511503,
    -41.34170040531769,
    81.60513138580204,
    -76.7030153539128,
    42.02592698618416,
    -14.899846668691637,
    3.238137510515757,
)
COS_POLY = (
    0.9999999890590228,
    -19.739204499454026,
    64.93911745990036,
    -85.45013953095037,
    60.16763093136588,
    -25.96759924965491,
    6.528658162567069,
)


def pfb_window():
    n = np.arange(TAPS * FFTLEN, dtype=np.float64)
    offsets = (n - 0.5 * TAPS * FFTLEN + 0.5) / FFTLEN
    tapering = 0.54 - 0.46 * np.cos(TWO_PI * n / (TAPS * FFTLEN - 1))
    return (np.sinc(offsets) * tapering).reshape(TAPS, FFTLEN).astype(np.float32)


def dft_table():
    angles = TWO_PI * (np.arange(CH)[:, None] * np.arange(FFTLEN)[None, :] % FFTLEN) / FFTLEN
    stacked = np.stack([np.cos(angles), -np.sin(angles)], axis=1) / math.sqrt(FFTLEN)
    return stacked.reshape(2 * CH, FFTLEN).astype(np.float32)


def time_table(search):
    turns = np.arange(TIME)[:, None] * np.arange(1, HALF_BINS + 1)[None, :] % TIME
    angles = TWO_PI * turns / TIME
    table = np.concatenate([np.cos(angles), -np.sin(angles)], axis=1) / math.sqrt(TIME)
    full = np.einsum("tk,qp->tqpk", table, np.eye(search))
    return full.reshape(TIME * search, search * TIME).astype(np.float32)


def polynomial(z, coefficients):
    total = jnp.full_like(z, coefficients[-1])
    for value in coefficients[-2::-1]:
        total = total * z + value
    return total


def cos_sin_turns(turns):
    r = turns - jnp.round(turns)
    z = r * r
    return polynomial(z, COS_POLY), polynomial(z, SIN_POLY) * r


def split_bf16(x):
    high = x.astype(BF16)
    return high, (x - high.astype(F32)).astype(BF16)


def group_size(inputs):
    return 2 if inputs % 128 == 0 else 1


def spread_spectra(table, frames, spread_ref, inputs, t):
    rows = table.shape[0]
    out = lax.dot_general(table, frames, NT, preferred_element_type=F32)
    for part in range(frames.shape[0] // inputs):
        piece = out[:, part * inputs : (part + 1) * inputs]
        spread_ref[pl.ds(t + part, rows, stride=PITCH), :] = piece


def pack_spectra(spread_ref, out_ref):
    dests, chans = out_ref.shape[:2]

    def pack(dest, carry):
        for chan in range(chans):
            for part in range(2):
                start = pl.multiple_of(((dest * chans + chan) * 2 + part) * PITCH, 8)
                block = spread_ref[pl.ds(start, TIME), :].astype(BF16)
                out_ref[dest, chan, part * TIME : (part + 1) * TIME] = block
        return carry

    lax.fori_loop(0, dests, pack, 0, unroll=2)


def fold_kernel(block_ref, volt_ref, *refs):
    next_refs, refs = refs[: TAPS - 1], refs[TAPS - 1 :]
    window_ref, table_ref, out_ref, folded_ref, even_ref, odd_ref, spread_ref = refs
    step = pl.program_id(0)
    last = TIME // FRAMES
    inputs = out_ref.shape[-1]
    lanes = 256

    def fold_piece(row, lane, kept_ref):
        taps = [window_ref[j : j + 1, lane : lane + lanes] for j in range(TAPS)]
        frames = []
        for t in range(FRAMES + TAPS - 1):
            ref, place = (volt_ref, t) if t < FRAMES else (next_refs[t - FRAMES], 0)
            start = place * FFTLEN + lane
            frames.append(ref[row : row + 16, start : start + lanes].astype(F32))
        for t in range(FRAMES):
            total = taps[0] * frames[t]
            for j in range(1, TAPS):
                total = total + taps[j] * frames[t + j]
            total = total.astype(BF16)
            place = t * inputs + row
            folded_ref[place : place + 16, lane : lane + lanes] = total
            kept_ref[place : place + 16, lane : lane + lanes] = total

    pieces = [(row, lane) for lane in range(0, FFTLEN, lanes) for row in range(0, inputs, 16)]

    def fold_some(kept_ref, some):
        for row, lane in some:
            fold_piece(row, lane, kept_ref)

    def transform(kept_ref, index):
        group = group_size(inputs)
        start = index * group * inputs
        frames = kept_ref[start : start + group * inputs, :]
        t = (step - 1) * FRAMES + index * group
        spread_spectra(table_ref[...], frames, spread_ref, inputs, t)

    count = FRAMES // group_size(inputs)

    @pl.when(step == 0)
    def _():
        fold_some(even_ref, pieces)

    for parity, (old_ref, new_ref) in ((1, (even_ref, odd_ref)), (0, (odd_ref, even_ref))):

        @pl.when((step > 0) & (step < last) & (lax.rem(step, 2) == parity))
        def _(old_ref=old_ref, new_ref=new_ref):
            for index in range(count):
                fold_some(new_ref, pieces[index::count])
                transform(old_ref, index)

        @pl.when((step == last) & (lax.rem(step, 2) == parity))
        def _(old_ref=old_ref):
            for index in range(count):
                transform(old_ref, index)
            pack_spectra(spread_ref, out_ref)


def spectra_kernel(block_ref, folded_ref, table_ref, out_ref, spread_ref):
    inputs = out_ref.shape[-1]
    group = group_size(inputs)

    def step(index, carry):
        start = pl.multiple_of(index * (group * inputs), group * inputs)
        frames = folded_ref[pl.ds(start, group * inputs), :]
        spread_spectra(table_ref[...], frames, spread_ref, inputs, index * group)
        return carry

    lax.fori_loop(0, TIME // group, step, 0, unroll=4)
    pack_spectra(spread_ref, out_ref)


def phasor_kernel(first_ref, place_ref, dir_ref, *out_refs):
    depth, beams = out_refs[0].shape
    wide = 256

    def block(index, carry):
        rows = pl.ds(pl.multiple_of(index * 16, 16), 16)
        place = place_ref[rows, :]
        for lane in range(0, beams, wide):
            lanes = slice(lane, lane + wide)
            direction = dir_ref[:, lanes]
            geometry = place[:, 0:1] * direction[0:1, :]
            geometry = geometry + place[:, 1:2] * direction[1:2, :]
            geometry = geometry + place[:, 2:3] * direction[2:3, :]
            scales = [1.0 / CH]
            for k in range(len(out_refs) // 2 - 1):
                scales.append(1.0 + first_ref[k].astype(F32) * (1.0 / CH))
            for k, scale in enumerate(scales):
                c, s = cos_sin_turns(geometry * scale)
                out_refs[2 * k][rows, lanes], out_refs[2 * k + 1][rows, lanes] = c, s
        return carry

    lax.fori_loop(0, depth // 16, block, 0, unroll=2)


def beam_kernel(
    x_ref, gain_ref, dc_ref, ds_ref, c_ref, s_ref, out_ref, even_ref, odd_ref, sum_ref
):
    step = pl.program_id(0)
    tiles = pl.num_programs(0) - 1
    chans, _, beams = out_ref.shape
    depth = dc_ref.shape[0]
    wide = 256 if beams % 256 == 0 else 128
    chunk = depth // chans

    def generate(part, weight_ref):
        for sub in range(0, chunk, 16):
            row = pl.multiple_of(part * chunk + sub, 16)
            rows = pl.ds(row, 16)
            for lane in range(0, beams, wide):
                lanes = slice(lane, lane + wide)
                c, s = c_ref[rows, lanes], s_ref[rows, lanes]
                dc, ds = dc_ref[rows, lanes], ds_ref[rows, lanes]
                next_c, next_s = c * dc - s * ds, c * ds + s * dc
                twice = dc + dc
                for chan in range(chans):
                    weight_ref[chan, rows, lanes] = c.astype(BF16)
                    weight_ref[chan, pl.ds(depth + row, 16), lanes] = s.astype(BF16)
                    if chan + 2 < chans:
                        c, next_c = next_c, twice * next_c - c
                        s, next_s = next_s, twice * next_s - s
                    else:
                        c, s = next_c, next_s

    def accumulate(chan, weight_ref):
        blocks = x_ref.shape[0]
        data = jnp.concatenate([x_ref[k, chan] for k in range(blocks)], axis=1).astype(F32)
        real, imag = data[:TIME], data[TIME:]
        gain = gain_ref[chan]
        x0 = (gain[0:1] * real - gain[1:2] * imag).astype(BF16)
        x1 = (gain[0:1] * imag + gain[1:2] * real).astype(BF16)
        top = jnp.concatenate([x0, x1], axis=1)
        bottom = jnp.concatenate([x1, -x0], axis=1)
        both = jnp.concatenate([top, bottom], axis=0)
        return jnp.dot(both, weight_ref[chan], preferred_element_type=F32)

    def both(m, weights):
        sum_ref[m] += accumulate(m, weights[0])
        generate(m, weights[1])

    def last(m, weights):
        out_ref[m] = (sum_ref[m] + accumulate(m, weights[0])).astype(out_ref.dtype)

    def over_channels(body, weights, unroll=min(8, chans)):
        lax.fori_loop(0, chans, lambda m, v: (body(m, weights), v)[1], 0, unroll=unroll)

    @pl.when(step == 0)
    def _():
        sum_ref[...] = jnp.zeros_like(sum_ref)
        over_channels(generate, even_ref, 1)

    for parity, weights in ((1, (even_ref, odd_ref)), (0, (odd_ref, even_ref))):

        @pl.when((step > 0) & (step < tiles) & (lax.rem(step, 2) == parity))
        def _(weights=weights):
            over_channels(both, weights)

        @pl.when((step == tiles) & (lax.rem(step, 2) == parity))
        def _(weights=weights):
            over_channels(last, weights)


def pick_beams(rows, pick_ref, chans, search):
    per = 128 // search
    hit = lax.broadcasted_iota(jnp.int32, (rows.shape[1], 128), 0) == pick_ref[...]
    hot = jnp.where(hit, 1.0, 0.0).astype(BF16)
    if rows.dtype == BF16:
        picked = jnp.dot(rows, hot, preferred_element_type=F32)
    else:
        high, low = split_bf16(rows)
        picked = jnp.dot(high, hot, preferred_element_type=F32)
        picked = picked + jnp.dot(low, hot, preferred_element_type=F32)
    row_id = lax.broadcasted_iota(jnp.int32, (per, 128), 0)
    lane_id = lax.broadcasted_iota(jnp.int32, (per, 128), 1) // search
    chosen = []
    for chan in range(chans):
        pieces = []
        for j in range(TIME // per):
            start = chan * TIME + j * per
            piece = jnp.where(row_id == lane_id, picked[start : start + per], 0.0)
            pieces.append(jnp.sum(piece, axis=0, keepdims=True))
        chosen.append(jnp.concatenate(pieces, axis=1))
    return chosen


def far_pick_kernel(sum0_ref, sum1_ref, pick_ref, out_ref, picked_ref):
    step = pl.program_id(0)
    block = sum0_ref.shape[0]
    search = out_ref.shape[1] // TIME
    both = jnp.concatenate([sum0_ref[...], sum1_ref[...]], axis=2)
    rows = both.reshape(block * 2 * TIME, both.shape[2])
    half = picked_ref.shape[0] // 2
    for k, row in enumerate(pick_beams(rows, pick_ref, 2 * block, search)):
        place = (k % 2) * half + step * block + k // 2
        picked_ref[pl.ds(place, 1), :] = row

    @pl.when(step == pl.num_programs(0) - 1)
    def _():
        out_ref[...] = picked_ref[...].astype(BF16)


def spectrum_kernel(
    own_ref, far_ref, pick_ref, high_ref, low_ref, spec_ref, picked_ref, norm
):
    step = pl.program_id(0)
    block = own_ref.shape[0]
    copies, chans, width = spec_ref.shape
    search = width // TIME
    rows = own_ref[...].reshape(block * 2 * TIME, own_ref.shape[2])
    for k, row in enumerate(pick_beams(rows, pick_ref, 2 * block, search)):
        place = (k % 2) * chans + step * block + k // 2
        picked_ref[pl.ds(place, 1), :] = row

    @pl.when(step == pl.num_programs(0) - 1)
    def _():
        real = picked_ref[:chans] + far_ref[:chans].astype(F32)
        imag = picked_ref[chans:] + far_ref[chans:].astype(F32)
        g_high, g_low = split_bf16((real * real + imag * imag) * norm)
        spectrum = jnp.dot(g_high, high_ref[...], preferred_element_type=F32)
        spectrum = spectrum + jnp.dot(g_low, high_ref[...], preferred_element_type=F32)
        spectrum = spectrum + jnp.dot(g_high, low_ref[...], preferred_element_type=F32)
        spectrum = spectrum.astype(BF16)
        for dest in range(copies):
            spec_ref[dest] = spectrum


def power_kernel(own_ref, far0_ref, far1_ref, power_ref, norm):
    far = jnp.concatenate([far0_ref[...], far1_ref[...]], axis=2)
    total = own_ref[...] + far.astype(F32)
    real, imag = total[:, :TIME], total[:, TIME:]
    power_ref[...] = (real * real + imag * imag) * norm


def turn_kernel(delay_ref, turn_ref):
    trials, chans = delay_ref.shape
    dc, ds = cos_sin_turns(delay_ref[...].astype(F32) * (1.0 / TIME))
    c, s = dc, ds
    for k in range(HALF_BINS):
        rows = slice(k * trials, (k + 1) * trials)
        turn_ref[rows, :chans] = c.astype(BF16)
        turn_ref[rows, chans:] = s.astype(BF16)
        c, s = c * dc - s * ds, c * ds + s * dc


def plane_kernel(spec_ref, turn_ref, out_ref, both_ref, part_ref):
    chans, width = spec_ref.shape
    _, _, trials = out_ref.shape
    spec = spec_ref[...]
    values = spec.astype(F32)
    lane = lax.broadcasted_iota(jnp.int32, (chans, width), 1)
    ahead = pltpu.roll(values, width - HALF_BINS, 1)
    behind = pltpu.roll(values, HALF_BINS, 1)
    turned = jnp.where(lane % TIME < HALF_BINS, -ahead, behind)
    both_ref[:chans] = spec
    both_ref[chans:] = turned.astype(BF16)
    bin_id = lax.broadcasted_iota(jnp.int32, (trials, width), 1) % HALF_BINS
    plane = jnp.zeros((trials, width), F32)
    group = HALF_BINS // 2
    for first in range(0, HALF_BINS, group):
        rows = slice(first * trials, (first + group) * trials)
        part_ref[...] = jnp.dot(turn_ref[rows], both_ref[...], preferred_element_type=F32)
        for k in range(group):
            part = part_ref[k * trials : (k + 1) * trials]
            plane = jnp.where(bin_id == first + k, part, plane)
    out_ref[...] = (plane.T * (1.0 / math.sqrt(CH))).reshape(out_ref.shape)


SMALL = pltpu.CompilerParams(vmem_limit_bytes=12 << 20)
LARGE = pltpu.CompilerParams(vmem_limit_bytes=60 << 20)


def fold(voltages, table, block_id, dests, chans):
    inputs = voltages.shape[0]
    rows = 2 * dests * chans
    window = jnp.asarray(pfb_window())
    last = TIME // FRAMES
    now = lambda i: jnp.minimum(i, last - 1)
    following = lambda j: pl.BlockSpec(
        (inputs, FFTLEN), lambda i, k: (0, (now(i) + 1) * FRAMES + j)
    )
    kept = pltpu.VMEM((FRAMES * inputs, FFTLEN), BF16)
    spectra = jax.ShapeDtypeStruct((dests, chans, 2 * TIME, inputs), BF16)
    folded = jax.ShapeDtypeStruct((TIME * inputs, FFTLEN), BF16)
    whole = lambda x: pl.BlockSpec(x.shape, lambda i, k: (0,) * len(x.shape))
    return pl.pallas_call(
        fold_kernel,
        out_shape=(spectra, folded),
        grid_spec=pltpu.PrefetchScalarGridSpec(
            num_scalar_prefetch=1,
            grid=(last + 1,),
            in_specs=[
                pl.BlockSpec((inputs, FRAMES * FFTLEN), lambda i, k: (0, now(i))),
                *[following(j) for j in range(TAPS - 1)],
                whole(window),
                pl.BlockSpec((rows, FFTLEN), lambda i, k: (k[0], 0)),
            ],
            out_specs=(
                whole(spectra),
                pl.BlockSpec((FRAMES * inputs, FFTLEN), lambda i, k: (now(i), 0)),
            ),
            scratch_shapes=[kept, kept, pltpu.VMEM((rows * PITCH, inputs), F32)],
        ),
        compiler_params=LARGE,
        cost_estimate=pl.CostEstimate(
            flops=8 * rows * FFTLEN * TIME * inputs, bytes_accessed=12 << 20, transcendentals=0
        ),
        name="fold",
    )(block_id, *[voltages] * TAPS, window, table)


def more_spectra(folded, table, block_id, dests, chans):
    rows = 2 * dests * chans
    inputs = folded.shape[0] // TIME
    out = jax.ShapeDtypeStruct((dests, chans, 2 * TIME, inputs), BF16)
    return pl.pallas_call(
        spectra_kernel,
        out_shape=out,
        grid_spec=pltpu.PrefetchScalarGridSpec(
            num_scalar_prefetch=1,
            grid=(1,),
            in_specs=[
                pl.BlockSpec(folded.shape, lambda i, k: (0, 0)),
                pl.BlockSpec((rows, FFTLEN), lambda i, k: (k[0], 0)),
            ],
            out_specs=pl.BlockSpec(out.shape, lambda i, k: (0, 0, 0, 0)),
            scratch_shapes=[pltpu.VMEM((rows * PITCH, inputs), F32)],
        ),
        compiler_params=LARGE,
        cost_estimate=pl.CostEstimate(
            flops=4 * rows * FFTLEN * TIME * inputs, bytes_accessed=6 << 20, transcendentals=0
        ),
        name="spectra",
    )(block_id, folded, table)


def phasors(firsts, places, directions):
    count = 2 + 2 * firsts.shape[0]
    total, beams = places.shape[0], directions.shape[1]
    depth = 128
    return pl.pallas_call(
        phasor_kernel,
        out_shape=[jax.ShapeDtypeStruct((total, beams), F32)] * count,
        grid_spec=pltpu.PrefetchScalarGridSpec(
            num_scalar_prefetch=1,
            grid=(total // depth,),
            in_specs=[
                pl.BlockSpec((depth, 3), lambda i, f: (i, 0)),
                pl.BlockSpec(directions.shape, lambda i, f: (0, 0)),
            ],
            out_specs=[pl.BlockSpec((depth, beams), lambda i, f: (i, 0))] * count,
        ),
        compiler_params=LARGE,
        cost_estimate=pl.CostEstimate(
            flops=8000 * total * beams, bytes_accessed=count * 4 * total * beams, transcendentals=0
        ),
        name="phasors",
    )(firsts, places, directions)


def form_beams(x, gains, state, block, beams, out_type):
    sources, chans, rows, inputs = x.shape
    total = sources * inputs
    if inputs != 128:
        x = x.transpose(1, 2, 0, 3).reshape(chans, rows, total // 128, 128)
        x = x.transpose(2, 0, 1, 3)
    depth = 256
    blocks = depth // 128
    tiles = total // depth
    late = lambda i: jnp.maximum(i - 1, 0)
    state_spec = pl.BlockSpec((depth, beams), lambda i: (jnp.minimum(i, tiles - 1), block))
    return pl.pallas_call(
        beam_kernel,
        out_shape=jax.ShapeDtypeStruct((chans, rows, beams), out_type),
        grid=(tiles + 1,),
        in_specs=[
            pl.BlockSpec((blocks, chans, rows, 128), lambda i: (late(i), 0, 0, 0)),
            pl.BlockSpec((chans, 2, depth), lambda i: (0, 0, late(i))),
        ]
        + [state_spec] * 4,
        out_specs=pl.BlockSpec((chans, rows, beams), lambda i: (0, 0, 0)),
        scratch_shapes=[
            pltpu.VMEM((chans, 2 * depth, beams), BF16),
            pltpu.VMEM((chans, 2 * depth, beams), BF16),
            pltpu.VMEM((chans, rows, beams), F32),
        ],
        compiler_params=LARGE,
        cost_estimate=pl.CostEstimate(
            flops=16 * chans * rows * total * beams, bytes_accessed=12 << 20, transcendentals=0
        ),
        name="beams",
    )(x, gains, *state)


def flat(shape):
    return pl.BlockSpec(shape, lambda i: (0,) * len(shape))


def cubes(block, *arrays):
    return [pl.BlockSpec((block, *x.shape[1:]), lambda i: (i, 0, 0)) for x in arrays]


def pick_far(sums0, sums1, pick, search):
    chans = sums0.shape[0]
    block = min(4, chans)
    out = jax.ShapeDtypeStruct((2 * chans, TIME * search), BF16)
    return pl.pallas_call(
        far_pick_kernel,
        out_shape=out,
        grid=(chans // block,),
        in_specs=cubes(block, sums0, sums1) + [flat(pick.shape)],
        out_specs=flat(out.shape),
        scratch_shapes=[pltpu.VMEM(out.shape, F32)],
        compiler_params=LARGE,
        cost_estimate=pl.CostEstimate(
            flops=1 << 30, bytes_accessed=2 << 20, transcendentals=0
        ),
        name="pick",
    )(sums0, sums1, pick)


def search_spectra(own, far, pick, search, copies, norm):
    chans = own.shape[0]
    width = TIME * search
    table = time_table(search)
    high = jnp.asarray(table).astype(BF16)
    low = (jnp.asarray(table) - high.astype(F32)).astype(BF16)
    block = min(4, chans)
    out = jax.ShapeDtypeStruct((copies, chans, width), BF16)
    return pl.pallas_call(
        functools.partial(spectrum_kernel, norm=norm),
        out_shape=out,
        grid=(chans // block,),
        in_specs=cubes(block, own) + [flat(x.shape) for x in (far, pick, high, low)],
        out_specs=flat(out.shape),
        scratch_shapes=[pltpu.VMEM((2 * chans, width), F32)],
        compiler_params=LARGE,
        cost_estimate=pl.CostEstimate(
            flops=2 << 30, bytes_accessed=4 << 20, transcendentals=0
        ),
        name="spectrum",
    )(own, far, pick, high, low)


def powers(own, far, norm):
    chans, _, beams = own.shape
    block = min(4, chans)
    out = jax.ShapeDtypeStruct((chans, TIME, beams), F32)
    return pl.pallas_call(
        functools.partial(power_kernel, norm=norm),
        out_shape=out,
        grid=(chans // block,),
        in_specs=cubes(block, own, *far),
        out_specs=cubes(block, out)[0],
        compiler_params=LARGE,
        cost_estimate=pl.CostEstimate(
            flops=1 << 28, bytes_accessed=5 << 20, transcendentals=0
        ),
        name="power",
    )(own, *far)


def on_device(voltages, gains, positions, directions, input_order, delays, search_beams):
    devices = lax.axis_size("crate")
    position = lax.axis_index("crate")
    chans = gains.shape[0]
    halves = 2
    per_half = devices // halves
    half_id = position // per_half
    members = [list(range(h * per_half, (h + 1) * per_half)) for h in range(halves)]
    partners = [(d, (d + per_half) % devices) for d in range(devices)]
    inputs = gains.shape[2] // halves
    own_inputs = half_id * inputs
    half_scalar = half_id.astype(jnp.int32).reshape(1)
    table = jnp.asarray(dft_table()).astype(BF16)
    far, folded = fold(voltages, table, 1 - half_scalar, per_half, chans)

    def exchange(x):
        return lax.all_to_all(
            x, "crate", split_axis=0, concat_axis=0, axis_index_groups=members, tiled=True
        )

    far = exchange(far)
    near = more_spectra(folded, table, half_scalar, per_half, chans)
    near, gains, positions = lax.optimization_barrier((near, gains, positions))
    far_gains = lax.dynamic_slice_in_dim(gains, inputs - own_inputs, inputs, 2)
    far_gains = lax.ppermute(far_gains, "crate", partners)
    near_gains = lax.dynamic_slice_in_dim(gains, own_inputs, inputs, 2)
    order = lax.dynamic_slice_in_dim(input_order, own_inputs, inputs, 0)
    places = jnp.take(positions.T, order, axis=0)
    search = search_beams.shape[0]
    pick = jnp.tile(search_beams, 128 // search)[None, :]
    firsts = jnp.stack([(position + per_half) % devices, position]) * chans
    dc, ds, far_c, far_s, near_c, near_s = phasors(
        firsts.astype(jnp.int32), places, directions
    )
    near, near_gains, pick, dc, ds, far_c, far_s = lax.optimization_barrier(
        (near, near_gains, pick, dc, ds, far_c, far_s)
    )
    near = exchange(near)

    beams = directions.shape[1]
    norm = 1.0 / gains.shape[2]
    far_state = (dc, ds, far_c, far_s)
    few = beams // 4
    sums1 = form_beams(far, far_gains, far_state, 3, few, BF16)
    far1 = lax.ppermute(sums1, "crate", partners)
    far, far1_sums = lax.optimization_barrier((far, sums1))
    sums0 = form_beams(far, far_gains, far_state, 0, beams - few, BF16)
    picked = pick_far(sums0, far1_sums, pick, search)
    far_picked = lax.ppermute(picked, "crate", partners)
    far0 = lax.ppermute(sums0, "crate", partners)
    near_sums = form_beams(near, near_gains, (dc, ds, near_c, near_s), 0, beams, F32)

    spectrum = search_spectra(near_sums, far_picked, pick, search, devices, norm)
    near_sums, spectrum = lax.optimization_barrier((near_sums, spectrum))
    spectrum = lax.all_to_all(spectrum, "crate", split_axis=0, concat_axis=0, tiled=True)
    beam_power = powers(near_sums, (far0, far1), norm)
    width = spectrum.shape[-1]
    trials = delays.shape[0] // devices
    own_delays = lax.dynamic_slice_in_dim(delays, position * trials, trials, 0)
    turns = pl.pallas_call(
        turn_kernel,
        out_shape=jax.ShapeDtypeStruct((HALF_BINS * trials, 2 * CH), BF16),
        compiler_params=LARGE,
        name="turns",
    )(own_delays)
    dm_plane = pl.pallas_call(
        plane_kernel,
        out_shape=jax.ShapeDtypeStruct((search, TIME, trials), F32),
        scratch_shapes=[
            pltpu.VMEM((2 * CH, width), BF16),
            pltpu.VMEM((HALF_BINS // 2 * trials, width), F32),
        ],
        compiler_params=SMALL,
        name="plane",
    )(spectrum.reshape(CH, width), turns)
    return beam_power.transpose(0, 2, 1), dm_plane.transpose(2, 0, 1)


def solution(mesh):
    in_specs = (P(("groups", "crate"), None), P("crate", None, None), P(), P(), P(), P(), P())
    out_specs = (P(("groups", "crate"), None, None), P(("groups", "crate"), None, None))
    return jax.shard_map(
        on_device, mesh=mesh, in_specs=in_specs, out_specs=out_specs, check_vma=False
    )
```

```python
import functools
import math

import jax
import jax.numpy as jnp
import numpy as np
from jax import lax
from jax.experimental import pallas as pl
from jax.experimental.pallas import tpu as pltpu
from jax.sharding import PartitionSpec as P

CH = 256
TAPS = 4
TIME = 32
PITCH = 40
FRAMES = 4
FFTLEN = 512
HALF_BINS = TIME // 2
TWO_PI = 2.0 * math.pi
F32 = jnp.float32
BF16 = jnp.bfloat16
NT = (((1,), (1,)), ((), ()))

SIN_POLY = (
    6.283185302511503,
    -41.34170040531769,
    81.60513138580204,
    -76.7030153539128,
    42.02592698618416,
    -14.899846668691637,
    3.238137510515757,
)
COS_POLY = (
    0.9999999890590228,
    -19.739204499454026,
    64.93911745990036,
    -85.45013953095037,
    60.16763093136588,
    -25.96759924965491,
    6.528658162567069,
)


def pfb_window():
    n = np.arange(TAPS * FFTLEN, dtype=np.float64)
    offsets = (n - 0.5 * TAPS * FFTLEN + 0.5) / FFTLEN
    tapering = 0.54 - 0.46 * np.cos(TWO_PI * n / (TAPS * FFTLEN - 1))
    return (np.sinc(offsets) * tapering).reshape(TAPS, FFTLEN).astype(np.float32)


def dft_table():
    angles = TWO_PI * (np.arange(CH)[:, None] * np.arange(FFTLEN)[None, :] % FFTLEN) / FFTLEN
    stacked = np.stack([np.cos(angles), -np.sin(angles)], axis=1) / math.sqrt(FFTLEN)
    return stacked.reshape(2 * CH, FFTLEN).astype(np.float32)


def time_table(search):
    turns = np.arange(TIME)[:, None] * np.arange(1, HALF_BINS + 1)[None, :] % TIME
    angles = TWO_PI * turns / TIME
    table = np.concatenate([np.cos(angles), -np.sin(angles)], axis=1) / math.sqrt(TIME)
    full = np.einsum("tk,qp->tqpk", table, np.eye(search))
    return full.reshape(TIME * search, search * TIME).astype(np.float32)


def polynomial(z, coefficients):
    total = jnp.full_like(z, coefficients[-1])
    for value in coefficients[-2::-1]:
        total = total * z + value
    return total


def cos_sin_turns(turns):
    r = turns - jnp.round(turns)
    z = r * r
    return polynomial(z, COS_POLY), polynomial(z, SIN_POLY) * r


def split_bf16(x):
    high = x.astype(BF16)
    return high, (x - high.astype(F32)).astype(BF16)


def group_size(inputs):
    return 2 if inputs % 128 == 0 else 1


def spread_spectra(table, frames, spread_ref, inputs, t):
    rows = table.shape[0]
    out = lax.dot_general(table, frames, NT, preferred_element_type=F32)
    for part in range(frames.shape[0] // inputs):
        piece = out[:, part * inputs : (part + 1) * inputs]
        spread_ref[pl.ds(t + part, rows, stride=PITCH), :] = piece


def pack_spectra(spread_ref, out_ref):
    dests, chans = out_ref.shape[:2]

    def pack(dest, carry):
        for chan in range(chans):
            for part in range(2):
                start = pl.multiple_of(((dest * chans + chan) * 2 + part) * PITCH, 8)
                block = spread_ref[pl.ds(start, TIME), :].astype(BF16)
                out_ref[dest, chan, part * TIME : (part + 1) * TIME] = block
        return carry

    lax.fori_loop(0, dests, pack, 0, unroll=2)


def fold_kernel(block_ref, volt_ref, *refs):
    next_refs, refs = refs[: TAPS - 1], refs[TAPS - 1 :]
    window_ref, table_ref, out_ref, folded_ref, even_ref, odd_ref, spread_ref = refs
    step = pl.program_id(0)
    last = TIME // FRAMES
    inputs = out_ref.shape[-1]
    lanes = 256

    def fold_piece(row, lane, kept_ref):
        taps = [window_ref[j : j + 1, lane : lane + lanes] for j in range(TAPS)]
        frames = []
        for t in range(FRAMES + TAPS - 1):
            ref, place = (volt_ref, t) if t < FRAMES else (next_refs[t - FRAMES], 0)
            start = place * FFTLEN + lane
            frames.append(ref[row : row + 16, start : start + lanes].astype(F32))
        for t in range(FRAMES):
            total = taps[0] * frames[t]
            for j in range(1, TAPS):
                total = total + taps[j] * frames[t + j]
            total = total.astype(BF16)
            place = t * inputs + row
            folded_ref[place : place + 16, lane : lane + lanes] = total
            kept_ref[place : place + 16, lane : lane + lanes] = total

    pieces = [(row, lane) for lane in range(0, FFTLEN, lanes) for row in range(0, inputs, 16)]

    def fold_some(kept_ref, some):
        for row, lane in some:
            fold_piece(row, lane, kept_ref)

    def transform(kept_ref, index):
        group = group_size(inputs)
        start = index * group * inputs
        frames = kept_ref[start : start + group * inputs, :]
        t = (step - 1) * FRAMES + index * group
        spread_spectra(table_ref[...], frames, spread_ref, inputs, t)

    count = FRAMES // group_size(inputs)

    @pl.when(step == 0)
    def _():
        fold_some(even_ref, pieces)

    for parity, (old_ref, new_ref) in ((1, (even_ref, odd_ref)), (0, (odd_ref, even_ref))):

        @pl.when((step > 0) & (step < last) & (lax.rem(step, 2) == parity))
        def _(old_ref=old_ref, new_ref=new_ref):
            for index in range(count):
                fold_some(new_ref, pieces[index::count])
                transform(old_ref, index)

        @pl.when((step == last) & (lax.rem(step, 2) == parity))
        def _(old_ref=old_ref):
            for index in range(count):
                transform(old_ref, index)
            pack_spectra(spread_ref, out_ref)


def spectra_kernel(block_ref, folded_ref, table_ref, out_ref, spread_ref):
    inputs = out_ref.shape[-1]
    group = group_size(inputs)

    def step(index, carry):
        start = pl.multiple_of(index * (group * inputs), group * inputs)
        frames = folded_ref[pl.ds(start, group * inputs), :]
        spread_spectra(table_ref[...], frames, spread_ref, inputs, index * group)
        return carry

    lax.fori_loop(0, TIME // group, step, 0, unroll=4)
    pack_spectra(spread_ref, out_ref)


def phasor_kernel(first_ref, place_ref, dir_ref, *out_refs):
    depth, beams = out_refs[0].shape
    wide = 256

    def block(index, carry):
        rows = pl.ds(pl.multiple_of(index * 16, 16), 16)
        place = place_ref[rows, :]
        for lane in range(0, beams, wide):
            lanes = slice(lane, lane + wide)
            direction = dir_ref[:, lanes]
            geometry = place[:, 0:1] * direction[0:1, :]
            geometry = geometry + place[:, 1:2] * direction[1:2, :]
            geometry = geometry + place[:, 2:3] * direction[2:3, :]
            scales = [1.0 / CH]
            for k in range(len(out_refs) // 2 - 1):
                scales.append(1.0 + first_ref[k].astype(F32) * (1.0 / CH))
            for k, scale in enumerate(scales):
                c, s = cos_sin_turns(geometry * scale)
                out_refs[2 * k][rows, lanes], out_refs[2 * k + 1][rows, lanes] = c, s
        return carry

    lax.fori_loop(0, depth // 16, block, 0, unroll=2)


def beam_kernel(
    x_ref, gain_ref, dc_ref, ds_ref, c_ref, s_ref, out_ref, even_ref, odd_ref, sum_ref
):
    step = pl.program_id(0)
    tiles = pl.num_programs(0) - 1
    chans, _, beams = out_ref.shape
    depth = dc_ref.shape[0]
    wide = 256 if beams % 256 == 0 else 128
    chunk = depth // chans

    def generate(part, weight_ref):
        for sub in range(0, chunk, 16):
            row = pl.multiple_of(part * chunk + sub, 16)
            rows = pl.ds(row, 16)
            for lane in range(0, beams, wide):
                lanes = slice(lane, lane + wide)
                c, s = c_ref[rows, lanes], s_ref[rows, lanes]
                dc, ds = dc_ref[rows, lanes], ds_ref[rows, lanes]
                next_c, next_s = c * dc - s * ds, c * ds + s * dc
                twice = dc + dc
                for chan in range(chans):
                    weight_ref[chan, rows, lanes] = c.astype(BF16)
                    weight_ref[chan, pl.ds(depth + row, 16), lanes] = s.astype(BF16)
                    if chan + 2 < chans:
                        c, next_c = next_c, twice * next_c - c
                        s, next_s = next_s, twice * next_s - s
                    else:
                        c, s = next_c, next_s

    def accumulate(chan, weight_ref):
        blocks = x_ref.shape[0]
        data = jnp.concatenate([x_ref[k, chan] for k in range(blocks)], axis=1).astype(F32)
        real, imag = data[:TIME], data[TIME:]
        gain = gain_ref[chan]
        x0 = (gain[0:1] * real - gain[1:2] * imag).astype(BF16)
        x1 = (gain[0:1] * imag + gain[1:2] * real).astype(BF16)
        top = jnp.concatenate([x0, x1], axis=1)
        bottom = jnp.concatenate([x1, -x0], axis=1)
        both = jnp.concatenate([top, bottom], axis=0)
        return jnp.dot(both, weight_ref[chan], preferred_element_type=F32)

    def both(m, weights):
        sum_ref[m] += accumulate(m, weights[0])
        generate(m, weights[1])

    def last(m, weights):
        out_ref[m] = (sum_ref[m] + accumulate(m, weights[0])).astype(out_ref.dtype)

    def over_channels(body, weights, unroll=min(8, chans)):
        lax.fori_loop(0, chans, lambda m, v: (body(m, weights), v)[1], 0, unroll=unroll)

    @pl.when(step == 0)
    def _():
        sum_ref[...] = jnp.zeros_like(sum_ref)
        over_channels(generate, even_ref, 1)

    for parity, weights in ((1, (even_ref, odd_ref)), (0, (odd_ref, even_ref))):

        @pl.when((step > 0) & (step < tiles) & (lax.rem(step, 2) == parity))
        def _(weights=weights):
            over_channels(both, weights)

        @pl.when((step == tiles) & (lax.rem(step, 2) == parity))
        def _(weights=weights):
            over_channels(last, weights)


def pick_beams(rows, pick_ref, chans, search):
    per = 128 // search
    hit = lax.broadcasted_iota(jnp.int32, (rows.shape[1], 128), 0) == pick_ref[...]
    hot = jnp.where(hit, 1.0, 0.0).astype(BF16)
    if rows.dtype == BF16:
        picked = jnp.dot(rows, hot, preferred_element_type=F32)
    else:
        high, low = split_bf16(rows)
        picked = jnp.dot(high, hot, preferred_element_type=F32)
        picked = picked + jnp.dot(low, hot, preferred_element_type=F32)
    row_id = lax.broadcasted_iota(jnp.int32, (per, 128), 0)
    lane_id = lax.broadcasted_iota(jnp.int32, (per, 128), 1) // search
    chosen = []
    for chan in range(chans):
        pieces = []
        for j in range(TIME // per):
            start = chan * TIME + j * per
            piece = jnp.where(row_id == lane_id, picked[start : start + per], 0.0)
            pieces.append(jnp.sum(piece, axis=0, keepdims=True))
        chosen.append(jnp.concatenate(pieces, axis=1))
    return chosen


def far_pick_kernel(sum0_ref, sum1_ref, pick_ref, out_ref, picked_ref):
    step = pl.program_id(0)
    block = sum0_ref.shape[0]
    search = out_ref.shape[1] // TIME
    both = jnp.concatenate([sum0_ref[...], sum1_ref[...]], axis=2)
    rows = both.reshape(block * 2 * TIME, both.shape[2])
    half = picked_ref.shape[0] // 2
    for k, row in enumerate(pick_beams(rows, pick_ref, 2 * block, search)):
        place = (k % 2) * half + step * block + k // 2
        picked_ref[pl.ds(place, 1), :] = row

    @pl.when(step == pl.num_programs(0) - 1)
    def _():
        out_ref[...] = picked_ref[...].astype(BF16)


def spectrum_kernel(
    own_ref, far_ref, pick_ref, high_ref, low_ref, spec_ref, picked_ref, norm
):
    step = pl.program_id(0)
    block = own_ref.shape[0]
    copies, chans, width = spec_ref.shape
    search = width // TIME
    rows = own_ref[...].reshape(block * 2 * TIME, own_ref.shape[2])
    for k, row in enumerate(pick_beams(rows, pick_ref, 2 * block, search)):
        place = (k % 2) * chans + step * block + k // 2
        picked_ref[pl.ds(place, 1), :] = row

    @pl.when(step == pl.num_programs(0) - 1)
    def _():
        real = picked_ref[:chans] + far_ref[:chans].astype(F32)
        imag = picked_ref[chans:] + far_ref[chans:].astype(F32)
        g_high, g_low = split_bf16((real * real + imag * imag) * norm)
        spectrum = jnp.dot(g_high, high_ref[...], preferred_element_type=F32)
        spectrum = spectrum + jnp.dot(g_low, high_ref[...], preferred_element_type=F32)
        spectrum = spectrum + jnp.dot(g_high, low_ref[...], preferred_element_type=F32)
        spectrum = spectrum.astype(BF16)
        for dest in range(copies):
            spec_ref[dest] = spectrum


def power_kernel(own_ref, far0_ref, far1_ref, power_ref, norm):
    far = jnp.concatenate([far0_ref[...], far1_ref[...]], axis=2)
    total = own_ref[...] + far.astype(F32)
    real, imag = total[:, :TIME], total[:, TIME:]
    power_ref[...] = (real * real + imag * imag) * norm


def turn_kernel(delay_ref, turn_ref):
    trials, chans = delay_ref.shape
    dc, ds = cos_sin_turns(delay_ref[...].astype(F32) * (1.0 / TIME))
    c, s = dc, ds
    for k in range(HALF_BINS):
        rows = slice(k * trials, (k + 1) * trials)
        turn_ref[rows, :chans] = c.astype(BF16)
        turn_ref[rows, chans:] = s.astype(BF16)
        c, s = c * dc - s * ds, c * ds + s * dc


def plane_kernel(spec_ref, turn_ref, out_ref, both_ref, part_ref):
    chans, width = spec_ref.shape
    _, _, trials = out_ref.shape
    spec = spec_ref[...]
    values = spec.astype(F32)
    lane = lax.broadcasted_iota(jnp.int32, (chans, width), 1)
    ahead = pltpu.roll(values, width - HALF_BINS, 1)
    behind = pltpu.roll(values, HALF_BINS, 1)
    turned = jnp.where(lane % TIME < HALF_BINS, -ahead, behind)
    both_ref[:chans] = spec
    both_ref[chans:] = turned.astype(BF16)
    bin_id = lax.broadcasted_iota(jnp.int32, (trials, width), 1) % HALF_BINS
    plane = jnp.zeros((trials, width), F32)
    group = HALF_BINS // 2
    for first in range(0, HALF_BINS, group):
        rows = slice(first * trials, (first + group) * trials)
        part_ref[...] = jnp.dot(turn_ref[rows], both_ref[...], preferred_element_type=F32)
        for k in range(group):
            part = part_ref[k * trials : (k + 1) * trials]
            plane = jnp.where(bin_id == first + k, part, plane)
    out_ref[...] = (plane.T * (1.0 / math.sqrt(CH))).reshape(out_ref.shape)


SMALL = pltpu.CompilerParams(vmem_limit_bytes=12 << 20)
LARGE = pltpu.CompilerParams(vmem_limit_bytes=60 << 20)


def fold(voltages, table, block_id, dests, chans):
    inputs = voltages.shape[0]
    rows = 2 * dests * chans
    window = jnp.asarray(pfb_window())
    last = TIME // FRAMES
    now = lambda i: jnp.minimum(i, last - 1)
    following = lambda j: pl.BlockSpec(
        (inputs, FFTLEN), lambda i, k: (0, (now(i) + 1) * FRAMES + j)
    )
    kept = pltpu.VMEM((FRAMES * inputs, FFTLEN), BF16)
    spectra = jax.ShapeDtypeStruct((dests, chans, 2 * TIME, inputs), BF16)
    folded = jax.ShapeDtypeStruct((TIME * inputs, FFTLEN), BF16)
    whole = lambda x: pl.BlockSpec(x.shape, lambda i, k: (0,) * len(x.shape))
    return pl.pallas_call(
        fold_kernel,
        out_shape=(spectra, folded),
        grid_spec=pltpu.PrefetchScalarGridSpec(
            num_scalar_prefetch=1,
            grid=(last + 1,),
            in_specs=[
                pl.BlockSpec((inputs, FRAMES * FFTLEN), lambda i, k: (0, now(i))),
                *[following(j) for j in range(TAPS - 1)],
                whole(window),
                pl.BlockSpec((rows, FFTLEN), lambda i, k: (k[0], 0)),
            ],
            out_specs=(
                whole(spectra),
                pl.BlockSpec((FRAMES * inputs, FFTLEN), lambda i, k: (now(i), 0)),
            ),
            scratch_shapes=[kept, kept, pltpu.VMEM((rows * PITCH, inputs), F32)],
        ),
        compiler_params=LARGE,
        cost_estimate=pl.CostEstimate(
            flops=8 * rows * FFTLEN * TIME * inputs, bytes_accessed=12 << 20, transcendentals=0
        ),
        name="fold",
    )(block_id, *[voltages] * TAPS, window, table)


def more_spectra(folded, table, block_id, dests, chans):
    rows = 2 * dests * chans
    inputs = folded.shape[0] // TIME
    out = jax.ShapeDtypeStruct((dests, chans, 2 * TIME, inputs), BF16)
    return pl.pallas_call(
        spectra_kernel,
        out_shape=out,
        grid_spec=pltpu.PrefetchScalarGridSpec(
            num_scalar_prefetch=1,
            grid=(1,),
            in_specs=[
                pl.BlockSpec(folded.shape, lambda i, k: (0, 0)),
                pl.BlockSpec((rows, FFTLEN), lambda i, k: (k[0], 0)),
            ],
            out_specs=pl.BlockSpec(out.shape, lambda i, k: (0, 0, 0, 0)),
            scratch_shapes=[pltpu.VMEM((rows * PITCH, inputs), F32)],
        ),
        compiler_params=LARGE,
        cost_estimate=pl.CostEstimate(
            flops=4 * rows * FFTLEN * TIME * inputs, bytes_accessed=6 << 20, transcendentals=0
        ),
        name="spectra",
    )(block_id, folded, table)


def phasors(firsts, places, directions):
    count = 2 + 2 * firsts.shape[0]
    total, beams = places.shape[0], directions.shape[1]
    depth = 128
    return pl.pallas_call(
        phasor_kernel,
        out_shape=[jax.ShapeDtypeStruct((total, beams), F32)] * count,
        grid_spec=pltpu.PrefetchScalarGridSpec(
            num_scalar_prefetch=1,
            grid=(total // depth,),
            in_specs=[
                pl.BlockSpec((depth, 3), lambda i, f: (i, 0)),
                pl.BlockSpec(directions.shape, lambda i, f: (0, 0)),
            ],
            out_specs=[pl.BlockSpec((depth, beams), lambda i, f: (i, 0))] * count,
        ),
        compiler_params=LARGE,
        cost_estimate=pl.CostEstimate(
            flops=8000 * total * beams, bytes_accessed=count * 4 * total * beams, transcendentals=0
        ),
        name="phasors",
    )(firsts, places, directions)


def form_beams(x, gains, state, block, beams, out_type):
    sources, chans, rows, inputs = x.shape
    total = sources * inputs
    if inputs != 128:
        x = x.transpose(1, 2, 0, 3).reshape(chans, rows, total // 128, 128)
        x = x.transpose(2, 0, 1, 3)
    depth = 256
    blocks = depth // 128
    tiles = total // depth
    late = lambda i: jnp.maximum(i - 1, 0)
    state_spec = pl.BlockSpec((depth, beams), lambda i: (jnp.minimum(i, tiles - 1), block))
    return pl.pallas_call(
        beam_kernel,
        out_shape=jax.ShapeDtypeStruct((chans, rows, beams), out_type),
        grid=(tiles + 1,),
        in_specs=[
            pl.BlockSpec((blocks, chans, rows, 128), lambda i: (late(i), 0, 0, 0)),
            pl.BlockSpec((chans, 2, depth), lambda i: (0, 0, late(i))),
        ]
        + [state_spec] * 4,
        out_specs=pl.BlockSpec((chans, rows, beams), lambda i: (0, 0, 0)),
        scratch_shapes=[
            pltpu.VMEM((chans, 2 * depth, beams), BF16),
            pltpu.VMEM((chans, 2 * depth, beams), BF16),
            pltpu.VMEM((chans, rows, beams), F32),
        ],
        compiler_params=LARGE,
        cost_estimate=pl.CostEstimate(
            flops=16 * chans * rows * total * beams, bytes_accessed=12 << 20, transcendentals=0
        ),
        name="beams",
    )(x, gains, *state)


def flat(shape):
    return pl.BlockSpec(shape, lambda i: (0,) * len(shape))


def cubes(block, *arrays):
    return [pl.BlockSpec((block, *x.shape[1:]), lambda i: (i, 0, 0)) for x in arrays]


def pick_far(sums0, sums1, pick, search):
    chans = sums0.shape[0]
    block = min(4, chans)
    out = jax.ShapeDtypeStruct((2 * chans, TIME * search), BF16)
    return pl.pallas_call(
        far_pick_kernel,
        out_shape=out,
        grid=(chans // block,),
        in_specs=cubes(block, sums0, sums1) + [flat(pick.shape)],
        out_specs=flat(out.shape),
        scratch_shapes=[pltpu.VMEM(out.shape, F32)],
        compiler_params=LARGE,
        cost_estimate=pl.CostEstimate(
            flops=1 << 30, bytes_accessed=2 << 20, transcendentals=0
        ),
        name="pick",
    )(sums0, sums1, pick)


def search_spectra(own, far, pick, search, copies, norm):
    chans = own.shape[0]
    width = TIME * search
    table = time_table(search)
    high = jnp.asarray(table).astype(BF16)
    low = (jnp.asarray(table) - high.astype(F32)).astype(BF16)
    block = min(4, chans)
    out = jax.ShapeDtypeStruct((copies, chans, width), BF16)
    return pl.pallas_call(
        functools.partial(spectrum_kernel, norm=norm),
        out_shape=out,
        grid=(chans // block,),
        in_specs=cubes(block, own) + [flat(x.shape) for x in (far, pick, high, low)],
        out_specs=flat(out.shape),
        scratch_shapes=[pltpu.VMEM((2 * chans, width), F32)],
        compiler_params=LARGE,
        cost_estimate=pl.CostEstimate(
            flops=2 << 30, bytes_accessed=4 << 20, transcendentals=0
        ),
        name="spectrum",
    )(own, far, pick, high, low)


def powers(own, far, norm):
    chans, _, beams = own.shape
    block = min(4, chans)
    out = jax.ShapeDtypeStruct((chans, TIME, beams), F32)
    return pl.pallas_call(
        functools.partial(power_kernel, norm=norm),
        out_shape=out,
        grid=(chans // block,),
        in_specs=cubes(block, own, *far),
        out_specs=cubes(block, out)[0],
        compiler_params=LARGE,
        cost_estimate=pl.CostEstimate(
            flops=1 << 28, bytes_accessed=5 << 20, transcendentals=0
        ),
        name="power",
    )(own, *far)


def on_device(voltages, gains, positions, directions, input_order, delays, search_beams):
    devices = lax.axis_size("crate")
    position = lax.axis_index("crate")
    chans = gains.shape[0]
    halves = 2
    per_half = devices // halves
    half_id = position // per_half
    members = [list(range(h * per_half, (h + 1) * per_half)) for h in range(halves)]
    partners = [(d, (d + per_half) % devices) for d in range(devices)]
    inputs = gains.shape[2] // halves
    own_inputs = half_id * inputs
    half_scalar = half_id.astype(jnp.int32).reshape(1)
    table = jnp.asarray(dft_table()).astype(BF16)
    far, folded = fold(voltages, table, 1 - half_scalar, per_half, chans)

    def exchange(x):
        return lax.all_to_all(
            x, "crate", split_axis=0, concat_axis=0, axis_index_groups=members, tiled=True
        )

    far = exchange(far)
    near = more_spectra(folded, table, half_scalar, per_half, chans)
    near, gains, positions = lax.optimization_barrier((near, gains, positions))
    far_gains = lax.dynamic_slice_in_dim(gains, inputs - own_inputs, inputs, 2)
    far_gains = lax.ppermute(far_gains, "crate", partners)
    near_gains = lax.dynamic_slice_in_dim(gains, own_inputs, inputs, 2)
    order = lax.dynamic_slice_in_dim(input_order, own_inputs, inputs, 0)
    places = jnp.take(positions.T, order, axis=0)
    search = search_beams.shape[0]
    pick = jnp.tile(search_beams, 128 // search)[None, :]
    firsts = jnp.stack([(position + per_half) % devices, position]) * chans
    dc, ds, far_c, far_s, near_c, near_s = phasors(
        firsts.astype(jnp.int32), places, directions
    )
    near, near_gains, pick, dc, ds, far_c, far_s = lax.optimization_barrier(
        (near, near_gains, pick, dc, ds, far_c, far_s)
    )
    near = exchange(near)

    beams = directions.shape[1]
    norm = 1.0 / gains.shape[2]
    far_state = (dc, ds, far_c, far_s)
    few = beams // 2
    sums1 = form_beams(far, far_gains, far_state, 1, few, BF16)
    far1 = lax.ppermute(sums1, "crate", partners)
    far, far1_sums = lax.optimization_barrier((far, sums1))
    sums0 = form_beams(far, far_gains, far_state, 0, beams - few, BF16)
    picked = pick_far(sums0, far1_sums, pick, search)
    far_picked = lax.ppermute(picked, "crate", partners)
    far0 = lax.ppermute(sums0, "crate", partners)
    near_sums = form_beams(near, near_gains, (dc, ds, near_c, near_s), 0, beams, F32)

    spectrum = search_spectra(near_sums, far_picked, pick, search, devices, norm)
    near_sums, spectrum = lax.optimization_barrier((near_sums, spectrum))
    spectrum = lax.all_to_all(spectrum, "crate", split_axis=0, concat_axis=0, tiled=True)
    beam_power = powers(near_sums, (far0, far1), norm)
    width = spectrum.shape[-1]
    trials = delays.shape[0] // devices
    own_delays = lax.dynamic_slice_in_dim(delays, position * trials, trials, 0)
    turns = pl.pallas_call(
        turn_kernel,
        out_shape=jax.ShapeDtypeStruct((HALF_BINS * trials, 2 * CH), BF16),
        compiler_params=LARGE,
        name="turns",
    )(own_delays)
    dm_plane = pl.pallas_call(
        plane_kernel,
        out_shape=jax.ShapeDtypeStruct((search, TIME, trials), F32),
        scratch_shapes=[
            pltpu.VMEM((2 * CH, width), BF16),
            pltpu.VMEM((HALF_BINS // 2 * trials, width), F32),
        ],
        compiler_params=SMALL,
        name="plane",
    )(spectrum.reshape(CH, width), turns)
    return beam_power.transpose(0, 2, 1), dm_plane.transpose(2, 0, 1)


def solution(mesh):
    in_specs = (P(("groups", "crate"), None), P("crate", None, None), P(), P(), P(), P(), P())
    out_specs = (P(("groups", "crate"), None, None), P(("groups", "crate"), None, None))
    return jax.shard_map(
        on_device, mesh=mesh, in_specs=in_specs, out_specs=out_specs, check_vma=False
    )
```
